32 devices in a mesh: dp: 8 (over z, y), seq: 4 (over x, core).
Axes of the slice: x: 2, y: 2, z: 4, core: 2. Of those that a mesh axis runs over, the one named last changes fastest.
Arguments:
- tokens: bfloat16 [16, 2048, 768], P('dp', 'seq'), may hold values from -6 to 6
- first_values: bfloat16 [16, 2048, 384], P('dp', 'seq'), may hold values from -6 to 6
- cotangent: bfloat16 [16, 2048, 768], P('dp', 'seq'), may hold values from -6 to 6
- lengths: int32 [16], P('dp'), may hold values from 64 to 2048, as said below
- master_tiles: float32 [416, 128, 128], P(('dp', 'seq'))
- left_stat: float32 [416, 128, 128], P(('dp', 'seq'))
- right_stat: float32 [416, 128, 128], P(('dp', 'seq'))
- left_root: float32 [416, 128, 128], P(('dp', 'seq'))
- right_root: float32 [416, 128, 128], P(('dp', 'seq'))
- vector_params: float32 [8832], replicated
- vector_stat: float32 [8832], replicated
Outputs:
- block_output: bfloat16 [16, 2048, 768], P('dp', 'seq')
- tokens_grad: float32 [16, 2048, 768], P('dp', 'seq')
- first_values_grad: float32 [16, 2048, 384], P('dp', 'seq')
- tile_grads: float32 [416, 128, 128], P(('dp', 'seq'))
- left_new: float32 [416, 128, 128], P(('dp', 'seq'))
- right_new: float32 [416, 128, 128], P(('dp', 'seq'))
- tiles_new: float32 [416, 128, 128], P(('dp', 'seq'))
- vector_grads: float32 [8832], replicated
- vector_stat_new: float32 [8832], replicated
- vector_new: float32 [8832], replicated
- grad_norm: float32 [], replicated
The draws below stay inside these ranges and needn't reach their ends.
Inputs may be any that keep to these rules, and one draw needn't show every extreme that they name: `lengths`: each sequence's length; in every draw some sequence has exactly 2048.
All inputs are finite; a program needn't handle non-finite values.
Results may differ from the reference program's by a relative error of at most 0.012.
The reference program's roundings to bfloat16 on the way count: a program that leaves them out, or rounds other values in their place, can miss the bound.
Values may be sent and summed in bfloat16 or wider, within the bound.
A program may use at most 192 MiB of HBM per device.

```python
import math
import jax
import jax.numpy as jnp
from jax import lax

D = 768
HEADS = 12
HD = 64
FF = 3072
VW = 384
BLEN = 2048
MINLEN = 64
QBLK = 512
TILE = 128
NSEQ = 16
NPARAM = 6782976
NT_PAD = 416
NVEC = 8832
CLIP = 256


def draw_lengths(key, part):
    key_one, key_two = jax.random.split(jax.random.fold_in(key, 7))
    sampled = jax.random.randint(key_one, (NSEQ,), MINLEN, BLEN + 1)
    chosen = jax.random.randint(key_two, (), 0, NSEQ)
    return jnp.where(jnp.arange(NSEQ) == chosen, BLEN, sampled).astype(jnp.int32)


def tile_spreads():
    amounts = [D // TILE * (D // TILE), D // TILE * (D // TILE), D // TILE * (VW // TILE), D // TILE * (D // TILE), D // TILE * (FF // TILE), FF // TILE * (D // TILE)]
    spreads = [(2.0 / D) ** 0.5, (2.0 / D) ** 0.5, D ** (-0.5), 4.0 * D ** (-0.5), D ** (-0.5), FF ** (-0.5)]
    tile_index = jnp.arange(NT_PAD)
    per_tile = jnp.full((NT_PAD,), D ** (-0.5), jnp.float32)
    offset = 0
    for amount, spread in zip(amounts, spreads):
        inside = (tile_index >= offset) & (tile_index < offset + amount)
        per_tile = jnp.where(inside, spread, per_tile)
        offset = offset + amount
    return per_tile


def draw_master_tiles(key, part):
    sub_key = jax.random.fold_in(key, 10)
    raw = jax.random.normal(sub_key, (NT_PAD, TILE, TILE), jnp.float32)
    return raw * tile_spreads()[:, None, None]


def symmetric(key):
    raw = jax.random.normal(key, (NT_PAD, TILE, TILE), jnp.float32)
    return (raw + jnp.swapaxes(raw, 1, 2)) * 0.5


def stat_draw(key):
    key_one, key_two = jax.random.split(key)
    energy = CLIP * CLIP / NPARAM
    level = jnp.exp(jax.random.uniform(key_one, (NT_PAD, 1, 1), jnp.float32, 0.0, math.log(4.0)))
    identity = jnp.eye(TILE, dtype=jnp.float32)
    return energy * (level * TILE * identity + TILE ** 0.5 * symmetric(key_two))


def root_draw(key):
    energy = CLIP * CLIP / NPARAM
    base_level = (TILE * energy) ** (-0.25)
    identity = jnp.eye(TILE, dtype=jnp.float32)
    return base_level * (identity + symmetric(key) * (0.5 / TILE ** 0.5))


def draw_left_stat(key, part):
    return stat_draw(jax.random.fold_in(key, 11))


def draw_right_stat(key, part):
    return stat_draw(jax.random.fold_in(key, 12))


def draw_left_root(key, part):
    return root_draw(jax.random.fold_in(key, 13))


def draw_right_root(key, part):
    return root_draw(jax.random.fold_in(key, 14))


def draw_vector_params(key, part):
    key_one, key_two = jax.random.split(jax.random.fold_in(key, 21))
    gains = 1.0 + 0.1 * jax.random.normal(key_one, (NVEC,), jnp.float32)
    shifts = 0.2 * jax.random.normal(key_two, (NVEC,), jnp.float32)
    position = jnp.arange(NVEC)
    is_gain = (position < D) | (position >= 2 * D) & (position < 3 * D)
    return jnp.where(is_gain, gains, shifts)


def draw_vector_stat(key, part):
    energy = CLIP * CLIP / NPARAM
    spread = jax.random.uniform(jax.random.fold_in(key, 22), (NVEC,), jnp.float32, 0.0, math.log(16.0))
    return energy * jnp.exp(spread)


def block_levels(own_key, dims, cuts, low, high):
    gain = 1.0
    for dim, shards_of in cuts:
        heights = jax.random.uniform(jax.random.fold_in(jax.random.fold_in(own_key, 6), dim), (shards_of,), jnp.float32, low / len(cuts), high / len(cuts))
        gain = gain * jnp.repeat(jnp.exp(heights), dims[dim] // shards_of).reshape((-1,) + (1,) * (len(dims) - 1 - dim))
    return gain


def normal_values(key, extent, deviation, limit, cuts=(), held_as=jnp.bfloat16):
    drawn = jax.random.normal(key, extent, jnp.float32) * deviation
    if len(cuts) > 0:
        drawn = block_levels(key, extent, cuts, -0.22, 0.18) * drawn
    return jnp.clip(drawn, min=-limit, max=limit).astype(held_as)


def setup_inputs(seed: int = 0) -> dict:
    arg_keys = jax.random.split(jax.random.key(seed), 12)
    return {
        "tokens": normal_values(arg_keys[0], (NSEQ, BLEN, D), 1.0, 6.0, ((0, 8), (1, 4))),
        "first_values": normal_values(arg_keys[1], (NSEQ, BLEN, VW), 1.0, 6.0, ((0, 8), (1, 4))),
        "cotangent": normal_values(arg_keys[2], (NSEQ, BLEN, D), 1.0, 6.0, ((0, 8), (1, 4))),
        "lengths": draw_lengths(jax.random.fold_in(arg_keys[11], 71), 0),
        "master_tiles": draw_master_tiles(jax.random.fold_in(arg_keys[11], 71), 0),
        "left_stat": draw_left_stat(jax.random.fold_in(arg_keys[11], 71), 0),
        "right_stat": draw_right_stat(jax.random.fold_in(arg_keys[11], 71), 0),
        "left_root": draw_left_root(jax.random.fold_in(arg_keys[11], 71), 0),
        "right_root": draw_right_root(jax.random.fold_in(arg_keys[11], 71), 0),
        "vector_params": draw_vector_params(jax.random.fold_in(arg_keys[11], 71), 0),
        "vector_stat": draw_vector_stat(jax.random.fold_in(arg_keys[11], 71), 0),
    }


@jax.custom_vjp
def low(v):
    return lax.optimization_barrier(v.astype(jnp.bfloat16)).astype(jnp.float32)

@jax.custom_vjp
def low_back(v):
    return v

def low_keep(v):
    return (low(v), None)

def low_pass(kept, grad):
    return (grad,)

def back_keep(v):
    return (v, None)

def back_low(kept, grad):
    return (low(grad),)
low.defvjp(low_keep, low_pass)
low_back.defvjp(back_keep, back_low)
highest = lax.Precision.HIGHEST
norm_eps = 1e-05
clip_eps = 1e-06
decay_rate = 0.5
matrix_rate = 0.3
vector_rate = 0.1
moment_eps = 1e-08
masked_score = -1e+30

def matrix_shapes():
    return ((D, D), (D, D), (D, VW), (D, D), (D, FF), (FF, D))

def untile(stacked, row_count, col_count):
    shaped = stacked.reshape(row_count // TILE, col_count // TILE, TILE, TILE)
    return shaped.transpose(0, 2, 1, 3).reshape(row_count, col_count)

def retile(matrix):
    row_count, col_count = matrix.shape
    shaped = matrix.reshape(row_count // TILE, TILE, col_count // TILE, TILE)
    return shaped.transpose(0, 2, 1, 3).reshape(-1, TILE, TILE)

def split_tiles(stacked):
    matrices = []
    offset = 0
    for row_count, col_count in matrix_shapes():
        amount = row_count // TILE * (col_count // TILE)
        matrices.append(untile(stacked[offset:offset + amount], row_count, col_count))
        offset = offset + amount
    return matrices

def join_tiles(matrices, total_tiles):
    joined = jnp.concatenate([retile(matrix) for matrix in matrices], axis=0)
    padding = jnp.zeros((total_tiles - joined.shape[0], TILE, TILE), joined.dtype)
    return jnp.concatenate([joined, padding], axis=0)

def split_vector(vector):
    pieces = []
    offset = 0
    for length in (D, D, D, D, D, D, D, VW, FF):
        pieces.append(vector[offset:offset + length])
        offset = offset + length
    return pieces

def layer_norm(values, gain_row, shift_row):
    centered = values - lax.optimization_barrier(jnp.mean(values, axis=-1, keepdims=True))
    variance = lax.optimization_barrier(jnp.mean(centered * centered, axis=-1, keepdims=True))
    return centered * lax.rsqrt(variance + norm_eps) * gain_row + shift_row

def attend_sequence(inputs):
    queries, keys_all, values_all, length = inputs
    key_pos = jnp.arange(BLEN, dtype=jnp.int32)

    def score_block(block_index):
        query_rows = lax.dynamic_slice_in_dim(queries, block_index * QBLK, QBLK, 0)
        scores = jnp.einsum('qhd,khd->hqk', query_rows, keys_all, precision=highest) * HD ** (-0.5)
        scores = low_back(scores)
        query_pos = block_index * QBLK + jnp.arange(QBLK, dtype=jnp.int32)
        allowed = (key_pos[None, :] <= query_pos[:, None]) & (key_pos[None, :] < length)
        scores = jnp.where(allowed[None], scores, masked_score)
        weights = low(jax.nn.softmax(scores, axis=-1))
        return jnp.einsum('hqk,khd->qhd', weights, values_all, precision=highest)
    blocks = lax.map(jax.checkpoint(score_block), jnp.arange(BLEN // QBLK, dtype=jnp.int32))
    return blocks.reshape(BLEN, HEADS * HD)

def forward(tokens_in, first_in, matrices, vector, lengths):
    w_query, w_key, w_value, w_out, w_hidden, w_proj = [low(matrix) for matrix in matrices]
    gain_one, shift_one, gain_two, shift_two, query_bias, out_bias, proj_bias, value_bias, hidden_bias = split_vector(vector)
    flat_tokens = tokens_in.reshape(-1, D)
    normed_one = low(layer_norm(flat_tokens, gain_one, shift_one))
    queries = low_back(low(jnp.dot(normed_one, w_query, precision=highest) + query_bias))
    keys_all = low_back(low(jnp.dot(normed_one, w_key, precision=highest)))
    fresh = low_back(low(jnp.dot(normed_one, w_value, precision=highest) + value_bias))
    first_vals = low_back(first_in.reshape(-1, VW))
    values_all = jnp.concatenate([fresh, first_vals], axis=-1)
    shaped = (NSEQ, BLEN, HEADS, HD)
    attended = lax.map(attend_sequence, (queries.reshape(shaped), keys_all.reshape(shaped), values_all.reshape(shaped), lengths))
    attended = low_back(low(attended.reshape(-1, D)))
    branch = low_back(jnp.dot(attended, w_out, precision=highest) + out_bias)
    residual = flat_tokens + branch
    normed_two = low(layer_norm(residual, gain_two, shift_two))
    hidden = low_back(jnp.dot(normed_two, w_hidden, precision=highest) + hidden_bias)
    active = low(jax.nn.gelu(hidden, approximate=True))
    output = residual + jnp.dot(active, w_proj, precision=highest) + proj_bias
    return output.reshape(NSEQ, BLEN, D)

def reference(tokens, first_values, cotangent, lengths, master_tiles, left_stat, right_stat, left_root, right_root, vector_params, vector_stat):
    total_tiles = master_tiles.shape[0]
    matrices = split_tiles(master_tiles)

    def run(tokens_in, first_in, matrix_list, vector):
        return forward(tokens_in, first_in, matrix_list, vector, lengths)
    output, backward = jax.vjp(run, tokens.astype(jnp.float32), first_values.astype(jnp.float32), matrices, vector_params)
    live = (jnp.arange(BLEN, dtype=jnp.int32)[None, :] < lengths[:, None]).astype(jnp.float32)
    tokens_grad, first_grad, matrix_grads, raw_vector = backward(cotangent.astype(jnp.float32) * live[:, :, None])
    raw_tiles = join_tiles(matrix_grads, total_tiles)
    square_sum = jnp.sum(raw_tiles * raw_tiles) + jnp.sum(raw_vector * raw_vector)
    grad_norm = jnp.sqrt(square_sum)
    factor = jnp.minimum(1.0, CLIP / (grad_norm + clip_eps))
    tile_grads = raw_tiles * factor
    vector_grads = raw_vector * factor
    left_gram = jnp.einsum('tij,tkj->tik', tile_grads, tile_grads, precision=highest)
    right_gram = jnp.einsum('tji,tjk->tik', tile_grads, tile_grads, precision=highest)
    left_new = decay_rate * left_stat + (1.0 - decay_rate) * left_gram
    right_new = decay_rate * right_stat + (1.0 - decay_rate) * right_gram
    inner = jnp.einsum('tij,tjk->tik', tile_grads, right_root, precision=highest)
    step = jnp.einsum('tij,tjk->tik', left_root, inner, precision=highest)
    tiles_new = master_tiles - matrix_rate * step
    vector_stat_new = decay_rate * vector_stat + (1.0 - decay_rate) * vector_grads * vector_grads
    vector_new = vector_params - vector_rate * vector_grads / (jnp.sqrt(vector_stat_new) + moment_eps)
    return (output.astype(jnp.bfloat16), tokens_grad, first_grad, tile_grads, left_new, right_new, tiles_new, vector_grads, vector_stat_new, vector_new, grad_norm)
```

```python
import functools

import jax
import jax.numpy as jnp
from jax import lax
from jax.experimental import pallas as pl
from jax.experimental.pallas import tpu as pltpu
from jax.sharding import PartitionSpec as P

D = 768
HD = 64
FF = 3072
VW = 384
TILE = 128
CLIP = 256
LOG2E = 1.4426950408889634
SCALE = HD**-0.5
QUERY_BLOCK = 512
KEY_BLOCK = 512
BACK_QUERY_BLOCK = 512
BACK_KEY_BLOCK = 512
N_QKV = 90
N_OUT = 36
N_HID = 144
N_PROJ = 144
N_REST = N_OUT + N_HID + N_PROJ
FIRST_PROJ = N_QKV + N_OUT + N_HID

highest = lax.Precision.HIGHEST
norm_eps = 1e-05
clip_eps = 1e-06
decay_rate = 0.5
matrix_rate = 0.3
vector_rate = 0.1
moment_eps = 1e-08
masked_score = -1e30

f32 = jnp.float32
bf16 = jnp.bfloat16
NN = (((1,), (0,)), ((), ()))
NT = (((1,), (1,)), ((), ()))
TN = (((0,), (0,)), ((), ()))
VMEM_LIMIT = 60 << 20


def dot(left_in, right_in, dims=NN):
    return lax.dot_general(left_in, right_in, dims, preferred_element_type=f32)


def split_vector(vector):
    pieces = []
    offset = 0
    for length in (D, D, D, D, D, D, D, VW, FF):
        pieces.append(vector[offset : offset + length])
        offset = offset + length
    return pieces


def norm_forward(values, gain_row, shift_row):
    centered = values - jnp.mean(values, axis=-1, keepdims=True)
    variance = jnp.mean(centered * centered, axis=-1, keepdims=True)
    inv_std = lax.rsqrt(variance + norm_eps)
    unit_rows = centered * inv_std
    return (unit_rows * gain_row + shift_row, unit_rows, inv_std)


def norm_backward(grad_in, unit_rows, inv_std, gain_row):
    scaled = grad_in * gain_row
    term = (
        scaled
        - jnp.mean(scaled, axis=-1, keepdims=True)
        - unit_rows * jnp.mean(scaled * unit_rows, axis=-1, keepdims=True)
    )
    return term * inv_std


def whole(shape):
    return pl.BlockSpec(shape, lambda i, *_: (0,) * len(shape))


def params():
    return pltpu.CompilerParams(dimension_semantics=("arbitrary",), vmem_limit_bytes=VMEM_LIMIT)


def attend_forward_kernel(
    heads,
    len_ref,
    fresh_ref,
    x_ref,
    wq_ref,
    wk_ref,
    wv_ref,
    qb_ref,
    vb_ref,
    fv_ref,
    o_ref,
    q_ref,
    k_ref,
    v_ref,
    lse_ref,
    k_heads,
    values,
    acc,
    top,
    total,
):
    blocks, _, span, width_in = x_ref.shape
    count = blocks * span
    length = len_ref[pl.program_id(0)]
    x = x_ref[...].reshape(count, width_in)
    q_ref[0] = (dot(wq_ref[...], x, NT) + qb_ref[...]).astype(bf16)
    keys = dot(x, wk_ref[...], NT).astype(bf16)
    k_ref[0] = keys
    for h in range(heads):
        k_heads[h] = keys[:, h * HD : (h + 1) * HD]

    @pl.when(fresh_ref[0] == 1)
    def _():
        values[...] = (dot(wv_ref[...], x, NT) + vb_ref[...]).astype(bf16)

    @pl.when(fresh_ref[0] == 0)
    def _():
        for b in range(blocks):
            values[:, b * span : (b + 1) * span] = fv_ref[b, 0]

    v_ref[0] = values[...].T
    bq, bk = QUERY_BLOCK, KEY_BLOCK

    def one_query_block(qi, carry):
        q0 = pl.multiple_of(qi * bq, bq)
        top[...] = jnp.full_like(top, masked_score)
        total[...] = jnp.zeros_like(total)
        acc[...] = jnp.zeros_like(acc)

        def step(ki, masked):
            k0 = pl.multiple_of(ki * bk, bk)
            if masked:
                key_pos = k0 + lax.broadcasted_iota(jnp.int32, (bk, bq), 0)
                query_pos = q0 + lax.broadcasted_iota(jnp.int32, (bk, bq), 1)
                allowed = (key_pos <= query_pos) & (key_pos < length)
            for h in range(heads):
                rows = slice(h * HD, (h + 1) * HD)
                s = dot(k_heads[h, pl.ds(k0, bk), :], q_ref[0, rows, pl.ds(q0, bq)])
                s = s * (SCALE * LOG2E)
                if masked:
                    s = jnp.where(allowed, s, masked_score)
                top_old = top[h : h + 1, :]
                top_new = jnp.maximum(top_old, jnp.max(s, axis=0, keepdims=True))
                p = jnp.exp2(s - top_new)
                fade = jnp.exp2(top_old - top_new)
                top[h : h + 1, :] = top_new
                total[h : h + 1, :] = total[h : h + 1, :] * fade + jnp.sum(
                    p, axis=0, keepdims=True
                )
                acc[rows, :] = acc[rows, :] * fade + dot(
                    values[rows, pl.ds(k0, bk)], p.astype(bf16)
                )

        plain = jnp.minimum(q0, length) // bk
        end = (jnp.minimum(q0 + bq, length) + bk - 1) // bk
        lax.fori_loop(0, plain, lambda i, c: (step(i, False), c)[1], 0)
        lax.fori_loop(plain, end, lambda i, c: (step(i, True), c)[1], 0)
        for h in range(heads):
            rows = slice(h * HD, (h + 1) * HD)
            sums = total[h : h + 1, :]
            o_ref[qi, 0, rows, :] = (acc[rows, :] / sums).astype(bf16)
            lse_ref[0, h : h + 1, pl.ds(q0, bq)] = top[h : h + 1, :] + jnp.log2(sums)
        return carry

    lax.fori_loop(0, count // bq, one_query_block, 0)


def attend_forward(lengths, fresh, x, wq, wk, wv, qb, vb, fv):
    blocks, seqs, span, _ = x.shape
    width = wq.shape[0]
    heads = width // HD
    count = blocks * span
    one = lambda shape: pl.BlockSpec((1,) + shape, lambda i, *_: (i,) + (0,) * len(shape))
    mid = lambda shape: pl.BlockSpec((blocks, 1) + shape, lambda i, *_: (0, i, 0, 0))
    return pl.pallas_call(
        functools.partial(attend_forward_kernel, heads),
        grid_spec=pltpu.PrefetchScalarGridSpec(
            num_scalar_prefetch=2,
            grid=(seqs,),
            in_specs=[mid((span, D))]
            + [whole((width, D))] * 3
            + [whole((width, 1))] * 2
            + [mid((width, span))],
            out_specs=[
                mid((width, span)),
                one((width, count)),
                one((count, width)),
                one((count, width)),
                one((8, count)),
            ],
            scratch_shapes=[
                pltpu.VMEM((heads, count, HD), bf16),
                pltpu.VMEM((width, count), bf16),
                pltpu.VMEM((width, QUERY_BLOCK), f32),
                pltpu.VMEM((8, QUERY_BLOCK), f32),
                pltpu.VMEM((8, QUERY_BLOCK), f32),
            ],
        ),
        out_shape=[
            jax.ShapeDtypeStruct((blocks, seqs, width, span), bf16),
            jax.ShapeDtypeStruct((seqs, width, count), bf16),
            jax.ShapeDtypeStruct((seqs, count, width), bf16),
            jax.ShapeDtypeStruct((seqs, count, width), bf16),
            jax.ShapeDtypeStruct((seqs, 8, count), f32),
        ],
        compiler_params=params(),
        cost_estimate=pl.CostEstimate(
            flops=40_000_000_000, bytes_accessed=20_000_000, transcendentals=0
        ),
        name="attend_forward",
    )(lengths, fresh, x, wq, wk, wv, qb, vb, fv)


def attend_backward_kernel(
    heads,
    len_ref,
    fresh_ref,
    q_ref,
    k_ref,
    v_ref,
    o_ref,
    g_ref,
    lse_ref,
    x_ref,
    w_ref,
    dx_ref,
    dv_ref,
    dw_ref,
    db_ref,
    k_heads,
    v_heads,
    q_heads,
    g_heads,
    k_turned,
    g_turned,
    dq_acc,
    delta,
    grads,
    dk_acc,
    dv_acc,
):
    n = pl.program_id(0)
    blocks, _, span, width_in = x_ref.shape
    count = blocks * span
    width = heads * HD
    length = len_ref[n]
    bq, bk = BACK_QUERY_BLOCK, BACK_KEY_BLOCK
    delta[...] = jnp.zeros_like(delta)
    for h in range(heads):
        rows = slice(h * HD, (h + 1) * HD)
        k_heads[h] = k_ref[0, :, rows]
        v_heads[h] = v_ref[0, :, rows]
        q_heads[h] = q_ref[0, rows, :].T
    for b in range(blocks):
        at = slice(b * span, (b + 1) * span)
        g_block = g_ref[b, 0]
        g_turned[:, at] = g_block
        product = o_ref[b, 0].astype(f32) * g_block.astype(f32)
        for h in range(heads):
            rows = slice(h * HD, (h + 1) * HD)
            g_heads[h, at, :] = g_block[rows, :].T
            delta[h : h + 1, at] = jnp.sum(product[rows, :], axis=0, keepdims=True)
    k_turned[...] = k_ref[0].T
    dq_acc[...] = jnp.zeros_like(dq_acc)
    grads[...] = jnp.zeros_like(grads)
    key_blocks = (length + bk - 1) // bk
    query_blocks = (length + bq - 1) // bq

    def one_key_block(ki, carry):
        k0 = pl.multiple_of(ki * bk, bk)
        dk_acc[...] = jnp.zeros_like(dk_acc)
        dv_acc[...] = jnp.zeros_like(dv_acc)

        def step(qi, masked):
            q0 = pl.multiple_of(qi * bq, bq)
            at = pl.ds(q0, bq)
            if masked:
                key_pos = k0 + lax.broadcasted_iota(jnp.int32, (bk, bq), 0)
                query_pos = q0 + lax.broadcasted_iota(jnp.int32, (bk, bq), 1)
                allowed = (key_pos <= query_pos) & (key_pos < length)
            for h in range(heads):
                rows = slice(h * HD, (h + 1) * HD)
                s = dot(k_heads[h, pl.ds(k0, bk), :], q_ref[0, rows, at])
                dp = dot(v_heads[h, pl.ds(k0, bk), :], g_turned[rows, at])
                p = jnp.exp2(s * (SCALE * LOG2E) - lse_ref[0, h : h + 1, at])
                if masked:
                    p = jnp.where(allowed, p, 0.0)
                ds = (p * (dp - delta[h : h + 1, at])).astype(bf16)
                dv_acc[h] = dv_acc[h] + dot(p.astype(bf16), g_heads[h, at, :])
                dk_acc[h] = dk_acc[h] + dot(ds, q_heads[h, at, :])
                dq_acc[rows, at] = dq_acc[rows, at] + dot(k_turned[rows, pl.ds(k0, bk)], ds)

        first = k0 // bq
        plain = jnp.where(k0 + bk <= length, (k0 + bk + bq - 1) // bq, query_blocks)
        plain = jnp.minimum(plain, query_blocks)
        lax.fori_loop(first, plain, lambda i, c: (step(i, True), c)[1], 0)
        lax.fori_loop(plain, query_blocks, lambda i, c: (step(i, False), c)[1], 0)
        for h in range(heads):
            grads[pl.ds(k0, bk), width + h * HD : width + (h + 1) * HD] = (
                dk_acc[h] * SCALE
            ).astype(bf16)
            grads[pl.ds(k0, bk), 2 * width + h * HD : 2 * width + (h + 1) * HD] = dv_acc[h].astype(
                bf16
            )
        return carry

    lax.fori_loop(0, key_blocks, one_key_block, 0)
    grads[:, 0:width] = (dq_acc[...] * SCALE).astype(bf16).T
    for b in range(blocks):
        dv_ref[b, 0] = grads[b * span : (b + 1) * span, 2 * width : 3 * width].T

    @pl.when(fresh_ref[0] == 0)
    def _():
        grads[:, 2 * width : 3 * width] = jnp.zeros((count, width), bf16)

    dx_ref[...] = dot(grads[...], w_ref[...]).astype(bf16).reshape(dx_ref.shape)
    dw = dot(grads[...], x_ref[...].reshape(count, width_in), TN)
    db = jnp.sum(grads[...].astype(f32), axis=0, keepdims=True)

    @pl.when(n == 0)
    def _():
        dw_ref[...] = dw
        db_ref[...] = db

    @pl.when(n > 0)
    def _():
        dw_ref[...] += dw
        db_ref[...] += db


def attend_backward(lengths, fresh, q, k, v, o, g, lse, x, w):
    blocks, seqs, span, _ = x.shape
    width = q.shape[1]
    heads = width // HD
    count = blocks * span
    one = lambda shape: pl.BlockSpec((1,) + shape, lambda i, *_: (i,) + (0,) * len(shape))
    mid = lambda shape: pl.BlockSpec((blocks, 1) + shape, lambda i, *_: (0, i, 0, 0))
    return pl.pallas_call(
        functools.partial(attend_backward_kernel, heads),
        grid_spec=pltpu.PrefetchScalarGridSpec(
            num_scalar_prefetch=2,
            grid=(seqs,),
            in_specs=[
                one((width, count)),
                one((count, width)),
                one((count, width)),
                mid((width, span)),
                mid((width, span)),
                one((8, count)),
                mid((span, D)),
                whole((3 * width, D)),
            ],
            out_specs=[
                mid((span, D)),
                mid((width, span)),
                whole((3 * width, D)),
                whole((1, 3 * width)),
            ],
            scratch_shapes=[pltpu.VMEM((heads, count, HD), bf16)] * 4
            + [
                pltpu.VMEM((width, count), bf16),
                pltpu.VMEM((width, count), bf16),
                pltpu.VMEM((width, count), f32),
                pltpu.VMEM((8, count), f32),
                pltpu.VMEM((count, 3 * width), bf16),
                pltpu.VMEM((heads, BACK_KEY_BLOCK, HD), f32),
                pltpu.VMEM((heads, BACK_KEY_BLOCK, HD), f32),
            ],
        ),
        out_shape=[
            jax.ShapeDtypeStruct((blocks, seqs, span, D), bf16),
            jax.ShapeDtypeStruct((blocks, seqs, width, span), bf16),
            jax.ShapeDtypeStruct((3 * width, D), f32),
            jax.ShapeDtypeStruct((1, 3 * width), f32),
        ],
        compiler_params=params(),
        cost_estimate=pl.CostEstimate(
            flops=70_000_000_000, bytes_accessed=25_000_000, transcendentals=0
        ),
        name="attend_backward",
    )(lengths, fresh, q, k, v, o, g, lse, x, w)


HIDDEN_CHUNK = 512
GELU_A = 0.7978845608028654
GELU_B = 0.044715


def feed_forward_kernel(
    len_ref,
    pos_ref,
    att_ref,
    tok_ref,
    cot_ref,
    tiles_ref,
    rows_ref,
    hb_ref,
    out_ref,
    rg_ref,
    ag_ref,
    act_ref,
    hg_ref,
    nt_ref,
    bg_ref,
    og_ref,
    sums_ref,
    hsum_ref,
    tiles,
    w_out,
    w_hidden,
    w_proj,
    sem,
):
    n = pl.program_id(0)
    span = tok_ref.shape[1]

    @pl.when(n == 0)
    def _():
        copies = []
        for i, (start, amount) in enumerate(
            ((0, N_OUT), (N_OUT, N_HID), (N_OUT + N_HID, N_PROJ))
        ):
            copy = pltpu.make_async_copy(
                tiles_ref.at[pl.ds(N_QKV + start, amount)],
                tiles.at[pl.ds(start, amount)],
                sem.at[i],
            )
            copy.start()
            copies.append(copy)
        for copy, start, matrix in zip(
            copies, (0, N_OUT, N_OUT + N_HID), (w_out, w_hidden, w_proj)
        ):
            copy.wait()
            row_tiles, col_tiles = matrix.shape[0] // TILE, matrix.shape[1] // TILE
            for r in range(row_tiles):
                for c in range(col_tiles):
                    matrix[r * TILE : (r + 1) * TILE, c * TILE : (c + 1) * TILE] = tiles[
                        start + r * col_tiles + c
                    ]
        sums_ref[...] = jnp.zeros_like(sums_ref)
        hsum_ref[...] = jnp.zeros_like(hsum_ref)

    gain_two, shift_two = rows_ref[0:1, :], rows_ref[1:2, :]
    out_bias, proj_bias = rows_ref[2:3, :], rows_ref[3:4, :]
    attended = att_ref[...].reshape(D, span)
    residual = tok_ref[0].astype(f32) + dot(attended, w_out[...], TN) + out_bias
    normed, unit, inv = norm_forward(residual, gain_two, shift_two)
    normed = normed.astype(bf16)
    nt_ref[...] = normed
    live = pos_ref[0] + lax.broadcasted_iota(jnp.int32, (span, 1), 0) < len_ref[n]
    out_grad = jnp.where(live, cot_ref[0].astype(f32), 0.0)
    out_grad_low = out_grad.astype(bf16)
    og_ref[...] = out_grad_low
    output = residual + proj_bias
    norm_in = jnp.zeros((span, D), f32)
    for c in range(FF // HIDDEN_CHUNK):
        cols = slice(c * HIDDEN_CHUNK, (c + 1) * HIDDEN_CHUNK)
        hidden = dot(normed, w_hidden[:, cols]) + hb_ref[:, cols]
        square = hidden * hidden
        bend = jnp.tanh(GELU_A * (hidden + GELU_B * (hidden * square)))
        active = (0.5 * hidden * (1.0 + bend)).astype(bf16)
        slope = 0.5 * (1.0 + bend) + 0.5 * hidden * (1.0 - bend * bend) * (
            GELU_A * (1.0 + (3.0 * GELU_B) * square)
        )
        act_ref[:, cols] = active
        hidden_grad = (dot(out_grad_low, w_proj[cols, :], NT) * slope).astype(bf16)
        hg_ref[:, cols] = hidden_grad
        hsum_ref[:, cols] += jnp.sum(hidden_grad.astype(f32), axis=0, keepdims=True)
        output = output + dot(active, w_proj[cols, :])
        norm_in = norm_in + dot(hidden_grad, w_hidden[:, cols], NT)
    out_ref[0] = output.astype(bf16)
    residual_grad = out_grad + norm_backward(norm_in, unit, inv, gain_two)
    rg_ref[0] = residual_grad
    branch = residual_grad.astype(bf16)
    bg_ref[...] = branch
    ag_ref[...] = dot(w_out[...], branch, NT).astype(bf16).reshape(ag_ref.shape)
    sums_ref[0:1, :] += jnp.sum(norm_in * unit, axis=0, keepdims=True)
    sums_ref[1:2, :] += jnp.sum(norm_in, axis=0, keepdims=True)
    sums_ref[2:3, :] += jnp.sum(branch.astype(f32), axis=0, keepdims=True)
    sums_ref[3:4, :] += jnp.sum(out_grad, axis=0, keepdims=True)


def feed_forward(lengths, position, att, tokens, cotangent, tiles, rows, hidden_bias):
    groups, seqs, width, span = att.shape
    one = lambda shape: pl.BlockSpec((1,) + shape, lambda i, *_: (i,) + (0,) * len(shape))
    mid = lambda shape: pl.BlockSpec((groups, 1) + shape, lambda i, *_: (0, i, 0, 0))
    row = lambda cols: pl.BlockSpec((span, cols), lambda i, *_: (i, 0))
    total = seqs * span
    return pl.pallas_call(
        feed_forward_kernel,
        grid_spec=pltpu.PrefetchScalarGridSpec(
            num_scalar_prefetch=2,
            grid=(seqs,),
            in_specs=[
                mid((width, span)),
                one((span, D)),
                one((span, D)),
                pl.BlockSpec(memory_space=pl.ANY),
                whole((8, D)),
                whole((1, FF)),
            ],
            out_specs=[
                one((span, D)),
                one((span, D)),
                mid((width, span)),
                row(FF),
                row(FF),
                row(D),
                row(D),
                row(D),
                whole((8, D)),
                whole((1, FF)),
            ],
            scratch_shapes=[
                pltpu.VMEM((N_REST, TILE, TILE), bf16),
                pltpu.VMEM((D, D), bf16),
                pltpu.VMEM((D, FF), bf16),
                pltpu.VMEM((FF, D), bf16),
                pltpu.SemaphoreType.DMA((3,)),
            ],
        ),
        out_shape=[
            jax.ShapeDtypeStruct((seqs, span, D), bf16),
            jax.ShapeDtypeStruct((seqs, span, D), f32),
            jax.ShapeDtypeStruct((groups, seqs, width, span), bf16),
            jax.ShapeDtypeStruct((total, FF), bf16),
            jax.ShapeDtypeStruct((total, FF), bf16),
            jax.ShapeDtypeStruct((total, D), bf16),
            jax.ShapeDtypeStruct((total, D), bf16),
            jax.ShapeDtypeStruct((total, D), bf16),
            jax.ShapeDtypeStruct((8, D), f32),
            jax.ShapeDtypeStruct((1, FF), f32),
        ],
        compiler_params=params(),
        cost_estimate=pl.CostEstimate(
            flops=24_000_000_000, bytes_accessed=40_000_000, transcendentals=0
        ),
        name="feed_forward",
    )(lengths, position, att, tokens, cotangent, tiles, rows, hidden_bias)


GRAD_CHUNK = 256


def weight_grad_kernel(
    att_ref, bg_ref, og_ref, nt_ref, act_ref, hg_ref, out_ref, hid_ref, proj_ref, og_turned, nt_turned
):
    i = pl.program_id(0)
    groups, seqs, width, span = att_ref.shape

    @pl.when(i == 0)
    def _():
        og_turned[...] = og_ref[...].T
        nt_turned[...] = nt_ref[...].T
        total = jnp.zeros((D, D), f32)
        for s in range(seqs):
            total = total + dot(
                att_ref[:, s].reshape(groups * width, span), bg_ref[s * span : (s + 1) * span, :]
            )
        total = total.astype(bf16)
        for r in range(D // TILE):
            for c in range(D // TILE):
                out_ref[r * (D // TILE) + c] = total[
                    r * TILE : (r + 1) * TILE, c * TILE : (c + 1) * TILE
                ]

    proj = dot(og_turned[...], act_ref[...]).astype(bf16)
    hid = dot(nt_turned[...], hg_ref[...]).astype(bf16)
    for c in range(GRAD_CHUNK // TILE):
        for r in range(D // TILE):
            rows, cols = slice(r * TILE, (r + 1) * TILE), slice(c * TILE, (c + 1) * TILE)
            proj_ref[c * (D // TILE) + r] = proj[rows, cols]
            hid_ref[r, c] = hid[rows, cols]


def weight_grads(att, bg, og, nt, act, hg):
    total = bg.shape[0]
    chunks = FF // GRAD_CHUNK
    per = GRAD_CHUNK // TILE
    return pl.pallas_call(
        weight_grad_kernel,
        grid=(chunks,),
        in_specs=[
            whole(att.shape),
            whole(bg.shape),
            whole(og.shape),
            whole(nt.shape),
            pl.BlockSpec((total, GRAD_CHUNK), lambda i: (0, i)),
            pl.BlockSpec((total, GRAD_CHUNK), lambda i: (0, i)),
        ],
        out_specs=[
            whole((N_OUT, TILE, TILE)),
            pl.BlockSpec((D // TILE, per, TILE, TILE), lambda i: (0, i, 0, 0)),
            pl.BlockSpec((per * (D // TILE), TILE, TILE), lambda i: (i, 0, 0)),
        ],
        out_shape=[
            jax.ShapeDtypeStruct((N_OUT, TILE, TILE), bf16),
            jax.ShapeDtypeStruct((D // TILE, FF // TILE, TILE, TILE), bf16),
            jax.ShapeDtypeStruct((N_PROJ, TILE, TILE), bf16),
        ],
        scratch_shapes=[pltpu.VMEM((D, total), bf16), pltpu.VMEM((D, total), bf16)],
        compiler_params=params(),
        cost_estimate=pl.CostEstimate(
            flops=12_000_000_000, bytes_accessed=40_000_000, transcendentals=0
        ),
        name="weight_grads",
    )(att, bg, og, nt, act, hg)


def per_device(
    tokens,
    first_values,
    cotangent,
    lengths,
    master_tiles,
    left_stat,
    right_stat,
    left_root,
    right_root,
    vector_params,
    vector_stat,
):
    seqs, span, _ = tokens.shape
    owned_count = master_tiles.shape[0]
    groups = lax.axis_size("seq")
    me_seq = lax.axis_index("seq")
    me = lax.axis_index("dp") * groups + me_seq
    width = D // groups
    fresh_groups = VW // width
    total_tiles = owned_count * groups * lax.axis_size("dp")

    (
        gain_one,
        shift_one,
        gain_two,
        shift_two,
        query_bias,
        out_bias,
        proj_bias,
        value_bias,
        hidden_bias,
    ) = split_vector(vector_params)

    gathered = lax.all_gather(master_tiles.astype(bf16), ("dp", "seq"), axis=0, tiled=True)
    flat_tokens = tokens.reshape(-1, D).astype(f32)
    normed_one, unit_one, inv_one = norm_forward(flat_tokens, gain_one, shift_one)
    normed_one = normed_one.astype(bf16).reshape(seqs, span, D)
    x_all = lax.all_gather(normed_one, "seq", axis=0, tiled=False)
    first_turned = first_values.transpose(2, 0, 1).reshape(groups - fresh_groups, width, seqs, span)
    first_turned = first_turned.transpose(0, 2, 1, 3)
    first_send = jnp.concatenate(
        [jnp.zeros((fresh_groups,) + first_turned.shape[1:], bf16), first_turned], axis=0
    )
    first_mine = lax.all_to_all(first_send, "seq", 0, 0, tiled=True)

    is_fresh = (me_seq < fresh_groups).astype(jnp.int32).reshape(1)
    fresh_seq = jnp.minimum(me_seq, fresh_groups - 1)

    def turned(start, cols):
        amount = D // TILE * (cols // TILE)
        tiles = gathered[start : start + amount].reshape(D // TILE, cols // TILE, TILE, TILE)
        return tiles.transpose(1, 3, 0, 2).reshape(cols, D)

    wq = lax.dynamic_slice_in_dim(turned(0, D), me_seq * width, width, 0)
    wk = lax.dynamic_slice_in_dim(turned(N_OUT, D), me_seq * width, width, 0)
    wv = lax.dynamic_slice_in_dim(turned(2 * N_OUT, VW), fresh_seq * width, width, 0)
    qb = lax.dynamic_slice_in_dim(query_bias, me_seq * width, width, 0).reshape(width, 1)
    vb = lax.dynamic_slice_in_dim(value_bias, fresh_seq * width, width, 0).reshape(width, 1)

    o_heads, q, k, v, lse = attend_forward(
        lengths, is_fresh, x_all, wq, wk, wv, qb, vb, first_mine
    )
    att = lax.all_to_all(o_heads, "seq", 0, 0, tiled=True)
    rows = jnp.concatenate(
        [jnp.stack([gain_two, shift_two, out_bias, proj_bias]), jnp.zeros((4, D), f32)]
    )
    position = (me_seq * span).astype(jnp.int32).reshape(1)
    (
        block_output,
        residual_grad,
        att_grad,
        act,
        hidden_grad,
        normed_two,
        branch_grad,
        out_grad,
        row_sums,
        hidden_bias_grad,
    ) = feed_forward(
        lengths, position, att, tokens, cotangent, gathered, rows, hidden_bias.reshape(1, FF)
    )
    g_heads = lax.all_to_all(att_grad, "seq", 0, 0, tiled=True)
    grad_out, grad_hidden, grad_proj = weight_grads(
        att, branch_grad, out_grad, normed_two, act, hidden_grad
    )
    w_mine = jnp.concatenate([wq, wk, wv], axis=0)
    dx, dv, dw, db = attend_backward(
        lengths, is_fresh, q, k, v, o_heads, g_heads, lse, x_all, w_mine
    )
    norm_one_in = (
        lax.psum_scatter(dx, "seq", scatter_dimension=0, tiled=True)
        .reshape(-1, D)
        .astype(f32)
    )
    dv_back = lax.all_to_all(dv, "seq", 0, 0, tiled=True)
    first_grad = (
        dv_back[fresh_groups:]
        .transpose(1, 3, 0, 2)
        .reshape(first_values.shape)
        .astype(f32)
    )
    token_part = norm_backward(norm_one_in, unit_one, inv_one, gain_one)
    tokens_grad = residual_grad + token_part.reshape(tokens.shape)
    gain_one_grad = jnp.sum(norm_one_in * unit_one, axis=0)
    shift_one_grad = jnp.sum(norm_one_in, axis=0)

    dw = dw.astype(bf16)
    big = jnp.zeros((2 * D, D), bf16)
    big = lax.dynamic_update_slice(big, dw[0:width], (me_seq * width, 0))
    big = lax.dynamic_update_slice(big, dw[width : 2 * width], (D + me_seq * width, 0))
    small = lax.dynamic_update_slice(
        jnp.zeros((VW, D), bf16), dw[2 * width :], (fresh_seq * width, 0)
    )

    def turned_tiles(matrix):
        cols = matrix.shape[0]
        return (
            matrix.reshape(cols // TILE, TILE, D // TILE, TILE)
            .transpose(2, 0, 1, 3)
            .reshape(-1, TILE, TILE)
        )

    grad_stack = jnp.concatenate(
        [
            turned_tiles(big[:D]),
            turned_tiles(big[D:]),
            turned_tiles(small),
            grad_out,
            grad_hidden.reshape(N_HID, TILE, TILE),
            grad_proj,
            jnp.zeros((total_tiles - N_QKV - N_REST, TILE, TILE), bf16),
        ],
        axis=0,
    )
    owned = lax.psum_scatter(grad_stack, ("dp", "seq"), scatter_dimension=0, tiled=True)
    index = me * owned_count + jnp.arange(owned_count)
    flipped = (index < N_QKV) | (index >= FIRST_PROJ)
    owned = owned.astype(f32)
    owned = jnp.where(flipped[:, None, None], owned.swapaxes(1, 2), owned)

    query_bias_grad = lax.dynamic_update_slice(
        jnp.zeros((D,), f32), db[0, 0:width], (me_seq * width,)
    )
    value_bias_grad = lax.dynamic_update_slice(
        jnp.zeros((VW,), f32), db[0, 2 * width :], (fresh_seq * width,)
    )
    vector_local = jnp.concatenate(
        [
            gain_one_grad,
            shift_one_grad,
            row_sums[0],
            row_sums[1],
            query_bias_grad,
            row_sums[2],
            row_sums[3],
            value_bias_grad,
            hidden_bias_grad[0],
        ]
    )
    summed_vector, owned_square = lax.psum((vector_local, jnp.sum(owned * owned)), ("dp", "seq"))
    grad_norm = jnp.sqrt(owned_square + jnp.sum(summed_vector * summed_vector))
    factor = jnp.minimum(1.0, CLIP / (grad_norm + clip_eps))
    clipped = owned * factor
    left_gram = jnp.einsum("tij,tkj->tik", clipped, clipped, precision=highest)
    right_gram = jnp.einsum("tji,tjk->tik", clipped, clipped, precision=highest)
    inner = jnp.einsum("tij,tjk->tik", clipped, right_root, precision=highest)
    step = jnp.einsum("tij,tjk->tik", left_root, inner, precision=highest)
    left_new = decay_rate * left_stat + (1.0 - decay_rate) * left_gram
    right_new = decay_rate * right_stat + (1.0 - decay_rate) * right_gram
    tiles_new = master_tiles - matrix_rate * step
    vector_grads = summed_vector * factor
    vector_stat_new = decay_rate * vector_stat + (1.0 - decay_rate) * vector_grads * vector_grads
    vector_new = vector_params - vector_rate * vector_grads / (
        jnp.sqrt(vector_stat_new) + moment_eps
    )
    return (
        block_output,
        tokens_grad,
        first_grad,
        clipped,
        left_new,
        right_new,
        tiles_new,
        vector_grads,
        vector_stat_new,
        vector_new,
        grad_norm,
    )


def solution(mesh):
    tiles = P(("dp", "seq"), None, None)
    seqs = P("dp", "seq", None)
    in_specs = (seqs, seqs, seqs, P("dp"), tiles, tiles, tiles, tiles, tiles, P(), P())
    out_specs = (seqs, seqs, seqs, tiles, tiles, tiles, tiles, P(), P(), P(), P())
    return jax.shard_map(
        per_device, mesh=mesh, in_specs=in_specs, out_specs=out_specs, check_vma=False
    )
```

```python
import functools

import jax
import jax.numpy as jnp
from jax import lax
from jax.experimental import pallas as pl
from jax.experimental.pallas import tpu as pltpu
from jax.sharding import PartitionSpec as P

D = 768
HD = 64
FF = 3072
VW = 384
TILE = 128
CLIP = 256
LOG2E = 1.4426950408889634
SCALE = HD**-0.5
QUERY_BLOCK = 512
KEY_BLOCK = 512
BACK_QUERY_BLOCK = 512
BACK_KEY_BLOCK = 512
HALF_BLOCK = 256
SUB_ROWS = 256
SUB_COLS = 256
N_QKV = 90
N_OUT = 36
N_HID = 144
N_PROJ = 144
N_REST = N_OUT + N_HID + N_PROJ
FIRST_PROJ = N_QKV + N_OUT + N_HID

highest = lax.Precision.HIGHEST
norm_eps = 1e-05
clip_eps = 1e-06
decay_rate = 0.5
matrix_rate = 0.3
vector_rate = 0.1
moment_eps = 1e-08
masked_score = -1e30

f32 = jnp.float32
bf16 = jnp.bfloat16
NN = (((1,), (0,)), ((), ()))
NT = (((1,), (1,)), ((), ()))
TN = (((0,), (0,)), ((), ()))
VMEM_LIMIT = 60 << 20
MESH = pl.DeviceIdType.MESH


def dot(left_in, right_in, dims=NN):
    return lax.dot_general(left_in, right_in, dims, preferred_element_type=f32)


def split_vector(vector):
    pieces = []
    offset = 0
    for length in (D, D, D, D, D, D, D, VW, FF):
        pieces.append(vector[offset : offset + length])
        offset = offset + length
    return pieces


def norm_forward(values, gain_row, shift_row):
    centered = values - jnp.mean(values, axis=-1, keepdims=True)
    variance = jnp.mean(centered * centered, axis=-1, keepdims=True)
    inv_std = lax.rsqrt(variance + norm_eps)
    unit_rows = centered * inv_std
    return (unit_rows * gain_row + shift_row, unit_rows, inv_std)


def norm_backward(grad_in, unit_rows, inv_std, gain_row):
    scaled = grad_in * gain_row
    term = (
        scaled
        - jnp.mean(scaled, axis=-1, keepdims=True)
        - unit_rows * jnp.mean(scaled * unit_rows, axis=-1, keepdims=True)
    )
    return term * inv_std


def whole(shape):
    return pl.BlockSpec(shape, lambda i, *_: (0,) * len(shape))


def params():
    return pltpu.CompilerParams(dimension_semantics=("arbitrary",), vmem_limit_bytes=VMEM_LIMIT)


W_SLOTS = 56
W_SHARE = W_SLOTS // 4
W_CHUNKS = ((0, 4), (4, 4), (8, 4), (12, 2))
X_CHUNKS = 4


def front_fits(dp, seq, owned):
    return dp == 8 and seq == 4 and 8 * owned >= N_QKV


def front_kernel(
    tok_ref,
    rows_ref,
    master_ref,
    x_ref,
    w_ref,
    normed,
    staged,
    slots,
    x_send,
    x_recv,
    own_sem,
    first_send,
    first_recv,
    w_send,
    w_recv,
):
    dp, s = lax.axis_index("dp"), lax.axis_index("seq")
    depth = lax.axis_size("dp") // 2
    z, y, x, core = dp // 2, dp % 2, s // 2, s % 2
    owned = master_ref.shape[0]
    first = (dp * 4 + s) * owned
    seqs, span, _ = tok_ref.shape
    other_y, other_x, sibling = dp + 1 - 2 * y, s + 2 - 4 * x, s + 1 - 2 * core

    barrier = pltpu.get_barrier_semaphore()
    for dy in range(2):
        for ds in range(4):
            if dy or ds:
                mate = (2 * z + (y + dy) % 2, (s + ds) % 4)
                pl.semaphore_signal(barrier, inc=1, device_id=mate, device_id_type=MESH)

    @pl.when(z > 0)
    def _():
        pl.semaphore_signal(barrier, inc=1, device_id=(dp - 2, s), device_id_type=MESH)

    @pl.when(z < depth - 1)
    def _():
        pl.semaphore_signal(barrier, inc=1, device_id=(dp + 2, s), device_id_type=MESH)

    at_end = (z == 0) | (z == depth - 1)

    @pl.when(at_end)
    def _():
        pl.semaphore_wait(barrier, 8)

    @pl.when(jnp.logical_not(at_end))
    def _():
        pl.semaphore_wait(barrier, 9)

    def tile_sends(t, act):
        index = first + t
        is_value = index >= 2 * N_OUT
        within = index % N_OUT
        col = within % (D // TILE)
        slot = jnp.where(
            is_value,
            index,
            (index // N_OUT) * 18 + (within // (D // TILE)) * 3 + col % 3,
        )
        slot = jnp.where(is_value, index - N_OUT, slot)
        share = slot // W_SHARE
        chunk = (slot % W_SHARE) // 4
        for copy_index in range(2):
            to_x = jnp.where(is_value, copy_index, col // 3)
            target = (share // 2, to_x * 2 + share % 2)
            needed = (index < N_QKV) & (is_value | (copy_index == 0))
            here = (target[0] == dp) & (target[1] == s)

            @pl.when(needed & here)
            def _():
                if act == "start":
                    pltpu.make_async_copy(
                        staged.at[t], slots.at[slot], first_recv.at[chunk]
                    ).start()

            @pl.when(needed & jnp.logical_not(here))
            def _():
                copy = pltpu.make_async_remote_copy(
                    src_ref=staged.at[t],
                    dst_ref=slots.at[slot],
                    send_sem=first_send.at[t, copy_index],
                    recv_sem=first_recv.at[chunk],
                    device_id=target,
                    device_id_type=MESH,
                )
                if act == "start":
                    copy.start()
                else:
                    copy.wait_send()

    @pl.when(first < N_QKV)
    def _():
        for t in range(owned):
            staged[t] = master_ref[t].astype(bf16).T
        for t in range(owned):
            tile_sends(t, "start")

    rows_each = seqs * span // X_CHUNKS
    per_seq = span // rows_each

    def x_copy(kind, j):
        n, part = j // per_seq, j % per_seq
        at = pl.ds(part * rows_each, rows_each)
        block = other_x if kind == 2 else s
        return pltpu.make_async_remote_copy(
            src_ref=x_ref.at[block, n, at] if kind == 2 else normed.at[n, at],
            dst_ref=x_ref.at[block, n, at],
            send_sem=x_send.at[kind, j],
            recv_sem=x_recv.at[kind, j],
            device_id=(dp, other_x) if kind == 0 else (dp, sibling),
            device_id_type=MESH,
        )

    def own_copy(j):
        n, part = j // per_seq, j % per_seq
        at = pl.ds(part * rows_each, rows_each)
        return pltpu.make_async_copy(normed.at[n, at], x_ref.at[s, n, at], own_sem.at[j])

    for j in range(X_CHUNKS):
        n, part = j // per_seq, j % per_seq
        at = pl.ds(part * rows_each, rows_each)
        value = tok_ref[n, at, :].astype(f32)
        normed[n, at, :] = norm_forward(value, rows_ref[0:1, :], rows_ref[1:2, :])[0].astype(bf16)
        x_copy(0, j).start()
        x_copy(1, j).start()
        own_copy(j).start()

    share = y * 2 + core

    def w_copy(kind, j):
        low, size = W_CHUNKS[j]
        base = ((1 - y) * 2 + core) * W_SHARE if kind == 3 else share * W_SHARE
        at = pl.ds(base + low, size)
        device = ((dp + 2, s), (other_y, s), (dp, sibling), (dp, sibling))[kind]
        return pltpu.make_async_remote_copy(
            src_ref=slots.at[at],
            dst_ref=slots.at[at],
            send_sem=w_send.at[kind, j],
            recv_sem=w_recv.at[kind, j],
            device_id=device,
            device_id_type=MESH,
        )

    def landed(j, size):
        low, _ = W_CHUNKS[j]
        at = pl.ds(share * W_SHARE + low, size)
        pltpu.make_async_copy(slots.at[at], slots.at[at], first_recv.at[j]).wait()

    used = 3 * 18 - 3 * W_SHARE
    @pl.when((z == 0) & (share == 3))
    def _():
        slots[3 * W_SHARE + used : W_SLOTS] = jnp.zeros(
            (W_SHARE - used,) + slots.shape[1:], bf16
        )

    for j in range(max(len(W_CHUNKS), X_CHUNKS)):
        if j < len(W_CHUNKS):
            low, size = W_CHUNKS[j]
            short = min(size, used - low)

            @pl.when((z == 0) & (share < 3))
            def _():
                landed(j, size)

            if short > 0:

                @pl.when((z == 0) & (share == 3))
                def _():
                    landed(j, short)

            @pl.when(z > 0)
            def _():
                w_copy(0, j).wait_recv()

            @pl.when(z < depth - 1)
            def _():
                w_copy(0, j).start()

            w_copy(1, j).start()
            w_copy(2, j).start()
        if j < X_CHUNKS:
            x_copy(0, j).wait_recv()
            x_copy(2, j).start()
        if j < len(W_CHUNKS):
            w_copy(1, j).wait_recv()
            w_copy(3, j).start()
    for j in range(len(W_CHUNKS)):
        w_copy(2, j).wait_recv()
        w_copy(3, j).wait_recv()
    width = HD * 3
    for which in range(3):
        for piece in range(3):
            unit = core * 3 + piece
            rows = pl.ds(pl.multiple_of((unit % 2) * HD, HD), HD)
            at = which * width + piece * HD
            for r in range(D // TILE):
                w_ref[at : at + HD, r * TILE : (r + 1) * TILE] = slots[
                    which * 18 + r * 3 + unit // 2, rows, :
                ]
    for j in range(X_CHUNKS):
        x_copy(1, j).wait_recv()
        x_copy(2, j).wait_recv()
        own_copy(j).wait()
        for kind in range(3):
            x_copy(kind, j).wait_send()
    for j in range(len(W_CHUNKS)):

        @pl.when(z < depth - 1)
        def _():
            w_copy(0, j).wait_send()

        for kind in range(1, 4):
            w_copy(kind, j).wait_send()

    @pl.when(first < N_QKV)
    def _():
        for t in range(owned):
            tile_sends(t, "wait")


def front(tokens, rows, master):
    seqs, span, _ = tokens.shape
    owned = master.shape[0]
    vm = pl.BlockSpec(memory_space=pltpu.VMEM)
    dma = pltpu.SemaphoreType.DMA
    chunks = len(W_CHUNKS)
    return pl.pallas_call(
        front_kernel,
        in_specs=[vm] * 3,
        out_specs=[pl.BlockSpec(memory_space=pl.ANY), vm],
        out_shape=[
            jax.ShapeDtypeStruct((4, seqs, span, D), bf16),
            jax.ShapeDtypeStruct((9 * HD, D), bf16),
        ],
        scratch_shapes=[
            pltpu.VMEM((seqs, span, D), bf16),
            pltpu.VMEM((owned, TILE, TILE), bf16),
            pltpu.VMEM((W_SLOTS, TILE, TILE), bf16),
            dma((3, X_CHUNKS)),
            dma((3, X_CHUNKS)),
            dma((X_CHUNKS,)),
            dma((owned, 2)),
            dma((chunks,)),
            dma((4, chunks)),
            dma((4, chunks)),
        ],
        compiler_params=pltpu.CompilerParams(
            collective_id=3, has_side_effects=True, vmem_limit_bytes=VMEM_LIMIT
        ),
        cost_estimate=pl.CostEstimate(
            flops=40_000_000_000, bytes_accessed=20_000_000, transcendentals=0
        ),
        name="front",
    )(tokens, rows, master)


def attend_forward_kernel(
    heads,
    len_ref,
    fresh_ref,
    x_ref,
    w_ref,
    qb_ref,
    vb_ref,
    fv_ref,
    o_ref,
    q_ref,
    k_ref,
    v_ref,
    lse_ref,
    k_heads,
    q_wide,
    values,
    acc,
    top,
):
    blocks, _, span, width_in = x_ref.shape
    count = blocks * span
    length = len_ref[pl.program_id(0)]
    x = x_ref[...].reshape(count, width_in)
    width = heads * HD
    q_ref[0] = (dot(w_ref[0:width, :], x, NT) + qb_ref[...]).astype(bf16)
    keys = dot(x, w_ref[width : 2 * width, :], NT).astype(bf16)
    k_ref[0] = keys.T
    dead = lax.broadcasted_iota(jnp.int32, (count, 1), 0) >= length
    bias = jnp.broadcast_to(jnp.where(dead, masked_score, 0.0).astype(bf16), (count, 16))
    ones = (lax.broadcasted_iota(jnp.int32, (16, count), 0) == 0).astype(f32).astype(bf16)
    for h in range(heads):
        k_heads[h, :, 0:HD] = keys[:, h * HD : (h + 1) * HD]
        k_heads[h, :, HD : HD + 16] = bias
        q_wide[h, 0:HD] = q_ref[0, h * HD : (h + 1) * HD, :]
        q_wide[h, HD : HD + 16] = ones

    @pl.when(fresh_ref[0] == 1)
    def _():
        v_ref[0] = (dot(w_ref[2 * width :, :], x, NT) + vb_ref[...]).astype(bf16)

    @pl.when(fresh_ref[0] == 0)
    def _():
        for b in range(blocks):
            v_ref[0, :, b * span : (b + 1) * span] = fv_ref[b, 0]

    for h in range(heads):
        values[h, 0:HD] = v_ref[0, h * HD : (h + 1) * HD, :]
        values[h, HD : HD + 16] = ones
    bq, bk = QUERY_BLOCK, KEY_BLOCK

    def one_query_block(qi, carry):
        q0 = pl.multiple_of(qi * bq, bq)
        top[...] = jnp.full_like(top, masked_score)
        acc[...] = jnp.zeros_like(acc)

        def step(ki, masked, low=0, rows_here=bk):
            k0 = pl.multiple_of(ki * bk + low, HALF_BLOCK)
            skip = low if masked else 0
            cols = slice(skip, bq)
            if masked:
                shape = (rows_here, bq - skip)
                key_pos = k0 + lax.broadcasted_iota(jnp.int32, shape, 0)
                query_pos = q0 + skip + lax.broadcasted_iota(jnp.int32, shape, 1)
                allowed = (key_pos <= query_pos) & (key_pos < length)
            for h in range(heads):
                rows = slice(h * HD, (h + 1) * HD)
                at = pl.ds(pl.multiple_of(q0 + skip, HALF_BLOCK), bq - skip)
                s = dot(k_heads[h, pl.ds(k0, rows_here), :], q_wide[h, :, at])
                s = s * (SCALE * LOG2E)
                if masked:
                    s = jnp.where(allowed, s, masked_score)
                top_old = top[h : h + 1, cols]
                top_new = jnp.maximum(top_old, jnp.max(s, axis=0, keepdims=True))
                p = jnp.exp2(s - top_new)
                fade = jnp.exp2(top_old - top_new)
                top[h : h + 1, cols] = top_new
                acc[h, :, cols] = acc[h, :, cols] * fade + dot(
                    values[h, :, pl.ds(k0, rows_here)], p.astype(bf16)
                )

        lax.fori_loop(
            0, jnp.minimum(qi, (length + bk - 1) // bk), lambda i, c: (step(i, False), c)[1], 0
        )

        @pl.when(q0 < length)
        def _():
            step(qi, True, 0, HALF_BLOCK)
            step(qi, True, HALF_BLOCK, HALF_BLOCK)

        for h in range(heads):
            rows = slice(h * HD, (h + 1) * HD)
            sums = acc[h, HD : HD + 1, :]
            o_ref[qi, 0, rows, :] = (acc[h, 0:HD, :] / sums).astype(bf16)
            lse_ref[0, h : h + 1, pl.ds(q0, bq)] = top[h : h + 1, :] + jnp.log2(sums)
        return carry

    lax.fori_loop(0, count // bq, one_query_block, 0)


def attend_forward(lengths, fresh, x, w, qb, vb, fv):
    blocks, seqs, span, _ = x.shape
    width = w.shape[0] // 3
    heads = width // HD
    count = blocks * span
    one = lambda shape: pl.BlockSpec((1,) + shape, lambda i, *_: (i,) + (0,) * len(shape))
    mid = lambda shape: pl.BlockSpec((blocks, 1) + shape, lambda i, *_: (0, i, 0, 0))
    return pl.pallas_call(
        functools.partial(attend_forward_kernel, heads),
        grid_spec=pltpu.PrefetchScalarGridSpec(
            num_scalar_prefetch=2,
            grid=(seqs,),
            in_specs=[mid((span, D))]
            + [whole((3 * width, D))]
            + [whole((width, 1))] * 2
            + [mid((width, span))],
            out_specs=[
                mid((width, span)),
                one((width, count)),
                one((width, count)),
                one((width, count)),
                one((8, count)),
            ],
            scratch_shapes=[
                pltpu.VMEM((heads, count, HD + 16), bf16),
                pltpu.VMEM((heads, HD + 16, count), bf16),
                pltpu.VMEM((heads, HD + 16, count), bf16),
                pltpu.VMEM((heads, HD + 16, QUERY_BLOCK), f32),
                pltpu.VMEM((8, QUERY_BLOCK), f32),
            ],
        ),
        out_shape=[
            jax.ShapeDtypeStruct((blocks, seqs, width, span), bf16),
            jax.ShapeDtypeStruct((seqs, width, count), bf16),
            jax.ShapeDtypeStruct((seqs, width, count), bf16),
            jax.ShapeDtypeStruct((seqs, width, count), bf16),
            jax.ShapeDtypeStruct((seqs, 8, count), f32),
        ],
        compiler_params=params(),
        cost_estimate=pl.CostEstimate(
            flops=40_000_000_000, bytes_accessed=20_000_000, transcendentals=0
        ),
        name="attend_forward",
    )(lengths, fresh, x, w, qb, vb, fv)


def attend_backward_kernel(
    heads,
    len_ref,
    fresh_ref,
    group_ref,
    q_ref,
    k_ref,
    v_ref,
    o_ref,
    g_ref,
    lse_ref,
    x_ref,
    w_ref,
    all_in_ref,
    dx_ref,
    dv_ref,
    all_ref,
    db_ref,
    dw_ref,
    tiles,
    sem,
    k_heads,
    v_heads,
    q_heads,
    g_heads,
    k_turned,
    g_turned,
    dq_acc,
    delta,
    grads,
    dk_acc,
    dv_acc,
):
    n = pl.program_id(0)
    blocks, _, span, width_in = x_ref.shape
    count = blocks * span
    width = heads * HD
    length = len_ref[n]
    bq, bk = BACK_QUERY_BLOCK, BACK_KEY_BLOCK
    delta[...] = jnp.zeros_like(delta)
    for h in range(heads):
        rows = slice(h * HD, (h + 1) * HD)
        k_heads[h] = k_ref[0, rows, :].T
        v_heads[h] = v_ref[0, rows, :].T
        q_heads[h] = q_ref[0, rows, :].T
    for b in range(blocks):
        at = slice(b * span, (b + 1) * span)
        g_block = g_ref[b, 0]
        g_turned[:, at] = g_block
        product = o_ref[b, 0].astype(f32) * g_block.astype(f32)
        for h in range(heads):
            rows = slice(h * HD, (h + 1) * HD)
            g_heads[h, at, :] = g_block[rows, :].T
            delta[h : h + 1, at] = jnp.sum(product[rows, :], axis=0, keepdims=True)
    k_turned[...] = k_ref[0]
    dq_acc[...] = jnp.zeros_like(dq_acc)
    grads[...] = jnp.zeros_like(grads)
    key_blocks = (length + bk - 1) // bk
    query_blocks = (length + bq - 1) // bq

    def one_key_block(ki, carry):
        k0 = pl.multiple_of(ki * bk, bk)
        dk_acc[...] = jnp.zeros_like(dk_acc)
        dv_acc[...] = jnp.zeros_like(dv_acc)

        def step(qi, masked):
            q0 = pl.multiple_of(qi * bq, bq)
            at = pl.ds(q0, bq)
            if masked:
                key_pos = k0 + lax.broadcasted_iota(jnp.int32, (bk, bq), 0)
                query_pos = q0 + lax.broadcasted_iota(jnp.int32, (bk, bq), 1)
                allowed = (key_pos <= query_pos) & (key_pos < length)
            for h in range(heads):
                rows = slice(h * HD, (h + 1) * HD)
                s = dot(k_heads[h, pl.ds(k0, bk), :], q_ref[0, rows, at])
                dp = dot(v_heads[h, pl.ds(k0, bk), :], g_turned[rows, at])
                p = jnp.exp2(s * (SCALE * LOG2E) - lse_ref[0, h : h + 1, at])
                if masked:
                    p = jnp.where(allowed, p, 0.0)
                ds = (p * (dp - delta[h : h + 1, at])).astype(bf16)
                dv_acc[h] = dv_acc[h] + dot(p.astype(bf16), g_heads[h, at, :])
                dk_acc[h] = dk_acc[h] + dot(ds, q_heads[h, at, :])
                dq_acc[rows, at] = dq_acc[rows, at] + dot(k_turned[rows, pl.ds(k0, bk)], ds)

        first = k0 // bq
        plain = jnp.where(k0 + bk <= length, (k0 + bk + bq - 1) // bq, query_blocks)
        plain = jnp.minimum(plain, query_blocks)
        lax.fori_loop(first, plain, lambda i, c: (step(i, True), c)[1], 0)
        lax.fori_loop(plain, query_blocks, lambda i, c: (step(i, False), c)[1], 0)
        for h in range(heads):
            grads[pl.ds(k0, bk), width + h * HD : width + (h + 1) * HD] = (
                dk_acc[h] * SCALE
            ).astype(bf16)
            grads[pl.ds(k0, bk), 2 * width + h * HD : 2 * width + (h + 1) * HD] = dv_acc[h].astype(
                bf16
            )
        return carry

    lax.fori_loop(0, key_blocks, one_key_block, 0)
    grads[:, 0:width] = (dq_acc[...] * SCALE).astype(bf16).T
    for b in range(blocks):
        dv_ref[b, 0] = grads[b * span : (b + 1) * span, 2 * width : 3 * width].T

    @pl.when(fresh_ref[0] == 0)
    def _():
        grads[:, 2 * width : 3 * width] = jnp.zeros((count, width), bf16)

    dx_ref[...] = dot(grads[...], w_ref[...]).astype(bf16).reshape(dx_ref.shape)
    dw = dot(grads[...], x_ref[...].reshape(count, width_in), TN)
    db = jnp.sum(grads[...].astype(f32), axis=0, keepdims=True)

    @pl.when(n == 0)
    def _():
        dw_ref[...] = dw
        db_ref[...] = db

    @pl.when(n > 0)
    def _():
        dw_ref[...] += dw
        db_ref[...] += db

    @pl.when(n == pl.num_programs(0) - 1)
    def _():
        tiles[...] = jnp.zeros_like(tiles)
        for which, (start, per_row) in enumerate(
            ((0, D // TILE), (N_OUT, D // TILE), (2 * N_OUT, VW // TILE))
        ):

            def put(group):
                for piece in range(heads):
                    unit = group * heads + piece
                    rows = pl.ds(pl.multiple_of((unit % 2) * HD, HD), HD)
                    at = which * width + piece * HD
                    for r in range(D // TILE):
                        tiles[start + r * per_row + unit // 2, rows, :] = dw_ref[
                            at : at + HD, r * TILE : (r + 1) * TILE
                        ].astype(bf16)

            if which < 2:
                put(group_ref[0])
            else:
                pl.when(fresh_ref[0] == 1)(lambda: put(group_ref[0]))
        copy = pltpu.make_async_copy(tiles, all_ref.at[pl.ds(0, N_QKV)], sem.at[0])
        copy.start()
        copy.wait()


def attend_backward(lengths, fresh, group, q, k, v, o, g, lse, x, w, all_tiles):
    blocks, seqs, span, _ = x.shape
    width = q.shape[1]
    heads = width // HD
    count = blocks * span
    one = lambda shape: pl.BlockSpec((1,) + shape, lambda i, *_: (i,) + (0,) * len(shape))
    mid = lambda shape: pl.BlockSpec((blocks, 1) + shape, lambda i, *_: (0, i, 0, 0))
    return pl.pallas_call(
        functools.partial(attend_backward_kernel, heads),
        grid_spec=pltpu.PrefetchScalarGridSpec(
            num_scalar_prefetch=3,
            grid=(seqs,),
            in_specs=[
                one((width, count)),
                one((width, count)),
                one((width, count)),
                mid((width, span)),
                mid((width, span)),
                one((8, count)),
                mid((span, D)),
                whole((3 * width, D)),
                pl.BlockSpec(memory_space=pl.ANY),
            ],
            out_specs=[
                mid((span, D)),
                mid((width, span)),
                pl.BlockSpec(memory_space=pl.ANY),
                whole((1, 3 * width)),
            ],
            scratch_shapes=[
                pltpu.VMEM((3 * width, D), f32),
                pltpu.VMEM((N_QKV, TILE, TILE), bf16),
                pltpu.SemaphoreType.DMA((1,)),
            ]
            + [pltpu.VMEM((heads, count, HD), bf16)] * 4
            + [
                pltpu.VMEM((width, count), bf16),
                pltpu.VMEM((width, count), bf16),
                pltpu.VMEM((width, count), f32),
                pltpu.VMEM((8, count), f32),
                pltpu.VMEM((count, 3 * width), bf16),
                pltpu.VMEM((heads, BACK_KEY_BLOCK, HD), f32),
                pltpu.VMEM((heads, BACK_KEY_BLOCK, HD), f32),
            ],
        ),
        out_shape=[
            jax.ShapeDtypeStruct((blocks, seqs, span, D), bf16),
            jax.ShapeDtypeStruct((blocks, seqs, width, span), bf16),
            jax.ShapeDtypeStruct(all_tiles.shape, bf16),
            jax.ShapeDtypeStruct((1, 3 * width), f32),
        ],
        input_output_aliases={11: 2},
        compiler_params=params(),
        cost_estimate=pl.CostEstimate(
            flops=70_000_000_000, bytes_accessed=25_000_000, transcendentals=0
        ),
        name="attend_backward",
    )(lengths, fresh, group, q, k, v, o, g, lse, x, w, all_tiles)


HIDDEN_CHUNK = 512
GELU_A = 0.7978845608028654
GELU_B = 0.044715


def feed_forward_kernel(
    len_ref,
    pos_ref,
    att_ref,
    tok_ref,
    cot_ref,
    tiles_ref,
    rows_ref,
    hb_ref,
    out_ref,
    rg_ref,
    ag_ref,
    act_ref,
    hg_ref,
    nt_ref,
    bg_ref,
    og_ref,
    sums_ref,
    hsum_ref,
    tiles,
    w_out,
    w_hidden,
    w_proj,
    output_acc,
    norm_acc,
    sem,
):
    n = pl.program_id(0)
    span = tok_ref.shape[1]

    @pl.when(n == 0)
    def _():
        copies = []
        for i, (start, amount) in enumerate(
            ((0, N_OUT), (N_OUT, N_HID), (N_OUT + N_HID, N_PROJ))
        ):
            copy = pltpu.make_async_copy(
                tiles_ref.at[pl.ds(N_QKV + start, amount)],
                tiles.at[pl.ds(start, amount)],
                sem.at[i],
            )
            copy.start()
            copies.append(copy)
        for copy, start, matrix in zip(
            copies, (0, N_OUT, N_OUT + N_HID), (w_out, w_hidden, w_proj)
        ):
            copy.wait()
            row_tiles, col_tiles = matrix.shape[0] // TILE, matrix.shape[1] // TILE

            def place(r, carry):
                at = pl.ds(pl.multiple_of(r * TILE, TILE), TILE)
                for c in range(col_tiles):
                    matrix[at, c * TILE : (c + 1) * TILE] = tiles[start + r * col_tiles + c]
                return carry

            lax.fori_loop(0, row_tiles, place, 0)
        sums_ref[...] = jnp.zeros_like(sums_ref)
        hsum_ref[...] = jnp.zeros_like(hsum_ref)

    gain_two, shift_two = rows_ref[0:1, :], rows_ref[1:2, :]
    out_bias, proj_bias = rows_ref[2:3, :], rows_ref[3:4, :]
    attended = att_ref[...].reshape(D, span)
    residual = tok_ref[0].astype(f32) + dot(attended, w_out[...], TN) + out_bias
    normed, unit, inv = norm_forward(residual, gain_two, shift_two)
    normed = normed.astype(bf16)
    nt_ref[...] = normed
    live = pos_ref[0] + lax.broadcasted_iota(jnp.int32, (span, 1), 0) < len_ref[n]
    out_grad = jnp.where(live, cot_ref[0].astype(f32), 0.0)
    out_grad_low = out_grad.astype(bf16)
    og_ref[...] = out_grad_low
    output_acc[...] = residual + proj_bias
    norm_acc[...] = jnp.zeros_like(norm_acc)

    def chunk(c, carry):
        cols = pl.ds(pl.multiple_of(c * HIDDEN_CHUNK, HIDDEN_CHUNK), HIDDEN_CHUNK)
        hidden = dot(nt_ref[...], w_hidden[:, cols]) + hb_ref[:, cols]
        square = hidden * hidden
        bend = jnp.tanh(GELU_A * (hidden + GELU_B * (hidden * square)))
        active = (0.5 * hidden * (1.0 + bend)).astype(bf16)
        slope = 0.5 * (1.0 + bend) + 0.5 * hidden * (1.0 - bend * bend) * (
            GELU_A * (1.0 + (3.0 * GELU_B) * square)
        )
        act_ref[:, cols] = active
        hidden_grad = (dot(og_ref[...], w_proj[cols, :], NT) * slope).astype(bf16)
        hg_ref[:, cols] = hidden_grad
        hsum_ref[:, cols] += jnp.sum(hidden_grad.astype(f32), axis=0, keepdims=True)
        output_acc[...] += dot(active, w_proj[cols, :])
        norm_acc[...] += dot(hidden_grad, w_hidden[:, cols], NT)
        return carry

    lax.fori_loop(0, FF // HIDDEN_CHUNK, chunk, 0)
    out_ref[0] = output_acc[...].astype(bf16)
    norm_in = norm_acc[...]
    residual_grad = out_grad + norm_backward(norm_in, unit, inv, gain_two)
    rg_ref[0] = residual_grad
    branch = residual_grad.astype(bf16)
    bg_ref[...] = branch
    ag_ref[...] = dot(w_out[...], branch, NT).astype(bf16).reshape(ag_ref.shape)
    sums_ref[0:1, :] += jnp.sum(norm_in * unit, axis=0, keepdims=True)
    sums_ref[1:2, :] += jnp.sum(norm_in, axis=0, keepdims=True)
    sums_ref[2:3, :] += jnp.sum(branch.astype(f32), axis=0, keepdims=True)
    sums_ref[3:4, :] += jnp.sum(out_grad, axis=0, keepdims=True)


def feed_forward(lengths, position, att, tokens, cotangent, tiles, rows, hidden_bias):
    groups, seqs, width, span = att.shape
    one = lambda shape: pl.BlockSpec((1,) + shape, lambda i, *_: (i,) + (0,) * len(shape))
    mid = lambda shape: pl.BlockSpec((groups, 1) + shape, lambda i, *_: (0, i, 0, 0))
    row = lambda cols: pl.BlockSpec((span, cols), lambda i, *_: (i, 0))
    total = seqs * span
    return pl.pallas_call(
        feed_forward_kernel,
        grid_spec=pltpu.PrefetchScalarGridSpec(
            num_scalar_prefetch=2,
            grid=(seqs,),
            in_specs=[
                mid((width, span)),
                one((span, D)),
                one((span, D)),
                pl.BlockSpec(memory_space=pl.ANY),
                whole((8, D)),
                whole((1, FF)),
            ],
            out_specs=[
                one((span, D)),
                one((span, D)),
                mid((width, span)),
                row(FF),
                row(FF),
                row(D),
                row(D),
                row(D),
                whole((8, D)),
                whole((1, FF)),
            ],
            scratch_shapes=[
                pltpu.VMEM((N_REST, TILE, TILE), bf16),
                pltpu.VMEM((D, D), bf16),
                pltpu.VMEM((D, FF), bf16),
                pltpu.VMEM((FF, D), bf16),
                pltpu.VMEM((span, D), f32),
                pltpu.VMEM((span, D), f32),
                pltpu.SemaphoreType.DMA((3,)),
            ],
        ),
        out_shape=[
            jax.ShapeDtypeStruct((seqs, span, D), bf16),
            jax.ShapeDtypeStruct((seqs, span, D), f32),
            jax.ShapeDtypeStruct((groups, seqs, width, span), bf16),
            jax.ShapeDtypeStruct((total, FF), bf16),
            jax.ShapeDtypeStruct((total, FF), bf16),
            jax.ShapeDtypeStruct((total, D), bf16),
            jax.ShapeDtypeStruct((total, D), bf16),
            jax.ShapeDtypeStruct((total, D), bf16),
            jax.ShapeDtypeStruct((8, D), f32),
            jax.ShapeDtypeStruct((1, FF), f32),
        ],
        compiler_params=params(),
        cost_estimate=pl.CostEstimate(
            flops=24_000_000_000, bytes_accessed=40_000_000, transcendentals=0
        ),
        name="feed_forward",
    )(lengths, position, att, tokens, cotangent, tiles, rows, hidden_bias)


GRAD_CHUNK = 256


def weight_grad_kernel(
    att_ref,
    bg_ref,
    og_ref,
    nt_ref,
    act_ref,
    hg_ref,
    all_ref,
    out_tiles,
    hid_tiles,
    proj_tiles,
    og_turned,
    nt_turned,
    sem,
    out_sem,
):
    i = pl.program_id(0)
    last = pl.num_programs(0) - 1
    groups, seqs, width, span = att_ref.shape
    d_tiles, f_tiles, per = D // TILE, FF // TILE, GRAD_CHUNK // TILE
    spare = all_ref.shape[0] - N_QKV - N_REST
    slot = lax.rem(i, 2)

    def first_copies():
        copies = [
            pltpu.make_async_copy(
                out_tiles.at[pl.ds(0, N_OUT)], all_ref.at[pl.ds(N_QKV, N_OUT)], out_sem.at[0]
            )
        ]
        if spare:
            copies.append(
                pltpu.make_async_copy(
                    out_tiles.at[pl.ds(N_OUT, spare)],
                    all_ref.at[pl.ds(N_QKV + N_REST, spare)],
                    out_sem.at[1],
                )
            )
        return copies

    def copies_of(step, slot):
        made = [
            pltpu.make_async_copy(
                hid_tiles.at[slot, r],
                all_ref.at[pl.ds(N_QKV + N_OUT + r * f_tiles + step * per, per)],
                sem.at[slot, r],
            )
            for r in range(d_tiles)
        ]
        made.append(
            pltpu.make_async_copy(
                proj_tiles.at[slot],
                all_ref.at[pl.ds(FIRST_PROJ + step * per * d_tiles, per * d_tiles)],
                sem.at[slot, d_tiles],
            )
        )
        return made

    @pl.when(i == 0)
    def _():
        og_turned[...] = og_ref[...].T
        nt_turned[...] = nt_ref[...].T
        total = jnp.zeros((D, D), f32)
        for s in range(seqs):
            total = total + dot(
                att_ref[:, s].reshape(groups * width, span), bg_ref[s * span : (s + 1) * span, :]
            )
        total = total.astype(bf16)
        for r in range(d_tiles):
            for c in range(d_tiles):
                out_tiles[r * d_tiles + c] = total[
                    r * TILE : (r + 1) * TILE, c * TILE : (c + 1) * TILE
                ]
        if spare:
            out_tiles[N_OUT : N_OUT + spare] = jnp.zeros((spare, TILE, TILE), bf16)
        for copy in first_copies():
            copy.start()

    proj = dot(og_turned[...], act_ref[...]).astype(bf16)
    hid = dot(nt_turned[...], hg_ref[...]).astype(bf16)

    @pl.when(i >= 2)
    def _():
        for copy in copies_of(i - 2, slot):
            copy.wait()

    for c in range(per):
        for r in range(d_tiles):
            rows, cols = slice(r * TILE, (r + 1) * TILE), slice(c * TILE, (c + 1) * TILE)
            proj_tiles[slot, c * d_tiles + r] = proj[rows, cols]
            hid_tiles[slot, r, c] = hid[rows, cols]
    for copy in copies_of(i, slot):
        copy.start()

    @pl.when(i == last)
    def _():
        for copy in copies_of(i - 1, 1 - slot):
            copy.wait()
        for copy in copies_of(i, slot):
            copy.wait()
        for copy in first_copies():
            copy.wait()


def weight_grads(total_tiles, att, bg, og, nt, act, hg):
    total = bg.shape[0]
    chunks = FF // GRAD_CHUNK
    per = GRAD_CHUNK // TILE
    spare = total_tiles - N_QKV - N_REST
    return pl.pallas_call(
        weight_grad_kernel,
        grid=(chunks,),
        in_specs=[
            whole(att.shape),
            whole(bg.shape),
            whole(og.shape),
            whole(nt.shape),
            pl.BlockSpec((total, GRAD_CHUNK), lambda i: (0, i)),
            pl.BlockSpec((total, GRAD_CHUNK), lambda i: (0, i)),
        ],
        out_specs=pl.BlockSpec(memory_space=pl.ANY),
        out_shape=jax.ShapeDtypeStruct((total_tiles, TILE, TILE), bf16),
        scratch_shapes=[
            pltpu.VMEM((N_OUT + spare, TILE, TILE), bf16),
            pltpu.VMEM((2, D // TILE, per, TILE, TILE), bf16),
            pltpu.VMEM((2, per * (D // TILE), TILE, TILE), bf16),
            pltpu.VMEM((D, total), bf16),
            pltpu.VMEM((D, total), bf16),
            pltpu.SemaphoreType.DMA((2, D // TILE + 1)),
            pltpu.SemaphoreType.DMA((2,)),
        ],
        compiler_params=params(),
        cost_estimate=pl.CostEstimate(
            flops=12_000_000_000, bytes_accessed=40_000_000, transcendentals=0
        ),
        name="weight_grads",
    )(att, bg, og, nt, act, hg)


def bits_of(size):
    return size.bit_length() - 1


def exchange_bits(dp, seq):
    return (
        [("seq", 0)]
        + [("dp", b) for b in range(bits_of(dp))]
        + [("seq", b) for b in range(1, bits_of(seq))]
    )


def partner_of(axis, bit):
    here = {"dp": lax.axis_index("dp"), "seq": lax.axis_index("seq")}
    side = (here[axis] // (1 << bit)) % 2
    here[axis] = here[axis] + (1 << bit) * (1 - 2 * side)
    return (here["dp"], here["seq"]), side


def greet(partners):
    barrier = pltpu.get_barrier_semaphore()
    for device in partners:
        pl.semaphore_signal(barrier, inc=1, device_id=device, device_id_type=MESH)
    pl.semaphore_wait(barrier, len(partners))


def tile_sum_kernel(stages, chunks, g_ref, out_ref, mine, *rest):
    count = len(stages)
    received = rest[:count]
    send_sem, recv_sem, copy_sem = rest[count:]
    partners = [partner_of(axis, bit) for axis, bit, _, _ in stages]
    greet([device for device, _ in partners])

    def view(ref, above, below):
        return ref.reshape(above, 2, below, *ref.shape[-3:])

    def send(stage, k):
        _, _, above, below = stages[stage]
        device, side = partners[stage]
        source = g_ref if stage == 0 else received[stage - 1]
        at = pl.ds(*chunks[k])
        return pltpu.make_async_remote_copy(
            src_ref=view(source, above, below).at[:, 1 - side, :, at],
            dst_ref=received[stage].reshape(above, below, *received[stage].shape[-3:]).at[:, :, at],
            send_sem=send_sem.at[stage, k],
            recv_sem=recv_sem.at[stage, k],
            device_id=device,
            device_id_type=MESH,
        )

    def own(k):
        _, _, above, below = stages[0]
        at = pl.ds(*chunks[k])
        return pltpu.make_async_copy(
            view(g_ref, above, below).at[:, partners[0][1], :, at],
            mine.reshape(above, below, *mine.shape[-3:]).at[:, :, at],
            copy_sem.at[k],
        )

    for k in range(len(chunks)):
        send(0, k).start()
        own(k).start()
    for step in range(1, len(chunks) + count):
        for k in range(len(chunks)):
            stage = step - k
            if not 1 <= stage <= count:
                continue
            send(stage - 1, k).wait_recv()
            _, _, above, below = stages[stage - 1]
            side = partners[stage - 1][1]
            at = pl.ds(*chunks[k])
            if stage == 1:
                own(k).wait()

            def add(i, carry):
                if stage == 1:
                    kept = mine[i, at]
                else:
                    up, low = i // below, i % below
                    kept = received[stage - 2][(up * 2 + side) * below + low, at]
                total = kept.astype(f32) + received[stage - 1][i, at].astype(f32)
                if stage == count:
                    out_ref[at] = total
                else:
                    received[stage - 1][i, at] = total.astype(bf16)
                return carry

            lax.fori_loop(0, above * below, add, 0)
            if stage < count:
                send(stage, k).start()
    for stage in range(count):
        for k in range(len(chunks)):
            send(stage, k).wait_send()


def tile_sum(g, dp, seq):
    devices = dp * seq
    owned = g.shape[0] // devices
    tail = (owned, TILE, TILE)
    left = [("dp", b) for b in reversed(range(bits_of(dp)))] + [
        ("seq", b) for b in reversed(range(bits_of(seq)))
    ]
    stages = []
    for axis, bit in exchange_bits(dp, seq):
        place = left.index((axis, bit))
        stages.append((axis, bit, 1 << place, 1 << (len(left) - 1 - place)))
        left.pop(place)
    pieces = min(4, owned)
    edges = [owned * p // pieces for p in range(pieces + 1)]
    chunks = [(low, high - low) for low, high in zip(edges, edges[1:])]
    buffers = [
        pltpu.VMEM((devices >> (i + 1),) + tail, bf16) for i in range(len(stages))
    ]
    return pl.pallas_call(
        functools.partial(tile_sum_kernel, stages, chunks),
        in_specs=[pl.BlockSpec(memory_space=pl.ANY)],
        out_specs=pl.BlockSpec(memory_space=pltpu.VMEM),
        out_shape=jax.ShapeDtypeStruct(tail, f32),
        scratch_shapes=[pltpu.VMEM((devices // 2,) + tail, bf16)]
        + buffers
        + [
            pltpu.SemaphoreType.DMA((len(stages), len(chunks))),
            pltpu.SemaphoreType.DMA((len(stages), len(chunks))),
            pltpu.SemaphoreType.DMA((len(chunks),)),
        ],
        compiler_params=pltpu.CompilerParams(
            collective_id=1, has_side_effects=True, vmem_limit_bytes=VMEM_LIMIT
        ),
        cost_estimate=pl.CostEstimate(
            flops=60_000_000_000, bytes_accessed=40_000_000, transcendentals=0
        ),
        name="tile_sum",
    )(g.reshape((devices,) + tail))


AXIS_BITS = {
    "far": ("dp", 2),
    "near": ("dp", 1),
    "y": ("dp", 0),
    "x": ("seq", 1),
    "core": ("seq", 0),
}
ADDRESS = ("far", "near", "y", "x")
FLOW_ORDERS = (("y", "near", "far", "x"), ("near", "x", "y", "far"), ("x", "y", "near", "far"))
HALF = TILE // 2


def flow_stages(order):
    left = list(ADDRESS)
    stages = []
    for name in order:
        place = left.index(name)
        stages.append((name, 1 << place, 1 << (len(left) - 1 - place)))
        left.pop(place)
    return stages


def paired_grad_kernel(
    att_ref,
    bg_ref,
    og_ref,
    nt_ref,
    act_ref,
    hg_ref,
    half_ref,
    made,
    landed,
    done,
    out_made,
    out_landed,
    out_done,
    zeros,
    og_turned,
    nt_turned,
    send_sem,
    recv_sem,
    done_sem,
    out_sem,
    zero_sem,
):
    i = pl.program_id(0)
    last = pl.num_programs(0) - 1
    groups, seqs, width, span = att_ref.shape
    d_tiles, f_tiles, per = D // TILE, FF // TILE, GRAD_CHUNK // TILE
    count = per * d_tiles
    spare = half_ref.shape[0] - N_QKV - N_REST
    sibling, core = partner_of("seq", 0)
    kept = pl.ds(pl.multiple_of(core * HALF, HALF), HALF)
    given = pl.ds(pl.multiple_of((1 - core) * HALF, HALF), HALF)
    slot = lax.rem(i, 2)

    def to_sibling(step, slot):
        return pltpu.make_async_remote_copy(
            src_ref=made.at[slot, :, given],
            dst_ref=landed.at[step],
            send_sem=send_sem.at[slot],
            recv_sem=recv_sem.at[step],
            device_id=sibling,
            device_id_type=MESH,
        )

    def out_to_sibling():
        return pltpu.make_async_remote_copy(
            src_ref=out_made.at[:, given],
            dst_ref=out_landed,
            send_sem=out_sem.at[0],
            recv_sem=out_sem.at[1],
            device_id=sibling,
            device_id_type=MESH,
        )

    def out_copy():
        return pltpu.make_async_copy(out_done, half_ref.at[pl.ds(N_QKV, N_OUT)], out_sem.at[2])

    def zero_copies():
        spots = [(N_QKV // 3 * j, N_QKV // 3) for j in range(3)]
        if spare:
            spots.append((N_QKV + N_REST, spare))
        return [
            pltpu.make_async_copy(
                zeros.at[pl.ds(0, size)], half_ref.at[pl.ds(low, size)], zero_sem.at[j]
            )
            for j, (low, size) in enumerate(spots)
        ]

    def done_copies(step, slot):
        copies = [
            pltpu.make_async_copy(
                done.at[slot, pl.ds(r * per, per)],
                half_ref.at[pl.ds(N_QKV + N_OUT + r * f_tiles + step * per, per)],
                done_sem.at[slot, r],
            )
            for r in range(d_tiles)
        ]
        copies.append(
            pltpu.make_async_copy(
                done.at[slot, pl.ds(count, count)],
                half_ref.at[pl.ds(FIRST_PROJ + step * count, count)],
                done_sem.at[slot, d_tiles],
            )
        )
        return copies

    @pl.when(i == 0)
    def _():
        greet([sibling])
        zeros[...] = jnp.zeros_like(zeros)
        for copy in zero_copies():
            copy.start()
        total = jnp.zeros((D, D), f32)
        for s in range(seqs):
            total = total + dot(
                att_ref[:, s].reshape(groups * width, span), bg_ref[s * span : (s + 1) * span, :]
            )
        total = total.astype(bf16)
        for r in range(d_tiles):
            for c in range(d_tiles):
                out_made[r * d_tiles + c] = total[
                    r * TILE : (r + 1) * TILE, c * TILE : (c + 1) * TILE
                ]
        out_to_sibling().start()
        og_turned[...] = og_ref[...].T
        nt_turned[...] = nt_ref[...].T

    @pl.when(i < last)
    def _():
        @pl.when(i >= 2)
        def _():
            to_sibling(i - 2, slot).wait_send()

        proj = dot(og_turned[...], act_ref[...]).astype(bf16)
        hid = dot(nt_turned[...], hg_ref[...]).astype(bf16)
        for c in range(per):
            for r in range(d_tiles):
                rows, cols = slice(r * TILE, (r + 1) * TILE), slice(c * TILE, (c + 1) * TILE)
                made[slot, count + c * d_tiles + r] = proj[rows, cols]
                made[slot, r * per + c] = hid[rows, cols]
        to_sibling(i, slot).start()

    @pl.when(i >= 1)
    def _():
        before = 1 - slot

        @pl.when(i >= 3)
        def _():
            for copy in done_copies(i - 3, before):
                copy.wait()

        to_sibling(i - 1, before).wait_recv()
        done[before] = (
            made[before, :, kept].astype(f32) + landed[i - 1].astype(f32)
        ).astype(bf16)
        for copy in done_copies(i - 1, before):
            copy.start()

    @pl.when(i == 1)
    def _():
        out_to_sibling().wait_recv()
        out_done[...] = (out_made[:, kept].astype(f32) + out_landed[...].astype(f32)).astype(bf16)
        out_copy().start()

    @pl.when(i == last)
    def _():
        to_sibling(i - 2, slot).wait_send()
        to_sibling(i - 1, 1 - slot).wait_send()
        out_to_sibling().wait_send()
        out_copy().wait()
        for copy in zero_copies():
            copy.wait()
        for copy in done_copies(i - 2, slot):
            copy.wait()
        for copy in done_copies(i - 1, 1 - slot):
            copy.wait()


def paired_grads(total_tiles, att, bg, og, nt, act, hg):
    total = bg.shape[0]
    chunks = FF // GRAD_CHUNK
    per = GRAD_CHUNK // TILE
    count = per * (D // TILE)
    dma = pltpu.SemaphoreType.DMA
    column = pl.BlockSpec((total, GRAD_CHUNK), lambda i: (0, jnp.minimum(i, chunks - 1)))
    return pl.pallas_call(
        paired_grad_kernel,
        grid=(chunks + 1,),
        in_specs=[whole(a.shape) for a in (att, bg, og, nt)] + [column, column],
        out_specs=pl.BlockSpec(memory_space=pl.ANY),
        out_shape=jax.ShapeDtypeStruct((total_tiles, HALF, TILE), bf16),
        scratch_shapes=[
            pltpu.VMEM((2, 2 * count, TILE, TILE), bf16),
            pltpu.VMEM((chunks, 2 * count, HALF, TILE), bf16),
            pltpu.VMEM((2, 2 * count, HALF, TILE), bf16),
            pltpu.VMEM((N_OUT, TILE, TILE), bf16),
            pltpu.VMEM((N_OUT, HALF, TILE), bf16),
            pltpu.VMEM((N_OUT, HALF, TILE), bf16),
            pltpu.VMEM((N_QKV // 3, HALF, TILE), bf16),
            pltpu.VMEM((D, total), bf16),
            pltpu.VMEM((D, total), bf16),
            dma((2,)),
            dma((chunks,)),
            dma((2, D // TILE + 1)),
            dma((3,)),
            dma((4,)),
        ],
        compiler_params=pltpu.CompilerParams(
            dimension_semantics=("arbitrary",),
            collective_id=4,
            has_side_effects=True,
            vmem_limit_bytes=VMEM_LIMIT,
        ),
        cost_estimate=pl.CostEstimate(
            flops=12_000_000_000, bytes_accessed=40_000_000, transcendentals=0
        ),
        name="paired_grads",
    )(att, bg, og, nt, act, hg)


Q_UNITS = 27


def attend_back_sum_kernel(
    heads,
    flows,
    len_ref,
    fresh_ref,
    q_ref,
    k_ref,
    v_ref,
    o_ref,
    g_ref,
    lse_ref,
    x_ref,
    w_ref,
    half_ref,
    in_ref,
    dv_ref,
    raw_ref,
    db_ref,
    dw,
    q_wide,
    k_wide,
    g_wide,
    v_wide,
    g_turned,
    dq_acc,
    delta,
    grads,
    dk_acc,
    dv_acc,
    probs,
    score_grads,
    dxs,
    dx_core,
    dx_across,
    in_made,
    mine,
    final,
    final_other,
    q_parts,
    q_y,
    q_near,
    q_far,
    q_own,
    core_sem,
    across_sem,
    in_sem,
    own_sem,
    flow_send,
    flow_recv,
    final_sem,
    q_send,
    q_recv,
    q_out,
    q_in,
    *lands,
):
    i = pl.program_id(0)
    blocks, _, span, width_in = x_ref.shape
    count = blocks * span
    width = heads * HD
    bq, bk = BACK_QUERY_BLOCK, BACK_KEY_BLOCK
    per_seq = count // bk
    seqs = dxs.shape[0]
    n, ki = i // per_seq, i % per_seq
    length = len_ref[n]
    dp, s = lax.axis_index("dp"), lax.axis_index("seq")
    y, x, core = dp % 2, s // 2, s % 2
    near, far = (dp // 2) % 2, dp // 4
    owned = raw_ref.shape[0]
    first_tile = (dp * 4 + s) * owned
    partners = {name: partner_of(axis, bit) for name, (axis, bit) in AXIS_BITS.items()}

    def view(ref, above, below):
        return ref.reshape(above, 2, below, *ref.shape[-3:])

    def flow_send_copy(f, k):
        low, size, stages = flows[f]
        name, above, below = stages[k]
        device, side = partners[name]
        land = lands[f * 4 + k]
        if k == 0:
            source = view(half_ref, above, below).at[:, 1 - side, :, pl.ds(low, size)]
        else:
            source = view(lands[f * 4 + k - 1], above, below).at[:, 1 - side]
        return pltpu.make_async_remote_copy(
            src_ref=source,
            dst_ref=land.reshape(above, below, *land.shape[-3:]),
            send_sem=flow_send.at[f, k],
            recv_sem=flow_recv.at[f, k],
            device_id=device,
            device_id_type=MESH,
        )

    def own_copy(f):
        low, size, stages = flows[f]
        name, above, below = stages[0]
        return pltpu.make_async_copy(
            view(half_ref, above, below).at[:, partners[name][1], :, pl.ds(low, size)],
            mine.reshape(above, below, *mine.shape[-3:]).at[:, :, pl.ds(0, size)],
            own_sem.at[f],
        )

    def flow_add(f, k):
        low, size, stages = flows[f]
        name, above, below = stages[k]
        side = partners[name][1]
        land = lands[f * 4 + k]
        flow_send_copy(f, k).wait_recv()
        if k == 0:
            own_copy(f).wait()

        def add(e, carry):
            if k == 0:
                kept = mine[e, 0:size]
            else:
                kept = lands[f * 4 + k - 1][((e // below) * 2 + side) * below + e % below]
            total = kept.astype(f32) + land[e].astype(f32)
            if k == 3:
                final[low : low + size] = total
            else:
                land[e] = total.astype(bf16)
            return carry

        lax.fori_loop(0, above * below, add, 0)

    def dx_core_copy(m, block):
        return pltpu.make_async_remote_copy(
            src_ref=dxs.at[m, block],
            dst_ref=dx_core.at[m, block // 2],
            send_sem=core_sem.at[m, block // 2, 0],
            recv_sem=core_sem.at[m, block // 2, 1],
            device_id=partners["core"][0],
            device_id_type=MESH,
        )

    def dx_across_copy(m):
        return pltpu.make_async_remote_copy(
            src_ref=dx_core.at[m, 1 - x],
            dst_ref=dx_across.at[m],
            send_sem=across_sem.at[m, 0],
            recv_sem=across_sem.at[m, 1],
            device_id=partners["x"][0],
            device_id_type=MESH,
        )

    def dx_pass(m, block):
        @pl.when(block % 2 == core)
        def _():
            dx_core_copy(m, block).wait_recv()

            @pl.when(block // 2 != x)
            def _():
                dx_core[m, 1 - x] = (
                    dxs[m, block].astype(f32) + dx_core[m, 1 - x].astype(f32)
                ).astype(bf16)
                dx_across_copy(m).start()

    def dx_end(m):
        dx_across_copy(m).wait_recv()
        if m:
            in_copy(m - 1).wait()
        in_made[...] = (
            dxs[m, s].astype(f32) + dx_core[m, x].astype(f32) + dx_across[m].astype(f32)
        )
        in_copy(m).start()

    def in_copy(m):
        return pltpu.make_async_copy(in_made, in_ref.at[m], in_sem.at[m])

    @pl.when(i == 0)
    def _():
        mates = [
            (dp - y + (y + dy) % 2, (s + ds) % 4) for dy in range(2) for ds in range(4) if dy or ds
        ]
        greet(mates + [partners["near"][0], partners["far"][0]])
        for f in range(3):
            flow_send_copy(f, 0).start()
        own_copy(0).start()
        delta[...] = jnp.zeros_like(delta)
        dw[...] = jnp.zeros_like(dw)
        db_ref[...] = jnp.zeros_like(db_ref)

    @pl.when(i == per_seq - 1)
    def _():
        for f in range(3):
            flow_add(f, 0)
            if f < 2:
                own_copy(f + 1).start()
            flow_send_copy(f, 1).start()

    @pl.when(i > 0)
    def _():
        dx_pass((i - 1) // per_seq, (i - 1) % per_seq)

    @pl.when(i == per_seq + 1)
    def _():
        for f in range(3):
            flow_add(f, 1)
            flow_send_copy(f, 2).start()

    @pl.when(i == per_seq + 2)
    def _():
        for f in range(1, 3):
            flow_add(f, 2)
            flow_send_copy(f, 3).start()

    @pl.when(i == per_seq + 3)
    def _():
        flow_add(0, 2)
        flow_send_copy(0, 3).start()

    @pl.when(ki == 0)
    def _():
        row = lax.broadcasted_iota(jnp.int32, (16, count), 0)
        dead = lax.broadcasted_iota(jnp.int32, (16, count), 1) >= length
        ones = jnp.where(row < 3, 1.0, 0.0)
        key_side = jnp.where((row == 3) & dead, masked_score, ones).astype(bf16)
        ones = ones.astype(bf16)

        def in_parts(line, last):
            high = line.astype(bf16).astype(f32)
            rest = line - high
            middle = rest.astype(bf16).astype(f32)
            low = rest - middle
            parts = jnp.where(row == 0, high, jnp.where(row == 1, middle, low))
            return jnp.where(row < 3, parts, jnp.where(row == 3, last, 0.0)).astype(bf16)

        for b in range(blocks):
            at = slice(b * span, (b + 1) * span)
            g_block = g_ref[b, 0]
            g_turned[:, at] = g_block
            product = o_ref[b, 0].astype(f32) * g_block.astype(f32)
            for h in range(heads):
                rows = slice(h * HD, (h + 1) * HD)
                delta[h : h + 1, at] = jnp.sum(product[rows, :], axis=0, keepdims=True)
        for h in range(heads):
            rows = slice(h * HD, (h + 1) * HD)
            lse_part = in_parts(lse_ref[0, h : h + 1, :] * (-1.0 / (SCALE * LOG2E)), 1.0)
            delta_part = in_parts(-delta[h : h + 1, :], 0.0)
            q_wide[h] = jnp.concatenate([q_ref[0, rows, :], lse_part], axis=0).T
            g_wide[h] = jnp.concatenate([g_turned[rows, :], delta_part], axis=0).T
            k_wide[h, 0:HD] = k_ref[0, rows, :]
            k_wide[h, HD : HD + 16] = key_side
            v_wide[h, 0:HD] = v_ref[0, rows, :]
            v_wide[h, HD : HD + 16] = ones
        dq_acc[...] = jnp.zeros_like(dq_acc)

    k0 = pl.multiple_of(ki * bk, bk)
    dk_acc[...] = jnp.zeros_like(dk_acc)
    dv_acc[...] = jnp.zeros_like(dv_acc)

    def step(qi, masked, low=0, cols_here=bk):
        skip = low if masked else 0
        here = slice(low, low + cols_here)
        keys = pl.ds(pl.multiple_of(k0 + low, HALF_BLOCK), cols_here)
        at = pl.ds(pl.multiple_of(qi * bq + skip, HALF_BLOCK), bq - skip)
        tall = bq - skip
        for h in range(heads):
            rows = slice(h * HD, (h + 1) * HD)
            for c0 in range(0, cols_here, SUB_COLS):
                some = pl.ds(pl.multiple_of(k0 + low + c0, TILE), SUB_COLS)
                cols = slice(c0, c0 + SUB_COLS)
                for r0 in range(0, tall, SUB_ROWS):
                    part = pl.ds(pl.multiple_of(qi * bq + skip + r0, TILE), SUB_ROWS)
                    p = jnp.exp2(dot(q_wide[h, part, :], k_wide[h, :, some]) * (SCALE * LOG2E))
                    if masked and r0 < c0 + SUB_COLS - 1:
                        shape = (SUB_ROWS, SUB_COLS)
                        allowed = c0 + lax.broadcasted_iota(
                            jnp.int32, shape, 1
                        ) <= r0 + lax.broadcasted_iota(jnp.int32, shape, 0)
                        p = jnp.where(allowed, p, 0.0)
                    probs[h, r0 : r0 + SUB_ROWS, cols] = p.astype(bf16)
                    score_grads[h, r0 : r0 + SUB_ROWS, cols] = (
                        p * dot(g_wide[h, part, :], v_wide[h, :, some])
                    ).astype(bf16)
        for h in range(heads):
            rows = slice(h * HD, (h + 1) * HD)
            p = probs[h, 0:tall, 0:cols_here]
            ds = score_grads[h, 0:tall, 0:cols_here]
            dv_acc[rows, here] = dv_acc[rows, here] + dot(g_turned[rows, at], p)
            dk_acc[rows, here] = dk_acc[rows, here] + dot(q_ref[0, rows, at], ds)
            dq_acc[rows, at] = dq_acc[rows, at] + dot(k_ref[0, rows, keys], ds, NT)

    step(ki, True, 0, HALF_BLOCK)
    step(ki, True, HALF_BLOCK, HALF_BLOCK)
    lax.fori_loop(ki + 1, count // bq, lambda j, c: (step(j, False), c)[1], 0)
    grads[0:width, :] = (dq_acc[:, pl.ds(k0, bk)] * SCALE).astype(bf16)
    grads[width : 2 * width, :] = (dk_acc[...] * SCALE).astype(bf16)
    grads[2 * width :, :] = dv_acc[...].astype(bf16)
    dv_ref[ki, 0] = grads[2 * width :, :]

    @pl.when(x == 1)
    def _():
        grads[2 * width :, :] = jnp.zeros((width, bk), bf16)

    dw[...] += dot(grads[...], x_ref[ki, 0])
    db_ref[...] += dot(jnp.ones((8, bk), bf16), grads[...], NT)[0:1]

    def q_copy(kind, c):
        at = pl.ds(c * 9, 9)
        if kind == 0:
            source, target, name = q_parts.at[1 - y, at], q_y.at[at], "y"
        elif kind == 1:
            source, target, name = q_y.at[at], q_near.at[at], "near"
        else:
            source, target, name = q_y.at[at], q_far.at[at], "far"
        return pltpu.make_async_remote_copy(
            src_ref=source,
            dst_ref=target,
            send_sem=q_send.at[kind, c],
            recv_sem=q_recv.at[kind, c],
            device_id=partners[name][0],
            device_id_type=MESH,
        )

    def q_deliver(c, act):
        for e in range(c * 9, c * 9 + 9):
            r = 3 * y + (e // 3) % 3
            unit = core * 3 + e % 3
            if c < 2:
                index = c * N_OUT + r * (D // TILE) + 3 * x + unit // 2
            else:
                index = 2 * N_OUT + r * (VW // TILE) + unit // 2
            owner = index // owned
            target = (owner // 4, owner % 4)
            rows = pl.ds(pl.multiple_of((unit % 2) * HALF, HALF), HALF)
            here = (target[0] == dp) & (target[1] == s)
            real = (x == 0) if c == 2 else (x >= 0)
            spot = q_own.at[index % owned, rows]

            @pl.when(real & here)
            def _():
                if act == "start":
                    pltpu.make_async_copy(q_y.at[e], spot, q_in).start()

            @pl.when(real & jnp.logical_not(here))
            def _():
                copy = pltpu.make_async_remote_copy(
                    src_ref=q_y.at[e],
                    dst_ref=spot,
                    send_sem=q_out.at[e],
                    recv_sem=q_in,
                    device_id=target,
                    device_id_type=MESH,
                )
                if act == "start":
                    copy.start()
                else:
                    copy.wait_send()

    def q_add(c, extra):
        at = slice(c * 9, c * 9 + 9)
        kept = q_parts[y, at] if extra is q_y else q_y[at]
        q_y[at] = (kept.astype(f32) + extra[at].astype(f32)).astype(bf16)

    @pl.when(i == seqs * per_seq - 1)
    def _():
        for e in range(Q_UNITS):
            which, rr, piece = e // 9, (e // 3) % 3, e % 3
            at = which * width + piece * HALF
            for yy in range(2):
                r = 3 * yy + rr
                q_parts[yy, e] = dw[at : at + HALF, r * TILE : (r + 1) * TILE].astype(bf16)
        for c in range(3):
            q_copy(0, c).start()

    dxs[n, ki] = dot(grads[...], w_ref[...], TN).astype(bf16)

    @pl.when(ki % 2 != core)
    def _():
        dx_core_copy(n, ki).start()

    @pl.when(i == seqs * per_seq - 1)
    def _():
        to_sibling = pltpu.make_async_remote_copy(
            src_ref=final.at[pl.ds((1 - core) * owned, owned)],
            dst_ref=final_other,
            send_sem=final_sem.at[0],
            recv_sem=final_sem.at[1],
            device_id=partners["core"][0],
            device_id_type=MESH,
        )

        def q_first(c):
            q_copy(0, c).wait_recv()
            q_add(c, q_y)

            @pl.when(near == 1)
            def _():
                q_copy(1, c).start()

        def q_second(c):
            @pl.when(near == 0)
            def _():
                q_copy(1, c).wait_recv()
                q_add(c, q_near)

                @pl.when(far == 1)
                def _():
                    q_copy(2, c).start()

        def q_third(c):
            @pl.when((near == 0) & (far == 0))
            def _():
                q_copy(2, c).wait_recv()
                q_add(c, q_far)
                q_deliver(c, "start")

        q_first(0)
        dx_pass(seqs - 1, per_seq - 1)
        q_first(1)
        q_second(0)
        q_first(2)
        q_second(1)
        for f in range(3):
            flow_add(f, 3)
        to_sibling.start()
        q_third(0)
        q_second(2)
        q_third(1)
        dx_end(0)
        q_third(2)
        to_sibling.wait_recv()
        kept = pl.ds(pl.multiple_of(core * HALF, HALF), HALF)
        given = pl.ds(pl.multiple_of((1 - core) * HALF, HALF), HALF)
        raw_ref[:, kept, :] = final[pl.ds(core * owned, owned)]
        raw_ref[:, given, :] = final_other[...]
        for m in range(1, seqs):
            dx_end(m)

        @pl.when(first_tile + owned <= N_QKV)
        def _():
            pltpu.make_async_copy(q_own, q_own, q_in).wait()
            raw_ref[...] = q_own[...].astype(f32)

        part = N_QKV % owned
        if part:

            @pl.when((first_tile < N_QKV) & (first_tile + owned > N_QKV))
            def _():
                at = pl.ds(0, part)
                pltpu.make_async_copy(q_own.at[at], q_own.at[at], q_in).wait()
                raw_ref[0:part] = q_own[0:part].astype(f32)

        in_copy(seqs - 1).wait()
        to_sibling.wait_send()
        for m in range(seqs):
            for pair in range(2):
                dx_core_copy(m, 2 * pair + 1 - core).wait_send()
            dx_across_copy(m).wait_send()
        for f in range(3):
            for k in range(4):
                flow_send_copy(f, k).wait_send()
        for c in range(3):
            q_copy(0, c).wait_send()

            @pl.when(near == 1)
            def _():
                q_copy(1, c).wait_send()

            @pl.when((near == 0) & (far == 1))
            def _():
                q_copy(2, c).wait_send()

            @pl.when((near == 0) & (far == 0))
            def _():
                q_deliver(c, "wait")


def attend_back_sum(lengths, fresh, q, k, v, o, g, lse, x, w, half):
    blocks, seqs, span, _ = x.shape
    width = q.shape[1]
    heads = width // HD
    count = blocks * span
    owned = half.shape[0] // 32
    per_seq = count // BACK_KEY_BLOCK
    pair = 2 * owned
    edges = [pair * p // 3 for p in range(4)]
    flows = [
        (low, high - low, flow_stages(order))
        for low, high, order in zip(edges, edges[1:], FLOW_ORDERS)
    ]
    one = lambda shape: pl.BlockSpec((1,) + shape, lambda i, *_: (i // per_seq,) + (0,) * len(shape))
    mid = lambda shape: pl.BlockSpec((blocks, 1) + shape, lambda i, *_: (0, i // per_seq, 0, 0))
    single = lambda shape: pl.BlockSpec(
        (1,) + shape, lambda i, *_: (i // per_seq, 0, 0), pipeline_mode=pl.Buffered(1)
    )
    dma = pltpu.SemaphoreType.DMA
    return pl.pallas_call(
        functools.partial(attend_back_sum_kernel, heads, flows),
        grid_spec=pltpu.PrefetchScalarGridSpec(
            num_scalar_prefetch=2,
            grid=(seqs * per_seq,),
            in_specs=[
                one((width, count)),
                single((width, count)),
                single((width, count)),
                pl.BlockSpec(
                    (blocks, 1, width, span),
                    lambda i, *_: (0, i // per_seq, 0, 0),
                    pipeline_mode=pl.Buffered(1),
                ),
                mid((width, span)),
                one((8, count)),
                pl.BlockSpec(
                    (blocks, 1, span, D),
                    lambda i, *_: (0, i // per_seq, 0, 0),
                    pipeline_mode=pl.Buffered(1),
                ),
                pl.BlockSpec(
                    (3 * width, D), lambda i, *_: (0, 0), pipeline_mode=pl.Buffered(1)
                ),
                pl.BlockSpec(memory_space=pl.ANY),
            ],
            out_specs=[
                pl.BlockSpec(memory_space=pl.ANY),
                mid((width, span)),
                whole((owned, TILE, TILE)),
                whole((1, 3 * width)),
            ],
            scratch_shapes=[
                pltpu.VMEM((3 * width, D), f32),
                pltpu.VMEM((heads, count, HD + 16), bf16),
                pltpu.VMEM((heads, HD + 16, count), bf16),
                pltpu.VMEM((heads, count, HD + 16), bf16),
                pltpu.VMEM((heads, HD + 16, count), bf16),
                pltpu.VMEM((width, count), bf16),
                pltpu.VMEM((width, count), f32),
                pltpu.VMEM((8, count), f32),
                pltpu.VMEM((3 * width, BACK_KEY_BLOCK), bf16),
                pltpu.VMEM((width, BACK_KEY_BLOCK), f32),
                pltpu.VMEM((width, BACK_KEY_BLOCK), f32),
                pltpu.VMEM((heads, BACK_QUERY_BLOCK, BACK_KEY_BLOCK), bf16),
                pltpu.VMEM((heads, BACK_QUERY_BLOCK, BACK_KEY_BLOCK), bf16),
                pltpu.VMEM((seqs, blocks, span, D), bf16),
                pltpu.VMEM((seqs, 2, span, D), bf16),
                pltpu.VMEM((seqs, span, D), bf16),
                pltpu.VMEM((span, D), f32),
                pltpu.VMEM((8, -(-pair // 3), HALF, TILE), bf16),
                pltpu.VMEM((pair, HALF, TILE), f32),
                pltpu.VMEM((owned, HALF, TILE), f32),
                pltpu.VMEM((2, Q_UNITS, HALF, TILE), bf16),
                pltpu.VMEM((Q_UNITS, HALF, TILE), bf16),
                pltpu.VMEM((Q_UNITS, HALF, TILE), bf16),
                pltpu.VMEM((Q_UNITS, HALF, TILE), bf16),
                pltpu.VMEM((owned, TILE, TILE), bf16),
                dma((seqs, 2, 2)),
                dma((seqs, 2)),
                dma((seqs,)),
                dma((3,)),
                dma((3, 4)),
                dma((3, 4)),
                dma((2,)),
                dma((3, 3)),
                dma((3, 3)),
                dma((Q_UNITS,)),
                dma(()),
            ]
            + [
                pltpu.VMEM((8 >> k, size, HALF, TILE), bf16)
                for _, size, _ in flows
                for k in range(4)
            ],
        ),
        out_shape=[
            jax.ShapeDtypeStruct((seqs, span, D), f32),
            jax.ShapeDtypeStruct((blocks, seqs, width, span), bf16),
            jax.ShapeDtypeStruct((owned, TILE, TILE), f32),
            jax.ShapeDtypeStruct((1, 3 * width), f32),
        ],
        compiler_params=pltpu.CompilerParams(
            dimension_semantics=("arbitrary",),
            collective_id=5,
            has_side_effects=True,
            vmem_limit_bytes=VMEM_LIMIT,
        ),
        cost_estimate=pl.CostEstimate(
            flops=70_000_000_000, bytes_accessed=25_000_000, transcendentals=0
        ),
        name="attend_back_sum",
    )(lengths, fresh, q, k, v, o, g, lse, x, w, half.reshape(16, pair, HALF, TILE))


VEC_ROWS = 72


def finish_kernel(
    stages,
    raw_ref,
    gain_ref,
    rows_ref,
    hsum_ref,
    db_ref,
    master_ref,
    left_ref,
    right_ref,
    left_root_ref,
    right_root_ref,
    par_ref,
    stat_ref,
    clip_out,
    left_out,
    right_out,
    tiles_out,
    vec_out,
    stat_out,
    par_out,
    norm_out,
    total,
    landing,
    send_sem,
    recv_sem,
):
    owned = raw_ref.shape[0]
    used = par_ref.shape[0]
    partners = [partner_of(axis, bit)[0] for axis, bit in stages]
    greet(partners)
    squares = jnp.zeros((TILE, TILE), f32)
    for t in range(owned):
        squares = squares + raw_ref[t] * raw_ref[t]
    per = D // TILE
    width = db_ref.shape[1] // 3
    group = lax.axis_index("seq")
    total[...] = jnp.zeros_like(total)
    for piece, (ref, row) in enumerate(
        ((gain_ref, 0), (gain_ref, 1), (rows_ref, 0), (rows_ref, 1), (None, 0), (rows_ref, 2), (rows_ref, 3))
    ):
        if ref is not None:
            for c in range(per):
                total[piece * per + c : piece * per + c + 1, :] = ref[
                    row : row + 1, c * TILE : (c + 1) * TILE
                ]
    for part, start in ((0, 4 * per), (2, 7 * per)):
        for unit in range(width // HALF):
            value = db_ref[:, part * width + unit * HALF : part * width + (unit + 1) * HALF]
            both = jnp.concatenate([value, value], axis=1)
            lane = lax.broadcasted_iota(jnp.int32, (1, TILE), 1) // HALF
            place = group * (width // HALF) + unit
            room = (D if part == 0 else VW) // HALF
            row = start + jnp.minimum(place, room - 1) // 2
            keep = (lane == place % 2) & (place < room)
            total[pl.ds(row, 1), :] = total[pl.ds(row, 1), :] + jnp.where(keep, both, 0.0)
    for c in range(FF // TILE):
        at = 7 * per + VW // TILE + c
        total[at : at + 1, :] = hsum_ref[:, c * TILE : (c + 1) * TILE]
    total[used : used + 1, :] = jnp.sum(squares, axis=0, keepdims=True)
    for i, device in enumerate(partners):
        landing[i, 0] = total[...]
        copy = pltpu.make_async_remote_copy(
            src_ref=landing.at[i, 0],
            dst_ref=landing.at[i, 1],
            send_sem=send_sem.at[i],
            recv_sem=recv_sem.at[i],
            device_id=device,
            device_id_type=MESH,
        )
        copy.start()
        copy.wait()
        total[...] = total[...] + landing[i, 1]
    vector = total[0:used, :]
    square_sum = jnp.sum(total[used : used + 1, :], axis=1, keepdims=True) + jnp.sum(
        jnp.sum(vector * vector, axis=0, keepdims=True), axis=1, keepdims=True
    )
    grad_norm = jnp.sqrt(square_sum)
    factor = jnp.minimum(1.0, CLIP / (grad_norm + clip_eps))
    norm_out[...] = jnp.broadcast_to(grad_norm, norm_out.shape)
    grads = vector * factor
    vec_out[...] = grads
    stat = decay_rate * stat_ref[...] + (1.0 - decay_rate) * grads * grads
    stat_out[...] = stat
    par_out[...] = par_ref[...] - vector_rate * grads / (jnp.sqrt(stat) + moment_eps)
    first = (lax.axis_index("dp") * lax.axis_size("seq") + lax.axis_index("seq")) * owned

    def exact(a, b, dims):
        return lax.dot_general(a, b, dims, precision=highest, preferred_element_type=f32)

    for t in range(owned):
        index = first + t
        turned = (index < N_QKV) | (index >= FIRST_PROJ)
        raw = raw_ref[t]
        tile = jnp.where(turned, raw.T, raw) * factor
        clip_out[t] = tile
        left_out[t] = decay_rate * left_ref[t] + (1.0 - decay_rate) * exact(tile, tile, NT)
        flipped = tile.T
        right_out[t] = decay_rate * right_ref[t] + (1.0 - decay_rate) * exact(flipped, flipped, NT)
        inner = exact(tile, right_root_ref[t], NN)
        tiles_out[t] = master_ref[t] - matrix_rate * exact(left_root_ref[t], inner, NN)


def finish(raw, vectors, master, left, right, left_root, right_root, par, stat, dp, seq):
    stages = exchange_bits(dp, seq)
    tiles = jax.ShapeDtypeStruct(raw.shape, f32)
    vector = jax.ShapeDtypeStruct(par.shape, f32)
    vm = pl.BlockSpec(memory_space=pltpu.VMEM)
    return pl.pallas_call(
        functools.partial(finish_kernel, stages),
        in_specs=[vm] * 12,
        out_specs=[vm] * 8,
        out_shape=[tiles] * 4 + [vector] * 3 + [jax.ShapeDtypeStruct((8, TILE), f32)],
        scratch_shapes=[
            pltpu.VMEM((VEC_ROWS, TILE), f32),
            pltpu.VMEM((len(stages), 2, VEC_ROWS, TILE), f32),
            pltpu.SemaphoreType.DMA((len(stages),)),
            pltpu.SemaphoreType.DMA((len(stages),)),
        ],
        compiler_params=pltpu.CompilerParams(
            collective_id=2, has_side_effects=True, vmem_limit_bytes=VMEM_LIMIT
        ),
        name="finish",
    )(raw, *vectors, master, left, right, left_root, right_root, par, stat)


def per_device(
    tokens,
    first_values,
    cotangent,
    lengths,
    master_tiles,
    left_stat,
    right_stat,
    left_root,
    right_root,
    vector_params,
    vector_stat,
):
    seqs, span, _ = tokens.shape
    owned_count = master_tiles.shape[0]
    groups = lax.axis_size("seq")
    me_seq = lax.axis_index("seq")
    width = D // groups
    fresh_groups = VW // width
    total_tiles = owned_count * groups * lax.axis_size("dp")

    (
        gain_one,
        shift_one,
        gain_two,
        shift_two,
        query_bias,
        out_bias,
        proj_bias,
        value_bias,
        hidden_bias,
    ) = split_vector(vector_params)

    gathered = lax.all_gather(master_tiles.astype(bf16), ("dp", "seq"), axis=0, tiled=True)
    fits = front_fits(lax.axis_size("dp"), groups, owned_count)
    flat_tokens = tokens.reshape(-1, D).astype(f32)
    normed_one, unit_one, inv_one = norm_forward(flat_tokens, gain_one, shift_one)
    if fits:
        norm_rows = jnp.concatenate(
            [jnp.stack([gain_one, shift_one]), jnp.zeros((6, D), f32)]
        )
        x_all, w_mine = front(tokens, norm_rows, master_tiles)
    else:
        normed_one = normed_one.astype(bf16).reshape(seqs, span, D)
        x_all = lax.all_gather(normed_one, "seq", axis=0, tiled=False)
    first_turned = first_values.transpose(2, 0, 1).reshape(groups - fresh_groups, width, seqs, span)
    first_turned = first_turned.transpose(0, 2, 1, 3)
    first_send = jnp.concatenate(
        [jnp.zeros((fresh_groups,) + first_turned.shape[1:], bf16), first_turned], axis=0
    )
    first_mine = lax.all_to_all(first_send, "seq", 0, 0, tiled=True)

    is_fresh = (me_seq < fresh_groups).astype(jnp.int32).reshape(1)
    fresh_seq = jnp.minimum(me_seq, fresh_groups - 1)

    def turned(start, cols):
        amount = D // TILE * (cols // TILE)
        tiles = gathered[start : start + amount].reshape(D // TILE, cols // TILE, TILE, TILE)
        return tiles.transpose(1, 3, 0, 2).reshape(cols, D)

    if not fits:
        wq = lax.dynamic_slice_in_dim(turned(0, D), me_seq * width, width, 0)
        wk = lax.dynamic_slice_in_dim(turned(N_OUT, D), me_seq * width, width, 0)
        wv = lax.dynamic_slice_in_dim(turned(2 * N_OUT, VW), fresh_seq * width, width, 0)
        w_mine = jnp.concatenate([wq, wk, wv], axis=0)
    qb = lax.dynamic_slice_in_dim(query_bias, me_seq * width, width, 0).reshape(width, 1)
    vb = lax.dynamic_slice_in_dim(value_bias, fresh_seq * width, width, 0).reshape(width, 1)

    o_heads, q, k, v, lse = attend_forward(
        lengths, is_fresh, x_all, w_mine, qb, vb, first_mine
    )
    att = lax.all_to_all(o_heads, "seq", 0, 0, tiled=True)
    rows = jnp.concatenate(
        [jnp.stack([gain_two, shift_two, out_bias, proj_bias]), jnp.zeros((4, D), f32)]
    )
    position = (me_seq * span).astype(jnp.int32).reshape(1)
    (
        block_output,
        residual_grad,
        att_grad,
        act,
        hidden_grad,
        normed_two,
        branch_grad,
        out_grad,
        row_sums,
        hidden_bias_grad,
    ) = feed_forward(
        lengths, position, att, tokens, cotangent, gathered, rows, hidden_bias.reshape(1, FF)
    )
    g_heads = lax.all_to_all(att_grad, "seq", 0, 0, tiled=True)
    grad_args = (att, branch_grad, out_grad, normed_two, act, hidden_grad)
    back_args = (q, k, v, o_heads, g_heads, lse, x_all, w_mine)
    if fits:
        half_tiles = paired_grads(total_tiles, *grad_args)
        norm_one_in, dv, owned, db = attend_back_sum(lengths, is_fresh, *back_args, half_tiles)
        norm_one_in = norm_one_in.reshape(-1, D)
    else:
        all_tiles = weight_grads(total_tiles, *grad_args)
        group = me_seq.astype(jnp.int32).reshape(1)
        dx, dv, all_tiles, db = attend_backward(lengths, is_fresh, group, *back_args, all_tiles)
        norm_one_in = (
            lax.psum_scatter(dx, "seq", scatter_dimension=0, tiled=True)
            .reshape(-1, D)
            .astype(f32)
        )
        owned = tile_sum(all_tiles, lax.axis_size("dp"), groups)
    dv_back = lax.all_to_all(dv, "seq", 0, 0, tiled=True)
    first_grad = (
        dv_back[fresh_groups:]
        .transpose(1, 3, 0, 2)
        .reshape(first_values.shape)
        .astype(f32)
    )
    token_part = norm_backward(norm_one_in, unit_one, inv_one, gain_one)
    tokens_grad = residual_grad + token_part.reshape(tokens.shape)
    gain_one_grad = jnp.sum(norm_one_in * unit_one, axis=0)
    shift_one_grad = jnp.sum(norm_one_in, axis=0)

    used = vector_params.shape[0] // TILE
    gain_sums = jnp.stack([gain_one_grad, shift_one_grad])
    clipped, left_new, right_new, tiles_new, vector_grads, vector_stat_new, vector_new, norm = (
        finish(
            owned,
            (gain_sums, row_sums, hidden_bias_grad, db),
            master_tiles,
            left_stat,
            right_stat,
            left_root,
            right_root,
            vector_params.reshape(used, TILE),
            vector_stat.reshape(used, TILE),
            lax.axis_size("dp"),
            groups,
        )
    )
    return (
        block_output,
        tokens_grad,
        first_grad,
        clipped,
        left_new,
        right_new,
        tiles_new,
        vector_grads.reshape(-1),
        vector_stat_new.reshape(-1),
        vector_new.reshape(-1),
        norm[0, 0],
    )


def solution(mesh):
    tiles = P(("dp", "seq"), None, None)
    seqs = P("dp", "seq", None)
    in_specs = (seqs, seqs, seqs, P("dp"), tiles, tiles, tiles, tiles, tiles, P(), P())
    out_specs = (seqs, seqs, seqs, tiles, tiles, tiles, tiles, P(), P(), P(), P())
    return jax.shard_map(
        per_device, mesh=mesh, in_specs=in_specs, out_specs=out_specs, check_vma=False
    )
```

```python
import functools

import jax
import jax.numpy as jnp
from jax import lax
from jax.experimental import pallas as pl
from jax.experimental.pallas import tpu as pltpu
from jax.sharding import PartitionSpec as P

D = 768
HD = 64
FF = 3072
VW = 384
TILE = 128
CLIP = 256
LOG2E = 1.4426950408889634
SCALE = HD**-0.5
QUERY_BLOCK = 512
KEY_BLOCK = 512
BACK_QUERY_BLOCK = 512
BACK_KEY_BLOCK = 512
HALF_BLOCK = 256
STRIPE = 256
SUB_ROWS = 256
SUB_COLS = 256
N_QKV = 90
N_OUT = 36
N_HID = 144
N_PROJ = 144
N_REST = N_OUT + N_HID + N_PROJ
FIRST_PROJ = N_QKV + N_OUT + N_HID

highest = lax.Precision.HIGHEST
norm_eps = 1e-05
clip_eps = 1e-06
decay_rate = 0.5
matrix_rate = 0.3
vector_rate = 0.1
moment_eps = 1e-08
masked_score = -1e30

f32 = jnp.float32
bf16 = jnp.bfloat16
NN = (((1,), (0,)), ((), ()))
NT = (((1,), (1,)), ((), ()))
TN = (((0,), (0,)), ((), ()))
VMEM_LIMIT = 60 << 20
MESH = pl.DeviceIdType.MESH


def dot(left_in, right_in, dims=NN):
    return lax.dot_general(left_in, right_in, dims, preferred_element_type=f32)


def split_vector(vector):
    pieces = []
    offset = 0
    for length in (D, D, D, D, D, D, D, VW, FF):
        pieces.append(vector[offset : offset + length])
        offset = offset + length
    return pieces


def norm_forward(values, gain_row, shift_row):
    centered = values - jnp.mean(values, axis=-1, keepdims=True)
    variance = jnp.mean(centered * centered, axis=-1, keepdims=True)
    inv_std = lax.rsqrt(variance + norm_eps)
    unit_rows = centered * inv_std
    return (unit_rows * gain_row + shift_row, unit_rows, inv_std)


def norm_backward(grad_in, unit_rows, inv_std, gain_row):
    scaled = grad_in * gain_row
    term = (
        scaled
        - jnp.mean(scaled, axis=-1, keepdims=True)
        - unit_rows * jnp.mean(scaled * unit_rows, axis=-1, keepdims=True)
    )
    return term * inv_std


def whole(shape):
    return pl.BlockSpec(shape, lambda i, *_: (0,) * len(shape))


def params():
    return pltpu.CompilerParams(dimension_semantics=("arbitrary",), vmem_limit_bytes=VMEM_LIMIT)


W_SLOTS = 56
W_SHARE = W_SLOTS // 4
W_CHUNKS = ((0, 4), (4, 4), (8, 4), (12, 2))
X_CHUNKS = 4


def front_fits(dp, seq, owned):
    return dp == 8 and seq == 4 and 8 * owned >= N_QKV


def front_kernel(
    tok_ref,
    rows_ref,
    master_ref,
    fv_ref,
    x_ref,
    w_ref,
    fv_all,
    g_one,
    g_two,
    normed,
    plain,
    staged,
    slots,
    x_send,
    x_recv,
    own_sem,
    first_send,
    first_recv,
    w_send,
    w_recv,
    g_own,
    g_send,
    g_recv,
    z_send,
    z_recv,
    fv_send,
    fv_recv,
):
    dp, s = lax.axis_index("dp"), lax.axis_index("seq")
    depth = lax.axis_size("dp") // 2
    z, y, x, core = dp // 2, dp % 2, s // 2, s % 2
    owned = master_ref.shape[0]
    first = (dp * 4 + s) * owned
    seqs, span, _ = tok_ref.shape
    other_y, other_x, sibling = dp + 1 - 2 * y, s + 2 - 4 * x, s + 1 - 2 * core

    barrier = pltpu.get_barrier_semaphore()
    for dy in range(2):
        for ds in range(4):
            if dy or ds:
                mate = (2 * z + (y + dy) % 2, (s + ds) % 4)
                pl.semaphore_signal(barrier, inc=1, device_id=mate, device_id_type=MESH)

    @pl.when(z > 0)
    def _():
        pl.semaphore_signal(barrier, inc=1, device_id=(dp - 2, s), device_id_type=MESH)

    @pl.when(z < depth - 1)
    def _():
        pl.semaphore_signal(barrier, inc=1, device_id=(dp + 2, s), device_id_type=MESH)

    at_end = (z == 0) | (z == depth - 1)

    @pl.when(at_end)
    def _():
        pl.semaphore_wait(barrier, 8)

    @pl.when(jnp.logical_not(at_end))
    def _():
        pl.semaphore_wait(barrier, 9)

    def tile_sends(t, act):
        index = first + t
        is_value = index >= 2 * N_OUT
        within = index % N_OUT
        col = within % (D // TILE)
        slot = jnp.where(
            is_value,
            index,
            (index // N_OUT) * 18 + (within // (D // TILE)) * 3 + col % 3,
        )
        slot = jnp.where(is_value, index - N_OUT, slot)
        share = slot // W_SHARE
        chunk = (slot % W_SHARE) // 4
        for copy_index in range(2):
            to_x = jnp.where(is_value, copy_index, col // 3)
            target = (share // 2, to_x * 2 + share % 2)
            needed = (index < N_QKV) & (is_value | (copy_index == 0))
            here = (target[0] == dp) & (target[1] == s)

            @pl.when(needed & here)
            def _():
                if act == "start":
                    pltpu.make_async_copy(
                        staged.at[t], slots.at[slot], first_recv.at[chunk]
                    ).start()

            @pl.when(needed & jnp.logical_not(here))
            def _():
                copy = pltpu.make_async_remote_copy(
                    src_ref=staged.at[t],
                    dst_ref=slots.at[slot],
                    send_sem=first_send.at[t, copy_index],
                    recv_sem=first_recv.at[chunk],
                    device_id=target,
                    device_id_type=MESH,
                )
                if act == "start":
                    copy.start()
                else:
                    copy.wait_send()

    one = g_one.shape[2]
    parts = (
        (plain.at[pl.ds(0, one)], g_one.at[z, x], (dp, other_x)),
        (plain.at[pl.ds(one, owned - one)], g_two.at[dp], (other_y, s)),
    )

    def g_local(f):
        source, target, _ = parts[f]
        return pltpu.make_async_copy(source, target, g_own.at[f])

    def g_first(f):
        source, target, device = parts[f]
        return pltpu.make_async_remote_copy(
            src_ref=source,
            dst_ref=target,
            send_sem=g_send.at[f],
            recv_sem=g_recv.at[f],
            device_id=device,
            device_id_type=MESH,
        )

    def z_copy(up, h, f):
        plane = z - h if up else z + h
        block = g_one.at[plane] if f == 0 else g_two.at[pl.ds(2 * plane, 2)]
        return pltpu.make_async_remote_copy(
            src_ref=block,
            dst_ref=block,
            send_sem=z_send.at[up, h, f],
            recv_sem=z_recv.at[up, h, f],
            device_id=(dp + 2, s) if up else (dp - 2, s),
            device_id_type=MESH,
        )

    def z_landed(up, h, f):
        plane = z - 1 - h if up else z + 1 + h
        block = g_one.at[plane] if f == 0 else g_two.at[pl.ds(2 * plane, 2)]
        return pltpu.make_async_copy(block, block, z_recv.at[up, h, f])

    def z_hop(h):
        for up in (1, 0):
            if h:
                came = (z - h >= 0) if up else (z + h <= depth - 1)

                @pl.when(came)
                def _():
                    for f in range(2):
                        z_landed(up, h - 1, f).wait()

            if h < z_send.shape[1]:
                goes = ((z < depth - 1) & (z - h >= 0)) if up else ((z > 0) & (z + h <= depth - 1))

                @pl.when(goes)
                def _():
                    for f in range(2):
                        z_copy(up, h, f).start()

    for t in range(owned):
        plain[t] = master_ref[t].astype(bf16)
    for f in range(2):
        g_first(f).start()
        g_local(f).start()

    @pl.when(first < N_QKV)
    def _():
        for t in range(owned):
            staged[t] = plain[t].T
        for t in range(owned):
            tile_sends(t, "start")

    rows_each = seqs * span // X_CHUNKS
    per_seq = span // rows_each

    def x_copy(kind, j):
        n, part = j // per_seq, j % per_seq
        at = pl.ds(part * rows_each, rows_each)
        block = other_x if kind == 2 else s
        return pltpu.make_async_remote_copy(
            src_ref=x_ref.at[block, n, at] if kind == 2 else normed.at[n, at],
            dst_ref=x_ref.at[block, n, at],
            send_sem=x_send.at[kind, j],
            recv_sem=x_recv.at[kind, j],
            device_id=(dp, other_x) if kind == 0 else (dp, sibling),
            device_id_type=MESH,
        )

    def own_copy(j):
        n, part = j // per_seq, j % per_seq
        at = pl.ds(part * rows_each, rows_each)
        return pltpu.make_async_copy(normed.at[n, at], x_ref.at[s, n, at], own_sem.at[j])

    for j in range(X_CHUNKS):
        n, part = j // per_seq, j % per_seq
        at = pl.ds(part * rows_each, rows_each)
        value = tok_ref[n, at, :].astype(f32)
        normed[n, at, :] = norm_forward(value, rows_ref[0:1, :], rows_ref[1:2, :])[0].astype(bf16)
        x_copy(0, j).start()
        x_copy(1, j).start()
        own_copy(j).start()

    def fv_copies(act):
        for c in range(2):
            to = 2 + c

            @pl.when(s == to)
            def _():
                copy = pltpu.make_async_copy(fv_ref.at[c], fv_all.at[s], fv_recv.at[to])
                if act == "start":
                    copy.start()

            @pl.when(s != to)
            def _():
                copy = pltpu.make_async_remote_copy(
                    src_ref=fv_ref.at[c],
                    dst_ref=fv_all.at[s],
                    send_sem=fv_send.at[c],
                    recv_sem=fv_recv.at[s],
                    device_id=(dp, to),
                    device_id_type=MESH,
                )
                copy.start() if act == "start" else copy.wait_send()

    fv_copies("start")

    share = y * 2 + core

    def w_copy(kind, j):
        low, size = W_CHUNKS[j]
        base = ((1 - y) * 2 + core) * W_SHARE if kind == 3 else share * W_SHARE
        at = pl.ds(base + low, size)
        device = ((dp + 2, s), (other_y, s), (dp, sibling), (dp, sibling))[kind]
        return pltpu.make_async_remote_copy(
            src_ref=slots.at[at],
            dst_ref=slots.at[at],
            send_sem=w_send.at[kind, j],
            recv_sem=w_recv.at[kind, j],
            device_id=device,
            device_id_type=MESH,
        )

    def landed(j, size):
        low, _ = W_CHUNKS[j]
        at = pl.ds(share * W_SHARE + low, size)
        pltpu.make_async_copy(slots.at[at], slots.at[at], first_recv.at[j]).wait()

    used = 3 * 18 - 3 * W_SHARE
    @pl.when((z == 0) & (share == 3))
    def _():
        slots[3 * W_SHARE + used : W_SLOTS] = jnp.zeros(
            (W_SHARE - used,) + slots.shape[1:], bf16
        )

    for f in range(2):
        g_first(f).wait_recv()
        g_local(f).wait()
    z_hop(0)
    for j in range(len(W_CHUNKS)):
        if j < len(W_CHUNKS):
            low, size = W_CHUNKS[j]
            short = min(size, used - low)

            @pl.when((z == 0) & (share < 3))
            def _():
                landed(j, size)

            if short > 0:

                @pl.when((z == 0) & (share == 3))
                def _():
                    landed(j, short)

            @pl.when(z > 0)
            def _():
                w_copy(0, j).wait_recv()

            @pl.when(z < depth - 1)
            def _():
                w_copy(0, j).start()

            w_copy(1, j).start()
            w_copy(2, j).start()
        if j < len(W_CHUNKS):
            w_copy(1, j).wait_recv()
            w_copy(3, j).start()
    z_hop(1)
    for j in range(X_CHUNKS):
        if j == X_CHUNKS - 1:
            z_hop(2)
        x_copy(0, j).wait_recv()
        x_copy(2, j).start()
    for j in range(len(W_CHUNKS)):
        w_copy(2, j).wait_recv()
        w_copy(3, j).wait_recv()
    width = HD * 3
    for which in range(3):
        for piece in range(3):
            unit = core * 3 + piece
            rows = pl.ds(pl.multiple_of((unit % 2) * HD, HD), HD)
            at = which * width + piece * HD
            for r in range(D // TILE):
                w_ref[at : at + HD, r * TILE : (r + 1) * TILE] = slots[
                    which * 18 + r * 3 + unit // 2, rows, :
                ]
    for j in range(X_CHUNKS):
        x_copy(1, j).wait_recv()
        x_copy(2, j).wait_recv()
        own_copy(j).wait()
        for kind in range(3):
            x_copy(kind, j).wait_send()
    @pl.when(x == 1)
    def _():
        for block in range(4):
            pltpu.make_async_copy(fv_all.at[block], fv_all.at[block], fv_recv.at[block]).wait()

    fv_copies("wait")
    z_hop(3)
    for f in range(2):
        g_first(f).wait_send()
        for h in range(z_send.shape[1]):

            @pl.when((z < depth - 1) & (z - h >= 0))
            def _():
                z_copy(1, h, f).wait_send()

            @pl.when((z > 0) & (z + h <= depth - 1))
            def _():
                z_copy(0, h, f).wait_send()

    for j in range(len(W_CHUNKS)):

        @pl.when(z < depth - 1)
        def _():
            w_copy(0, j).wait_send()

        for kind in range(1, 4):
            w_copy(kind, j).wait_send()

    @pl.when(first < N_QKV)
    def _():
        for t in range(owned):
            tile_sends(t, "wait")


def front(tokens, rows, master, first_turned):
    seqs, span, _ = tokens.shape
    owned = master.shape[0]
    one = (owned + 1) // 2
    vm, hbm = pl.BlockSpec(memory_space=pltpu.VMEM), pl.BlockSpec(memory_space=pl.ANY)
    dma = pltpu.SemaphoreType.DMA
    chunks = len(W_CHUNKS)
    return pl.pallas_call(
        front_kernel,
        in_specs=[vm] * 3 + [hbm],
        out_specs=[hbm, vm, hbm, hbm, hbm],
        out_shape=[
            jax.ShapeDtypeStruct((4, seqs, span, D), bf16),
            jax.ShapeDtypeStruct((9 * HD, D), bf16),
            jax.ShapeDtypeStruct((4,) + first_turned.shape[1:], bf16),
            jax.ShapeDtypeStruct((4, 2, one, TILE, TILE), bf16),
            jax.ShapeDtypeStruct((8, owned - one, TILE, TILE), bf16),
        ],
        scratch_shapes=[
            pltpu.VMEM((seqs, span, D), bf16),
            pltpu.VMEM((owned, TILE, TILE), bf16),
            pltpu.VMEM((owned, TILE, TILE), bf16),
            pltpu.VMEM((W_SLOTS, TILE, TILE), bf16),
            dma((3, X_CHUNKS)),
            dma((3, X_CHUNKS)),
            dma((X_CHUNKS,)),
            dma((owned, 2)),
            dma((chunks,)),
            dma((4, chunks)),
            dma((4, chunks)),
            dma((2,)),
            dma((2,)),
            dma((2,)),
            dma((2, 3, 2)),
            dma((2, 3, 2)),
            dma((2,)),
            dma((4,)),
        ],
        compiler_params=pltpu.CompilerParams(
            collective_id=3, has_side_effects=True, vmem_limit_bytes=VMEM_LIMIT
        ),
        cost_estimate=pl.CostEstimate(
            flops=40_000_000_000, bytes_accessed=20_000_000, transcendentals=0
        ),
        name="front",
    )(tokens, rows, master, first_turned)


def attend_forward_kernel(
    heads,
    len_ref,
    fresh_ref,
    x_ref,
    w_ref,
    qb_ref,
    vb_ref,
    fv_ref,
    o_ref,
    q_ref,
    k_ref,
    v_ref,
    lse_ref,
    k_heads,
    q_wide,
    values,
    acc,
    top,
    fades,
    probs,
):
    blocks, _, span, width_in = x_ref.shape
    count = blocks * span
    length = len_ref[pl.program_id(0)]
    x = x_ref[...].reshape(count, width_in)
    width = heads * HD
    q_ref[0] = (dot(w_ref[0:width, :], x, NT) + qb_ref[...]).astype(bf16)
    keys = dot(x, w_ref[width : 2 * width, :], NT).astype(bf16)
    k_ref[0] = keys.T
    dead = lax.broadcasted_iota(jnp.int32, (count, 1), 0) >= length
    bias = jnp.broadcast_to(jnp.where(dead, masked_score, 0.0).astype(bf16), (count, 16))
    ones = (lax.broadcasted_iota(jnp.int32, (16, count), 0) == 0).astype(f32).astype(bf16)
    for h in range(heads):
        k_heads[h, :, 0:HD] = keys[:, h * HD : (h + 1) * HD]
        k_heads[h, :, HD : HD + 16] = bias
        q_wide[h, 0:HD] = q_ref[0, h * HD : (h + 1) * HD, :]
        q_wide[h, HD : HD + 16] = ones

    @pl.when(fresh_ref[0] == 1)
    def _():
        v_ref[0] = (dot(w_ref[2 * width :, :], x, NT) + vb_ref[...]).astype(bf16)

    @pl.when(fresh_ref[0] == 0)
    def _():
        for b in range(blocks):
            v_ref[0, :, b * span : (b + 1) * span] = fv_ref[b, 0]

    for h in range(heads):
        values[h, 0:HD] = v_ref[0, h * HD : (h + 1) * HD, :]
        values[h, HD : HD + 16] = ones
    bq, bk = QUERY_BLOCK, KEY_BLOCK

    def one_query_block(qi, carry):
        q0 = pl.multiple_of(qi * bq, bq)
        top[...] = jnp.full_like(top, masked_score)
        acc[...] = jnp.zeros_like(acc)

        def step(ki, masked, low=0, rows_here=bk):
            k0 = pl.multiple_of(ki * bk + low, HALF_BLOCK)
            skip = low if masked else 0
            for h in range(heads):
                for c0 in range(skip, bq, STRIPE):
                    cols = slice(c0, c0 + STRIPE)
                    at = pl.ds(pl.multiple_of(q0 + c0, TILE), STRIPE)
                    parts = []
                    for r0 in range(0, rows_here, HALF_BLOCK):
                        keys = pl.ds(pl.multiple_of(k0 + r0, HALF_BLOCK), HALF_BLOCK)
                        s = dot(k_heads[h, keys, :], q_wide[h, :, at])
                        if masked and c0 - low - r0 < HALF_BLOCK:
                            shape = (HALF_BLOCK, STRIPE)
                            allowed = low + r0 + lax.broadcasted_iota(
                                jnp.int32, shape, 0
                            ) <= c0 + lax.broadcasted_iota(jnp.int32, shape, 1)
                            s = jnp.where(allowed, s, masked_score)
                        parts.append(s)
                    top_old = top[h : h + 1, cols]
                    top_new = top_old
                    for s in parts:
                        top_new = jnp.maximum(top_new, jnp.max(s, axis=0, keepdims=True))
                    top[h : h + 1, cols] = top_new
                    fades[h : h + 1, cols] = jnp.exp2((top_old - top_new) * (SCALE * LOG2E))
                    for part, s in enumerate(parts):
                        probs[h, part * HALF_BLOCK : (part + 1) * HALF_BLOCK, cols] = jnp.exp2(
                            (s - top_new) * (SCALE * LOG2E)
                        ).astype(bf16)
            wide = slice(skip, bq)
            for h in range(heads):
                acc[h, :, wide] = acc[h, :, wide] * fades[h : h + 1, wide] + dot(
                    values[h, :, pl.ds(k0, rows_here)], probs[h, 0:rows_here, wide]
                )

        lax.fori_loop(
            0, jnp.minimum(qi, (length + bk - 1) // bk), lambda i, c: (step(i, False), c)[1], 0
        )

        @pl.when(q0 < length)
        def _():
            step(qi, True, 0, HALF_BLOCK)
            step(qi, True, HALF_BLOCK, HALF_BLOCK)

        for h in range(heads):
            rows = slice(h * HD, (h + 1) * HD)
            sums = acc[h, HD : HD + 1, :]
            o_ref[qi, 0, rows, :] = (acc[h, 0:HD, :] / sums).astype(bf16)
            lse_ref[0, h : h + 1, pl.ds(q0, bq)] = (
                top[h : h + 1, :] * (SCALE * LOG2E) + jnp.log2(sums)
            )
        return carry

    lax.fori_loop(0, count // bq, one_query_block, 0)


def attend_forward(lengths, fresh, x, w, qb, vb, fv):
    blocks, seqs, span, _ = x.shape
    width = w.shape[0] // 3
    heads = width // HD
    count = blocks * span
    one = lambda shape: pl.BlockSpec((1,) + shape, lambda i, *_: (i,) + (0,) * len(shape))
    mid = lambda shape: pl.BlockSpec((blocks, 1) + shape, lambda i, *_: (0, i, 0, 0))
    return pl.pallas_call(
        functools.partial(attend_forward_kernel, heads),
        grid_spec=pltpu.PrefetchScalarGridSpec(
            num_scalar_prefetch=2,
            grid=(seqs,),
            in_specs=[mid((span, D))]
            + [whole((3 * width, D))]
            + [whole((width, 1))] * 2
            + [mid((width, span))],
            out_specs=[
                mid((width, span)),
                one((width, count)),
                one((width, count)),
                one((width, count)),
                one((8, count)),
            ],
            scratch_shapes=[
                pltpu.VMEM((heads, count, HD + 16), bf16),
                pltpu.VMEM((heads, HD + 16, count), bf16),
                pltpu.VMEM((heads, HD + 16, count), bf16),
                pltpu.VMEM((heads, HD + 16, QUERY_BLOCK), f32),
                pltpu.VMEM((8, QUERY_BLOCK), f32),
                pltpu.VMEM((8, QUERY_BLOCK), f32),
                pltpu.VMEM((heads, KEY_BLOCK, QUERY_BLOCK), bf16),
            ],
        ),
        out_shape=[
            jax.ShapeDtypeStruct((blocks, seqs, width, span), bf16),
            jax.ShapeDtypeStruct((seqs, width, count), bf16),
            jax.ShapeDtypeStruct((seqs, width, count), bf16),
            jax.ShapeDtypeStruct((seqs, width, count), bf16),
            jax.ShapeDtypeStruct((seqs, 8, count), f32),
        ],
        compiler_params=params(),
        cost_estimate=pl.CostEstimate(
            flops=40_000_000_000, bytes_accessed=20_000_000, transcendentals=0
        ),
        name="attend_forward",
    )(lengths, fresh, x, w, qb, vb, fv)


def attend_backward_kernel(
    heads,
    len_ref,
    fresh_ref,
    group_ref,
    q_ref,
    k_ref,
    v_ref,
    o_ref,
    g_ref,
    lse_ref,
    x_ref,
    w_ref,
    all_in_ref,
    dx_ref,
    dv_ref,
    all_ref,
    db_ref,
    dw_ref,
    tiles,
    sem,
    k_heads,
    v_heads,
    q_heads,
    g_heads,
    k_turned,
    g_turned,
    dq_acc,
    delta,
    grads,
    dk_acc,
    dv_acc,
):
    n = pl.program_id(0)
    blocks, _, span, width_in = x_ref.shape
    count = blocks * span
    width = heads * HD
    length = len_ref[n]
    bq, bk = BACK_QUERY_BLOCK, BACK_KEY_BLOCK
    delta[...] = jnp.zeros_like(delta)
    for h in range(heads):
        rows = slice(h * HD, (h + 1) * HD)
        k_heads[h] = k_ref[0, rows, :].T
        v_heads[h] = v_ref[0, rows, :].T
        q_heads[h] = q_ref[0, rows, :].T
    for b in range(blocks):
        at = slice(b * span, (b + 1) * span)
        g_block = g_ref[b, 0]
        g_turned[:, at] = g_block
        product = o_ref[b, 0].astype(f32) * g_block.astype(f32)
        for h in range(heads):
            rows = slice(h * HD, (h + 1) * HD)
            g_heads[h, at, :] = g_block[rows, :].T
            delta[h : h + 1, at] = jnp.sum(product[rows, :], axis=0, keepdims=True)
    k_turned[...] = k_ref[0]
    dq_acc[...] = jnp.zeros_like(dq_acc)
    grads[...] = jnp.zeros_like(grads)
    key_blocks = (length + bk - 1) // bk
    query_blocks = (length + bq - 1) // bq

    def one_key_block(ki, carry):
        k0 = pl.multiple_of(ki * bk, bk)
        dk_acc[...] = jnp.zeros_like(dk_acc)
        dv_acc[...] = jnp.zeros_like(dv_acc)

        def step(qi, masked):
            q0 = pl.multiple_of(qi * bq, bq)
            at = pl.ds(q0, bq)
            if masked:
                key_pos = k0 + lax.broadcasted_iota(jnp.int32, (bk, bq), 0)
                query_pos = q0 + lax.broadcasted_iota(jnp.int32, (bk, bq), 1)
                allowed = (key_pos <= query_pos) & (key_pos < length)
            for h in range(heads):
                rows = slice(h * HD, (h + 1) * HD)
                s = dot(k_heads[h, pl.ds(k0, bk), :], q_ref[0, rows, at])
                dp = dot(v_heads[h, pl.ds(k0, bk), :], g_turned[rows, at])
                p = jnp.exp2(s * (SCALE * LOG2E) - lse_ref[0, h : h + 1, at])
                if masked:
                    p = jnp.where(allowed, p, 0.0)
                ds = (p * (dp - delta[h : h + 1, at])).astype(bf16)
                dv_acc[h] = dv_acc[h] + dot(p.astype(bf16), g_heads[h, at, :])
                dk_acc[h] = dk_acc[h] + dot(ds, q_heads[h, at, :])
                dq_acc[rows, at] = dq_acc[rows, at] + dot(k_turned[rows, pl.ds(k0, bk)], ds)

        first = k0 // bq
        plain = jnp.where(k0 + bk <= length, (k0 + bk + bq - 1) // bq, query_blocks)
        plain = jnp.minimum(plain, query_blocks)
        lax.fori_loop(first, plain, lambda i, c: (step(i, True), c)[1], 0)
        lax.fori_loop(plain, query_blocks, lambda i, c: (step(i, False), c)[1], 0)
        for h in range(heads):
            grads[pl.ds(k0, bk), width + h * HD : width + (h + 1) * HD] = (
                dk_acc[h] * SCALE
            ).astype(bf16)
            grads[pl.ds(k0, bk), 2 * width + h * HD : 2 * width + (h + 1) * HD] = dv_acc[h].astype(
                bf16
            )
        return carry

    lax.fori_loop(0, key_blocks, one_key_block, 0)
    grads[:, 0:width] = (dq_acc[...] * SCALE).astype(bf16).T
    for b in range(blocks):
        dv_ref[b, 0] = grads[b * span : (b + 1) * span, 2 * width : 3 * width].T

    @pl.when(fresh_ref[0] == 0)
    def _():
        grads[:, 2 * width : 3 * width] = jnp.zeros((count, width), bf16)

    dx_ref[...] = dot(grads[...], w_ref[...]).astype(bf16).reshape(dx_ref.shape)
    dw = dot(grads[...], x_ref[...].reshape(count, width_in), TN)
    db = jnp.sum(grads[...].astype(f32), axis=0, keepdims=True)

    @pl.when(n == 0)
    def _():
        dw_ref[...] = dw
        db_ref[...] = db

    @pl.when(n > 0)
    def _():
        dw_ref[...] += dw
        db_ref[...] += db

    @pl.when(n == pl.num_programs(0) - 1)
    def _():
        tiles[...] = jnp.zeros_like(tiles)
        for which, (start, per_row) in enumerate(
            ((0, D // TILE), (N_OUT, D // TILE), (2 * N_OUT, VW // TILE))
        ):

            def put(group):
                for piece in range(heads):
                    unit = group * heads + piece
                    rows = pl.ds(pl.multiple_of((unit % 2) * HD, HD), HD)
                    at = which * width + piece * HD
                    for r in range(D // TILE):
                        tiles[start + r * per_row + unit // 2, rows, :] = dw_ref[
                            at : at + HD, r * TILE : (r + 1) * TILE
                        ].astype(bf16)

            if which < 2:
                put(group_ref[0])
            else:
                pl.when(fresh_ref[0] == 1)(lambda: put(group_ref[0]))
        copy = pltpu.make_async_copy(tiles, all_ref.at[pl.ds(0, N_QKV)], sem.at[0])
        copy.start()
        copy.wait()


def attend_backward(lengths, fresh, group, q, k, v, o, g, lse, x, w, all_tiles):
    blocks, seqs, span, _ = x.shape
    width = q.shape[1]
    heads = width // HD
    count = blocks * span
    one = lambda shape: pl.BlockSpec((1,) + shape, lambda i, *_: (i,) + (0,) * len(shape))
    mid = lambda shape: pl.BlockSpec((blocks, 1) + shape, lambda i, *_: (0, i, 0, 0))
    return pl.pallas_call(
        functools.partial(attend_backward_kernel, heads),
        grid_spec=pltpu.PrefetchScalarGridSpec(
            num_scalar_prefetch=3,
            grid=(seqs,),
            in_specs=[
                one((width, count)),
                one((width, count)),
                one((width, count)),
                mid((width, span)),
                mid((width, span)),
                one((8, count)),
                mid((span, D)),
                whole((3 * width, D)),
                pl.BlockSpec(memory_space=pl.ANY),
            ],
            out_specs=[
                mid((span, D)),
                mid((width, span)),
                pl.BlockSpec(memory_space=pl.ANY),
                whole((1, 3 * width)),
            ],
            scratch_shapes=[
                pltpu.VMEM((3 * width, D), f32),
                pltpu.VMEM((N_QKV, TILE, TILE), bf16),
                pltpu.SemaphoreType.DMA((1,)),
            ]
            + [pltpu.VMEM((heads, count, HD), bf16)] * 4
            + [
                pltpu.VMEM((width, count), bf16),
                pltpu.VMEM((width, count), bf16),
                pltpu.VMEM((width, count), f32),
                pltpu.VMEM((8, count), f32),
                pltpu.VMEM((count, 3 * width), bf16),
                pltpu.VMEM((heads, BACK_KEY_BLOCK, HD), f32),
                pltpu.VMEM((heads, BACK_KEY_BLOCK, HD), f32),
            ],
        ),
        out_shape=[
            jax.ShapeDtypeStruct((blocks, seqs, span, D), bf16),
            jax.ShapeDtypeStruct((blocks, seqs, width, span), bf16),
            jax.ShapeDtypeStruct(all_tiles.shape, bf16),
            jax.ShapeDtypeStruct((1, 3 * width), f32),
        ],
        input_output_aliases={11: 2},
        compiler_params=params(),
        cost_estimate=pl.CostEstimate(
            flops=70_000_000_000, bytes_accessed=25_000_000, transcendentals=0
        ),
        name="attend_backward",
    )(lengths, fresh, group, q, k, v, o, g, lse, x, w, all_tiles)


HIDDEN_CHUNK = 512
GELU_A = 0.7978845608028654
GELU_B = 0.044715


def feed_forward_kernel(
    part_count,
    len_ref,
    pos_ref,
    att_ref,
    tok_ref,
    cot_ref,
    rows_ref,
    hb_ref,
    *rest,
):
    sources, rest = rest[:part_count], rest[part_count:]
    feed_forward_body(
        len_ref, pos_ref, att_ref, tok_ref, cot_ref, rows_ref, hb_ref, sources, *rest
    )


def feed_forward_body(
    len_ref,
    pos_ref,
    att_ref,
    tok_ref,
    cot_ref,
    rows_ref,
    hb_ref,
    sources,
    out_ref,
    rg_ref,
    ag_ref,
    act_ref,
    hg_ref,
    nt_ref,
    bg_ref,
    og_ref,
    sums_ref,
    hsum_ref,
    tiles,
    w_out,
    w_hidden,
    w_proj,
    output_acc,
    sem,
):
    n = pl.program_id(0)
    span = tok_ref.shape[1]

    @pl.when(n == 0)
    def _():
        if len(sources) == 1:
            skipped = N_QKV
            copies = [
                pltpu.make_async_copy(
                    sources[0].at[pl.ds(N_QKV, N_REST)], tiles, sem.at[0]
                )
            ]
        else:
            skipped = 0
            dp, s = lax.axis_index("dp"), lax.axis_index("seq")
            y, x, core = dp % 2, s // 2, s % 2
            one = sources[0].shape[2]
            owned = tiles.shape[0] // 32
            spread = tiles.reshape(4, 2, 2, 2, owned, TILE, TILE)
            copies = []
            for c in range(2):
                at_core = core if c == 0 else 1 - core
                for other in range(2):
                    at_y = y if other == 0 else 1 - y
                    at_x = x if other == 0 else 1 - x
                    copies.append(
                        pltpu.make_async_copy(
                            sources[c * 4 + other],
                            spread.at[:, at_y, :, at_core, pl.ds(0, one)],
                            sem.at[c * 4 + other],
                        )
                    )
                    source = sources[c * 4 + 2 + other]
                    copies.append(
                        pltpu.make_async_copy(
                            source.reshape(4, 2, owned - one, TILE, TILE),
                            spread.at[:, :, at_x, at_core, pl.ds(one, owned - one)],
                            sem.at[c * 4 + 2 + other],
                        )
                    )
        for copy in copies:
            copy.start()
        for copy in copies:
            copy.wait()
        for start, matrix in zip((0, N_OUT, N_OUT + N_HID), (w_out, w_hidden, w_proj)):
            start = start + N_QKV - skipped
            row_tiles, col_tiles = matrix.shape[0] // TILE, matrix.shape[1] // TILE

            def place(r, carry):
                at = pl.ds(pl.multiple_of(r * TILE, TILE), TILE)
                for c in range(col_tiles):
                    matrix[at, c * TILE : (c + 1) * TILE] = tiles[start + r * col_tiles + c]
                return carry

            lax.fori_loop(0, row_tiles, place, 0)
        sums_ref[...] = jnp.zeros_like(sums_ref)
        hsum_ref[...] = jnp.zeros_like(hsum_ref)

    gain_two, shift_two = rows_ref[0:1, :], rows_ref[1:2, :]
    out_bias, proj_bias = rows_ref[2:3, :], rows_ref[3:4, :]
    attended = att_ref[...].reshape(D, span)
    residual = tok_ref[0].astype(f32) + dot(attended, w_out[...], TN) + out_bias
    normed, unit, inv = norm_forward(residual, gain_two, shift_two)
    normed = normed.astype(bf16)
    nt_ref[...] = normed
    live = pos_ref[0] + lax.broadcasted_iota(jnp.int32, (span, 1), 0) < len_ref[n]
    out_grad = jnp.where(live, cot_ref[0].astype(f32), 0.0)
    out_grad_low = out_grad.astype(bf16)
    og_ref[...] = out_grad_low
    output_acc[...] = residual + proj_bias
    rg_ref[0] = jnp.zeros((span, D), f32)

    def chunk(c, carry):
        cols = pl.ds(pl.multiple_of(c * HIDDEN_CHUNK, HIDDEN_CHUNK), HIDDEN_CHUNK)
        hidden = dot(nt_ref[...], w_hidden[:, cols]) + hb_ref[:, cols]
        square = hidden * hidden
        bend = jnp.tanh(GELU_A * (hidden + GELU_B * (hidden * square)))
        active = (0.5 * hidden * (1.0 + bend)).astype(bf16)
        slope = 0.5 * (1.0 + bend) + 0.5 * hidden * (1.0 - bend * bend) * (
            GELU_A * (1.0 + (3.0 * GELU_B) * square)
        )
        act_ref[:, cols] = active
        hidden_grad = (dot(og_ref[...], w_proj[cols, :], NT) * slope).astype(bf16)
        hg_ref[:, cols] = hidden_grad
        hsum_ref[:, cols] += jnp.sum(hidden_grad.astype(f32), axis=0, keepdims=True)
        output_acc[...] += dot(active, w_proj[cols, :])
        rg_ref[0] += dot(hidden_grad, w_hidden[:, cols], NT)
        return carry

    lax.fori_loop(0, FF // HIDDEN_CHUNK, chunk, 0)
    out_ref[0] = output_acc[...].astype(bf16)
    norm_in = rg_ref[0]
    residual_grad = out_grad + norm_backward(norm_in, unit, inv, gain_two)
    rg_ref[0] = residual_grad
    branch = residual_grad.astype(bf16)
    bg_ref[...] = branch
    ag_ref[...] = dot(w_out[...], branch, NT).astype(bf16).reshape(ag_ref.shape)
    sums_ref[0:1, :] += jnp.sum(norm_in * unit, axis=0, keepdims=True)
    sums_ref[1:2, :] += jnp.sum(norm_in, axis=0, keepdims=True)
    sums_ref[2:3, :] += jnp.sum(branch.astype(f32), axis=0, keepdims=True)
    sums_ref[3:4, :] += jnp.sum(out_grad, axis=0, keepdims=True)


def feed_forward(lengths, position, att, tokens, cotangent, sources, total_tiles, rows, hidden_bias):
    groups, seqs, width, span = att.shape
    one = lambda shape: pl.BlockSpec((1,) + shape, lambda i, *_: (i,) + (0,) * len(shape))
    mid = lambda shape: pl.BlockSpec((groups, 1) + shape, lambda i, *_: (0, i, 0, 0))
    row = lambda cols: pl.BlockSpec((span, cols), lambda i, *_: (i, 0))
    single = pl.BlockSpec(
        (1, span, D), lambda i, *_: (i, 0, 0), pipeline_mode=pl.Buffered(1)
    )
    total = seqs * span
    return pl.pallas_call(
        functools.partial(feed_forward_kernel, len(sources)),
        grid_spec=pltpu.PrefetchScalarGridSpec(
            num_scalar_prefetch=2,
            grid=(seqs,),
            in_specs=[
                pl.BlockSpec(
                    (groups, 1, width, span),
                    lambda i, *_: (0, i, 0, 0),
                    pipeline_mode=pl.Buffered(1),
                ),
                single,
                single,
                whole((8, D)),
                whole((1, FF)),
            ]
            + [pl.BlockSpec(memory_space=pl.ANY)] * len(sources),
            out_specs=[
                one((span, D)),
                one((span, D)),
                mid((width, span)),
                row(FF),
                row(FF),
                row(D),
                row(D),
                row(D),
                whole((8, D)),
                whole((1, FF)),
            ],
            scratch_shapes=[
                pltpu.VMEM((N_REST if len(sources) == 1 else total_tiles, TILE, TILE), bf16),
                pltpu.VMEM((D, D), bf16),
                pltpu.VMEM((D, FF), bf16),
                pltpu.VMEM((FF, D), bf16),
                pltpu.VMEM((span, D), f32),
                pltpu.SemaphoreType.DMA((8,)),
            ],
        ),
        out_shape=[
            jax.ShapeDtypeStruct((seqs, span, D), bf16),
            jax.ShapeDtypeStruct((seqs, span, D), f32),
            jax.ShapeDtypeStruct((groups, seqs, width, span), bf16),
            jax.ShapeDtypeStruct((total, FF), bf16),
            jax.ShapeDtypeStruct((total, FF), bf16),
            jax.ShapeDtypeStruct((total, D), bf16),
            jax.ShapeDtypeStruct((total, D), bf16),
            jax.ShapeDtypeStruct((total, D), bf16),
            jax.ShapeDtypeStruct((8, D), f32),
            jax.ShapeDtypeStruct((1, FF), f32),
        ],
        compiler_params=params(),
        cost_estimate=pl.CostEstimate(
            flops=24_000_000_000, bytes_accessed=40_000_000, transcendentals=0
        ),
        name="feed_forward",
    )(lengths, position, att, tokens, cotangent, rows, hidden_bias, *sources)


GRAD_CHUNK = 256


def weight_grad_kernel(
    att_ref,
    bg_ref,
    og_ref,
    nt_ref,
    act_ref,
    hg_ref,
    all_ref,
    out_tiles,
    hid_tiles,
    proj_tiles,
    og_turned,
    nt_turned,
    sem,
    out_sem,
):
    i = pl.program_id(0)
    last = pl.num_programs(0) - 1
    groups, seqs, width, span = att_ref.shape
    d_tiles, f_tiles, per = D // TILE, FF // TILE, GRAD_CHUNK // TILE
    spare = all_ref.shape[0] - N_QKV - N_REST
    slot = lax.rem(i, 2)

    def first_copies():
        copies = [
            pltpu.make_async_copy(
                out_tiles.at[pl.ds(0, N_OUT)], all_ref.at[pl.ds(N_QKV, N_OUT)], out_sem.at[0]
            )
        ]
        if spare:
            copies.append(
                pltpu.make_async_copy(
                    out_tiles.at[pl.ds(N_OUT, spare)],
                    all_ref.at[pl.ds(N_QKV + N_REST, spare)],
                    out_sem.at[1],
                )
            )
        return copies

    def copies_of(step, slot):
        made = [
            pltpu.make_async_copy(
                hid_tiles.at[slot, r],
                all_ref.at[pl.ds(N_QKV + N_OUT + r * f_tiles + step * per, per)],
                sem.at[slot, r],
            )
            for r in range(d_tiles)
        ]
        made.append(
            pltpu.make_async_copy(
                proj_tiles.at[slot],
                all_ref.at[pl.ds(FIRST_PROJ + step * per * d_tiles, per * d_tiles)],
                sem.at[slot, d_tiles],
            )
        )
        return made

    @pl.when(i == 0)
    def _():
        og_turned[...] = og_ref[...].T
        nt_turned[...] = nt_ref[...].T
        total = jnp.zeros((D, D), f32)
        for s in range(seqs):
            total = total + dot(
                att_ref[:, s].reshape(groups * width, span), bg_ref[s * span : (s + 1) * span, :]
            )
        total = total.astype(bf16)
        for r in range(d_tiles):
            for c in range(d_tiles):
                out_tiles[r * d_tiles + c] = total[
                    r * TILE : (r + 1) * TILE, c * TILE : (c + 1) * TILE
                ]
        if spare:
            out_tiles[N_OUT : N_OUT + spare] = jnp.zeros((spare, TILE, TILE), bf16)
        for copy in first_copies():
            copy.start()

    proj = dot(og_turned[...], act_ref[...]).astype(bf16)
    hid = dot(nt_turned[...], hg_ref[...]).astype(bf16)

    @pl.when(i >= 2)
    def _():
        for copy in copies_of(i - 2, slot):
            copy.wait()

    for c in range(per):
        for r in range(d_tiles):
            rows, cols = slice(r * TILE, (r + 1) * TILE), slice(c * TILE, (c + 1) * TILE)
            proj_tiles[slot, c * d_tiles + r] = proj[rows, cols]
            hid_tiles[slot, r, c] = hid[rows, cols]
    for copy in copies_of(i, slot):
        copy.start()

    @pl.when(i == last)
    def _():
        for copy in copies_of(i - 1, 1 - slot):
            copy.wait()
        for copy in copies_of(i, slot):
            copy.wait()
        for copy in first_copies():
            copy.wait()


def weight_grads(total_tiles, att, bg, og, nt, act, hg):
    total = bg.shape[0]
    chunks = FF // GRAD_CHUNK
    per = GRAD_CHUNK // TILE
    spare = total_tiles - N_QKV - N_REST
    return pl.pallas_call(
        weight_grad_kernel,
        grid=(chunks,),
        in_specs=[
            whole(att.shape),
            whole(bg.shape),
            whole(og.shape),
            whole(nt.shape),
            pl.BlockSpec((total, GRAD_CHUNK), lambda i: (0, i)),
            pl.BlockSpec((total, GRAD_CHUNK), lambda i: (0, i)),
        ],
        out_specs=pl.BlockSpec(memory_space=pl.ANY),
        out_shape=jax.ShapeDtypeStruct((total_tiles, TILE, TILE), bf16),
        scratch_shapes=[
            pltpu.VMEM((N_OUT + spare, TILE, TILE), bf16),
            pltpu.VMEM((2, D // TILE, per, TILE, TILE), bf16),
            pltpu.VMEM((2, per * (D // TILE), TILE, TILE), bf16),
            pltpu.VMEM((D, total), bf16),
            pltpu.VMEM((D, total), bf16),
            pltpu.SemaphoreType.DMA((2, D // TILE + 1)),
            pltpu.SemaphoreType.DMA((2,)),
        ],
        compiler_params=params(),
        cost_estimate=pl.CostEstimate(
            flops=12_000_000_000, bytes_accessed=40_000_000, transcendentals=0
        ),
        name="weight_grads",
    )(att, bg, og, nt, act, hg)


def bits_of(size):
    return size.bit_length() - 1


def exchange_bits(dp, seq):
    return (
        [("seq", 0)]
        + [("dp", b) for b in range(bits_of(dp))]
        + [("seq", b) for b in range(1, bits_of(seq))]
    )


def partner_of(axis, bit):
    here = {"dp": lax.axis_index("dp"), "seq": lax.axis_index("seq")}
    side = (here[axis] // (1 << bit)) % 2
    here[axis] = here[axis] + (1 << bit) * (1 - 2 * side)
    return (here["dp"], here["seq"]), side


def greet(partners):
    barrier = pltpu.get_barrier_semaphore()
    for device in partners:
        pl.semaphore_signal(barrier, inc=1, device_id=device, device_id_type=MESH)
    pl.semaphore_wait(barrier, len(partners))


def tile_sum_kernel(stages, chunks, g_ref, out_ref, mine, *rest):
    count = len(stages)
    received = rest[:count]
    send_sem, recv_sem, copy_sem = rest[count:]
    partners = [partner_of(axis, bit) for axis, bit, _, _ in stages]
    greet([device for device, _ in partners])

    def view(ref, above, below):
        return ref.reshape(above, 2, below, *ref.shape[-3:])

    def send(stage, k):
        _, _, above, below = stages[stage]
        device, side = partners[stage]
        source = g_ref if stage == 0 else received[stage - 1]
        at = pl.ds(*chunks[k])
        return pltpu.make_async_remote_copy(
            src_ref=view(source, above, below).at[:, 1 - side, :, at],
            dst_ref=received[stage].reshape(above, below, *received[stage].shape[-3:]).at[:, :, at],
            send_sem=send_sem.at[stage, k],
            recv_sem=recv_sem.at[stage, k],
            device_id=device,
            device_id_type=MESH,
        )

    def own(k):
        _, _, above, below = stages[0]
        at = pl.ds(*chunks[k])
        return pltpu.make_async_copy(
            view(g_ref, above, below).at[:, partners[0][1], :, at],
            mine.reshape(above, below, *mine.shape[-3:]).at[:, :, at],
            copy_sem.at[k],
        )

    for k in range(len(chunks)):
        send(0, k).start()
        own(k).start()
    for step in range(1, len(chunks) + count):
        for k in range(len(chunks)):
            stage = step - k
            if not 1 <= stage <= count:
                continue
            send(stage - 1, k).wait_recv()
            _, _, above, below = stages[stage - 1]
            side = partners[stage - 1][1]
            at = pl.ds(*chunks[k])
            if stage == 1:
                own(k).wait()

            def add(i, carry):
                if stage == 1:
                    kept = mine[i, at]
                else:
                    up, low = i // below, i % below
                    kept = received[stage - 2][(up * 2 + side) * below + low, at]
                total = kept.astype(f32) + received[stage - 1][i, at].astype(f32)
                if stage == count:
                    out_ref[at] = total
                else:
                    received[stage - 1][i, at] = total.astype(bf16)
                return carry

            lax.fori_loop(0, above * below, add, 0)
            if stage < count:
                send(stage, k).start()
    for stage in range(count):
        for k in range(len(chunks)):
            send(stage, k).wait_send()


def tile_sum(g, dp, seq):
    devices = dp * seq
    owned = g.shape[0] // devices
    tail = (owned, TILE, TILE)
    left = [("dp", b) for b in reversed(range(bits_of(dp)))] + [
        ("seq", b) for b in reversed(range(bits_of(seq)))
    ]
    stages = []
    for axis, bit in exchange_bits(dp, seq):
        place = left.index((axis, bit))
        stages.append((axis, bit, 1 << place, 1 << (len(left) - 1 - place)))
        left.pop(place)
    pieces = min(4, owned)
    edges = [owned * p // pieces for p in range(pieces + 1)]
    chunks = [(low, high - low) for low, high in zip(edges, edges[1:])]
    buffers = [
        pltpu.VMEM((devices >> (i + 1),) + tail, bf16) for i in range(len(stages))
    ]
    return pl.pallas_call(
        functools.partial(tile_sum_kernel, stages, chunks),
        in_specs=[pl.BlockSpec(memory_space=pl.ANY)],
        out_specs=pl.BlockSpec(memory_space=pltpu.VMEM),
        out_shape=jax.ShapeDtypeStruct(tail, f32),
        scratch_shapes=[pltpu.VMEM((devices // 2,) + tail, bf16)]
        + buffers
        + [
            pltpu.SemaphoreType.DMA((len(stages), len(chunks))),
            pltpu.SemaphoreType.DMA((len(stages), len(chunks))),
            pltpu.SemaphoreType.DMA((len(chunks),)),
        ],
        compiler_params=pltpu.CompilerParams(
            collective_id=1, has_side_effects=True, vmem_limit_bytes=VMEM_LIMIT
        ),
        cost_estimate=pl.CostEstimate(
            flops=60_000_000_000, bytes_accessed=40_000_000, transcendentals=0
        ),
        name="tile_sum",
    )(g.reshape((devices,) + tail))


AXIS_BITS = {
    "far": ("dp", 2),
    "near": ("dp", 1),
    "y": ("dp", 0),
    "x": ("seq", 1),
    "core": ("seq", 0),
}
ADDRESS = ("far", "near", "y", "x")
FLOW_ORDERS = (("y", "near", "far", "x"), ("near", "x", "y", "far"), ("x", "y", "near", "far"))
HALF = TILE // 2


def flow_stages(order):
    left = list(ADDRESS)
    stages = []
    for name in order:
        place = left.index(name)
        stages.append((name, 1 << place, 1 << (len(left) - 1 - place)))
        left.pop(place)
    return stages


def paired_grad_kernel(
    att_ref,
    bg_ref,
    og_ref,
    nt_ref,
    act_ref,
    hg_ref,
    half_ref,
    made,
    landed,
    done,
    out_made,
    out_landed,
    out_done,
    zeros,
    og_turned,
    nt_turned,
    send_sem,
    recv_sem,
    done_sem,
    out_sem,
    zero_sem,
):
    i = pl.program_id(0)
    last = pl.num_programs(0) - 1
    groups, seqs, width, span = att_ref.shape
    d_tiles, f_tiles, per = D // TILE, FF // TILE, GRAD_CHUNK // TILE
    count = per * d_tiles
    spare = half_ref.shape[0] - N_QKV - N_REST
    sibling, core = partner_of("seq", 0)
    kept = pl.ds(pl.multiple_of(core * HALF, HALF), HALF)
    given = pl.ds(pl.multiple_of((1 - core) * HALF, HALF), HALF)
    slot = lax.rem(i, 2)

    def to_sibling(step, slot):
        return pltpu.make_async_remote_copy(
            src_ref=made.at[slot, :, given],
            dst_ref=landed.at[step],
            send_sem=send_sem.at[slot],
            recv_sem=recv_sem.at[step],
            device_id=sibling,
            device_id_type=MESH,
        )

    def out_to_sibling():
        return pltpu.make_async_remote_copy(
            src_ref=out_made.at[:, given],
            dst_ref=out_landed,
            send_sem=out_sem.at[0],
            recv_sem=out_sem.at[1],
            device_id=sibling,
            device_id_type=MESH,
        )

    def out_copy():
        return pltpu.make_async_copy(out_done, half_ref.at[pl.ds(N_QKV, N_OUT)], out_sem.at[2])

    def zero_copies():
        spots = [(N_QKV // 3 * j, N_QKV // 3) for j in range(3)]
        if spare:
            spots.append((N_QKV + N_REST, spare))
        return [
            pltpu.make_async_copy(
                zeros.at[pl.ds(0, size)], half_ref.at[pl.ds(low, size)], zero_sem.at[j]
            )
            for j, (low, size) in enumerate(spots)
        ]

    def done_copies(step, slot):
        copies = [
            pltpu.make_async_copy(
                done.at[slot, pl.ds(r * per, per)],
                half_ref.at[pl.ds(N_QKV + N_OUT + r * f_tiles + step * per, per)],
                done_sem.at[slot, r],
            )
            for r in range(d_tiles)
        ]
        copies.append(
            pltpu.make_async_copy(
                done.at[slot, pl.ds(count, count)],
                half_ref.at[pl.ds(FIRST_PROJ + step * count, count)],
                done_sem.at[slot, d_tiles],
            )
        )
        return copies

    @pl.when(i == 0)
    def _():
        greet([sibling])
        zeros[...] = jnp.zeros_like(zeros)
        for copy in zero_copies():
            copy.start()
        total = jnp.zeros((D, D), f32)
        for s in range(seqs):
            total = total + dot(
                att_ref[:, s].reshape(groups * width, span), bg_ref[s * span : (s + 1) * span, :]
            )
        total = total.astype(bf16)
        for r in range(d_tiles):
            for c in range(d_tiles):
                out_made[r * d_tiles + c] = total[
                    r * TILE : (r + 1) * TILE, c * TILE : (c + 1) * TILE
                ]
        out_to_sibling().start()
        og_turned[...] = og_ref[...].T
        nt_turned[...] = nt_ref[...].T

    @pl.when(i < last)
    def _():
        @pl.when(i >= 2)
        def _():
            to_sibling(i - 2, slot).wait_send()

        proj = dot(og_turned[...], act_ref[...]).astype(bf16)
        hid = dot(nt_turned[...], hg_ref[...]).astype(bf16)
        for c in range(per):
            for r in range(d_tiles):
                rows, cols = slice(r * TILE, (r + 1) * TILE), slice(c * TILE, (c + 1) * TILE)
                made[slot, count + c * d_tiles + r] = proj[rows, cols]
                made[slot, r * per + c] = hid[rows, cols]
        to_sibling(i, slot).start()

    @pl.when(i >= 1)
    def _():
        before = 1 - slot

        @pl.when(i >= 3)
        def _():
            for copy in done_copies(i - 3, before):
                copy.wait()

        to_sibling(i - 1, before).wait_recv()
        done[before] = (
            made[before, :, kept].astype(f32) + landed[i - 1].astype(f32)
        ).astype(bf16)
        for copy in done_copies(i - 1, before):
            copy.start()

    @pl.when(i == 1)
    def _():
        out_to_sibling().wait_recv()
        out_done[...] = (out_made[:, kept].astype(f32) + out_landed[...].astype(f32)).astype(bf16)
        out_copy().start()

    @pl.when(i == last)
    def _():
        to_sibling(i - 2, slot).wait_send()
        to_sibling(i - 1, 1 - slot).wait_send()
        out_to_sibling().wait_send()
        out_copy().wait()
        for copy in zero_copies():
            copy.wait()
        for copy in done_copies(i - 2, slot):
            copy.wait()
        for copy in done_copies(i - 1, 1 - slot):
            copy.wait()


def paired_grads(total_tiles, att, bg, og, nt, act, hg):
    total = bg.shape[0]
    chunks = FF // GRAD_CHUNK
    per = GRAD_CHUNK // TILE
    count = per * (D // TILE)
    dma = pltpu.SemaphoreType.DMA
    column = pl.BlockSpec((total, GRAD_CHUNK), lambda i: (0, jnp.minimum(i, chunks - 1)))
    return pl.pallas_call(
        paired_grad_kernel,
        grid=(chunks + 1,),
        in_specs=[whole(a.shape) for a in (att, bg, og, nt)] + [column, column],
        out_specs=pl.BlockSpec(memory_space=pl.ANY),
        out_shape=jax.ShapeDtypeStruct((total_tiles, HALF, TILE), bf16),
        scratch_shapes=[
            pltpu.VMEM((2, 2 * count, TILE, TILE), bf16),
            pltpu.VMEM((chunks, 2 * count, HALF, TILE), bf16),
            pltpu.VMEM((2, 2 * count, HALF, TILE), bf16),
            pltpu.VMEM((N_OUT, TILE, TILE), bf16),
            pltpu.VMEM((N_OUT, HALF, TILE), bf16),
            pltpu.VMEM((N_OUT, HALF, TILE), bf16),
            pltpu.VMEM((N_QKV // 3, HALF, TILE), bf16),
            pltpu.VMEM((D, total), bf16),
            pltpu.VMEM((D, total), bf16),
            dma((2,)),
            dma((chunks,)),
            dma((2, D // TILE + 1)),
            dma((3,)),
            dma((4,)),
        ],
        compiler_params=pltpu.CompilerParams(
            dimension_semantics=("arbitrary",),
            collective_id=4,
            has_side_effects=True,
            vmem_limit_bytes=VMEM_LIMIT,
        ),
        cost_estimate=pl.CostEstimate(
            flops=12_000_000_000, bytes_accessed=40_000_000, transcendentals=0
        ),
        name="paired_grads",
    )(att, bg, og, nt, act, hg)


Q_UNITS = 27


def attend_back_sum_kernel(
    heads,
    flows,
    len_ref,
    fresh_ref,
    q_ref,
    k_ref,
    v_ref,
    o_ref,
    g_ref,
    lse_ref,
    x_ref,
    w_ref,
    half_ref,
    in_ref,
    dv_ref,
    raw_ref,
    db_ref,
    dw,
    q_wide,
    k_wide,
    g_wide,
    v_wide,
    g_turned,
    dq_acc,
    delta,
    grads,
    dk_acc,
    dv_acc,
    probs,
    score_grads,
    dxs,
    dx_core,
    dx_across,
    in_made,
    mine,
    final,
    final_other,
    q_parts,
    q_y,
    q_near,
    q_far,
    q_own,
    core_sem,
    across_sem,
    in_sem,
    own_sem,
    flow_send,
    flow_recv,
    final_sem,
    q_send,
    q_recv,
    q_out,
    q_in,
    *lands,
):
    i = pl.program_id(0)
    blocks, _, span, width_in = x_ref.shape
    count = blocks * span
    width = heads * HD
    bq, bk = BACK_QUERY_BLOCK, BACK_KEY_BLOCK
    per_seq = count // bk
    seqs = dxs.shape[0]
    n, ki = i // per_seq, i % per_seq
    length = len_ref[n]
    dp, s = lax.axis_index("dp"), lax.axis_index("seq")
    y, x, core = dp % 2, s // 2, s % 2
    near, far = (dp // 2) % 2, dp // 4
    owned = raw_ref.shape[0]
    first_tile = (dp * 4 + s) * owned
    partners = {name: partner_of(axis, bit) for name, (axis, bit) in AXIS_BITS.items()}

    def view(ref, above, below):
        return ref.reshape(above, 2, below, *ref.shape[-3:])

    def flow_send_copy(f, k):
        low, size, stages = flows[f]
        name, above, below = stages[k]
        device, side = partners[name]
        land = lands[f * 4 + k]
        if k == 0:
            source = view(half_ref, above, below).at[:, 1 - side, :, pl.ds(low, size)]
        else:
            source = view(lands[f * 4 + k - 1], above, below).at[:, 1 - side]
        return pltpu.make_async_remote_copy(
            src_ref=source,
            dst_ref=land.reshape(above, below, *land.shape[-3:]),
            send_sem=flow_send.at[f, k],
            recv_sem=flow_recv.at[f, k],
            device_id=device,
            device_id_type=MESH,
        )

    def own_copy(f):
        low, size, stages = flows[f]
        name, above, below = stages[0]
        return pltpu.make_async_copy(
            view(half_ref, above, below).at[:, partners[name][1], :, pl.ds(low, size)],
            mine.reshape(above, below, *mine.shape[-3:]).at[:, :, pl.ds(0, size)],
            own_sem.at[f],
        )

    def flow_add(f, k):
        low, size, stages = flows[f]
        name, above, below = stages[k]
        side = partners[name][1]
        land = lands[f * 4 + k]
        flow_send_copy(f, k).wait_recv()
        if k == 0:
            own_copy(f).wait()

        def add(e, carry):
            if k == 0:
                kept = mine[e, 0:size]
            else:
                kept = lands[f * 4 + k - 1][((e // below) * 2 + side) * below + e % below]
            total = kept.astype(f32) + land[e].astype(f32)
            if k == 3:
                final[low : low + size] = total
            else:
                land[e] = total.astype(bf16)
            return carry

        lax.fori_loop(0, above * below, add, 0)

    def dx_core_copy(m, block):
        return pltpu.make_async_remote_copy(
            src_ref=dxs.at[m, block],
            dst_ref=dx_core.at[m, block // 2],
            send_sem=core_sem.at[m, block // 2, 0],
            recv_sem=core_sem.at[m, block // 2, 1],
            device_id=partners["core"][0],
            device_id_type=MESH,
        )

    def dx_across_copy(m):
        return pltpu.make_async_remote_copy(
            src_ref=dx_core.at[m, 1 - x],
            dst_ref=dx_across.at[m],
            send_sem=across_sem.at[m, 0],
            recv_sem=across_sem.at[m, 1],
            device_id=partners["x"][0],
            device_id_type=MESH,
        )

    def dx_pass(m, block):
        @pl.when(block % 2 == core)
        def _():
            dx_core_copy(m, block).wait_recv()

            @pl.when(block // 2 != x)
            def _():
                dx_core[m, 1 - x] = (
                    dxs[m, block].astype(f32) + dx_core[m, 1 - x].astype(f32)
                ).astype(bf16)
                dx_across_copy(m).start()

    def dx_end(m):
        dx_across_copy(m).wait_recv()
        if m:
            in_copy(m - 1).wait()
        in_made[...] = (
            dxs[m, s].astype(f32) + dx_core[m, x].astype(f32) + dx_across[m].astype(f32)
        )
        in_copy(m).start()

    def in_copy(m):
        return pltpu.make_async_copy(in_made, in_ref.at[m], in_sem.at[m])

    @pl.when(i == 0)
    def _():
        mates = [
            (dp - y + (y + dy) % 2, (s + ds) % 4) for dy in range(2) for ds in range(4) if dy or ds
        ]
        greet(mates + [partners["near"][0], partners["far"][0]])
        for f in range(3):
            flow_send_copy(f, 0).start()
        own_copy(0).start()
        delta[...] = jnp.zeros_like(delta)
        dw[...] = jnp.zeros_like(dw)
        db_ref[...] = jnp.zeros_like(db_ref)

    @pl.when(i == per_seq - 1)
    def _():
        for f in range(3):
            flow_add(f, 0)
            if f < 2:
                own_copy(f + 1).start()
            flow_send_copy(f, 1).start()

    @pl.when(i > 0)
    def _():
        dx_pass((i - 1) // per_seq, (i - 1) % per_seq)

    @pl.when(i == per_seq + 1)
    def _():
        for f in range(3):
            flow_add(f, 1)
            flow_send_copy(f, 2).start()

    @pl.when(i == per_seq + 2)
    def _():
        for f in range(1, 3):
            flow_add(f, 2)
            flow_send_copy(f, 3).start()

    @pl.when(i == per_seq + 3)
    def _():
        flow_add(0, 2)
        flow_send_copy(0, 3).start()

    @pl.when(ki == 0)
    def _():
        row = lax.broadcasted_iota(jnp.int32, (16, count), 0)
        dead = lax.broadcasted_iota(jnp.int32, (16, count), 1) >= length
        ones = jnp.where(row < 3, 1.0, 0.0)
        key_side = jnp.where((row == 3) & dead, masked_score, ones).astype(bf16)
        ones = ones.astype(bf16)

        def in_parts(line, last):
            high = line.astype(bf16).astype(f32)
            rest = line - high
            middle = rest.astype(bf16).astype(f32)
            low = rest - middle
            parts = jnp.where(row == 0, high, jnp.where(row == 1, middle, low))
            return jnp.where(row < 3, parts, jnp.where(row == 3, last, 0.0)).astype(bf16)

        for b in range(blocks):
            at = slice(b * span, (b + 1) * span)
            g_block = g_ref[b, 0]
            g_turned[:, at] = g_block
            product = o_ref[b, 0].astype(f32) * g_block.astype(f32)
            for h in range(heads):
                rows = slice(h * HD, (h + 1) * HD)
                delta[h : h + 1, at] = jnp.sum(product[rows, :], axis=0, keepdims=True)
        for h in range(heads):
            rows = slice(h * HD, (h + 1) * HD)
            lse_part = in_parts(lse_ref[0, h : h + 1, :] * (-1.0 / (SCALE * LOG2E)), 1.0)
            delta_part = in_parts(-delta[h : h + 1, :], 0.0)
            q_wide[h] = jnp.concatenate([q_ref[0, rows, :], lse_part], axis=0).T
            g_wide[h] = jnp.concatenate([g_turned[rows, :], delta_part], axis=0).T
            k_wide[h, 0:HD] = k_ref[0, rows, :]
            k_wide[h, HD : HD + 16] = key_side
            v_wide[h, 0:HD] = v_ref[0, rows, :]
            v_wide[h, HD : HD + 16] = ones
        dq_acc[...] = jnp.zeros_like(dq_acc)

    k0 = pl.multiple_of(ki * bk, bk)
    dk_acc[...] = jnp.zeros_like(dk_acc)
    dv_acc[...] = jnp.zeros_like(dv_acc)

    def step(qi, masked, low=0, cols_here=bk):
        skip = low if masked else 0
        here = slice(low, low + cols_here)
        keys = pl.ds(pl.multiple_of(k0 + low, HALF_BLOCK), cols_here)
        at = pl.ds(pl.multiple_of(qi * bq + skip, HALF_BLOCK), bq - skip)
        tall = bq - skip
        for h in range(heads):
            rows = slice(h * HD, (h + 1) * HD)
            for c0 in range(0, cols_here, SUB_COLS):
                some = pl.ds(pl.multiple_of(k0 + low + c0, TILE), SUB_COLS)
                cols = slice(c0, c0 + SUB_COLS)
                for r0 in range(0, tall, SUB_ROWS):
                    part = pl.ds(pl.multiple_of(qi * bq + skip + r0, TILE), SUB_ROWS)
                    p = jnp.exp2(dot(q_wide[h, part, :], k_wide[h, :, some]) * (SCALE * LOG2E))
                    if masked and r0 < c0 + SUB_COLS - 1:
                        shape = (SUB_ROWS, SUB_COLS)
                        allowed = c0 + lax.broadcasted_iota(
                            jnp.int32, shape, 1
                        ) <= r0 + lax.broadcasted_iota(jnp.int32, shape, 0)
                        p = jnp.where(allowed, p, 0.0)
                    probs[h, r0 : r0 + SUB_ROWS, cols] = p.astype(bf16)
                    score_grads[h, r0 : r0 + SUB_ROWS, cols] = (
                        p * dot(g_wide[h, part, :], v_wide[h, :, some])
                    ).astype(bf16)
        for h in range(heads):
            rows = slice(h * HD, (h + 1) * HD)
            p = probs[h, 0:tall, 0:cols_here]
            ds = score_grads[h, 0:tall, 0:cols_here]
            dv_acc[rows, here] = dv_acc[rows, here] + dot(g_turned[rows, at], p)
            dk_acc[rows, here] = dk_acc[rows, here] + dot(q_ref[0, rows, at], ds)
            dq_acc[rows, at] = dq_acc[rows, at] + dot(k_ref[0, rows, keys], ds, NT)

    step(ki, True, 0, HALF_BLOCK)
    step(ki, True, HALF_BLOCK, HALF_BLOCK)
    lax.fori_loop(ki + 1, count // bq, lambda j, c: (step(j, False), c)[1], 0)
    grads[0:width, :] = (dq_acc[:, pl.ds(k0, bk)] * SCALE).astype(bf16)
    grads[width : 2 * width, :] = (dk_acc[...] * SCALE).astype(bf16)
    grads[2 * width :, :] = dv_acc[...].astype(bf16)
    dv_ref[ki, 0] = grads[2 * width :, :]

    @pl.when(x == 1)
    def _():
        grads[2 * width :, :] = jnp.zeros((width, bk), bf16)

    dw[...] += dot(grads[...], x_ref[ki, 0])
    db_ref[...] += dot(jnp.ones((8, bk), bf16), grads[...], NT)[0:1]

    def q_copy(kind, c):
        at = pl.ds(c * 9, 9)
        if kind == 0:
            source, target, name = q_parts.at[1 - y, at], q_y.at[at], "y"
        elif kind == 1:
            source, target, name = q_y.at[at], q_near.at[at], "near"
        else:
            source, target, name = q_y.at[at], q_far.at[at], "far"
        return pltpu.make_async_remote_copy(
            src_ref=source,
            dst_ref=target,
            send_sem=q_send.at[kind, c],
            recv_sem=q_recv.at[kind, c],
            device_id=partners[name][0],
            device_id_type=MESH,
        )

    def q_deliver(c, act):
        for e in range(c * 9, c * 9 + 9):
            r = 3 * y + (e // 3) % 3
            unit = core * 3 + e % 3
            if c < 2:
                index = c * N_OUT + r * (D // TILE) + 3 * x + unit // 2
            else:
                index = 2 * N_OUT + r * (VW // TILE) + unit // 2
            owner = index // owned
            target = (owner // 4, owner % 4)
            rows = pl.ds(pl.multiple_of((unit % 2) * HALF, HALF), HALF)
            here = (target[0] == dp) & (target[1] == s)
            real = (x == 0) if c == 2 else (x >= 0)
            spot = q_own.at[index % owned, rows]

            @pl.when(real & here)
            def _():
                if act == "start":
                    pltpu.make_async_copy(q_y.at[e], spot, q_in).start()

            @pl.when(real & jnp.logical_not(here))
            def _():
                copy = pltpu.make_async_remote_copy(
                    src_ref=q_y.at[e],
                    dst_ref=spot,
                    send_sem=q_out.at[e],
                    recv_sem=q_in,
                    device_id=target,
                    device_id_type=MESH,
                )
                if act == "start":
                    copy.start()
                else:
                    copy.wait_send()

    def q_add(c, extra):
        at = slice(c * 9, c * 9 + 9)
        kept = q_parts[y, at] if extra is q_y else q_y[at]
        q_y[at] = (kept.astype(f32) + extra[at].astype(f32)).astype(bf16)

    @pl.when(i == seqs * per_seq - 1)
    def _():
        for e in range(Q_UNITS):
            which, rr, piece = e // 9, (e // 3) % 3, e % 3
            at = which * width + piece * HALF
            for yy in range(2):
                r = 3 * yy + rr
                q_parts[yy, e] = dw[at : at + HALF, r * TILE : (r + 1) * TILE].astype(bf16)
        for c in range(3):
            q_copy(0, c).start()

    dxs[n, ki] = dot(grads[...], w_ref[...], TN).astype(bf16)

    @pl.when(ki % 2 != core)
    def _():
        dx_core_copy(n, ki).start()

    @pl.when(i == seqs * per_seq - 1)
    def _():
        to_sibling = pltpu.make_async_remote_copy(
            src_ref=final.at[pl.ds((1 - core) * owned, owned)],
            dst_ref=final_other,
            send_sem=final_sem.at[0],
            recv_sem=final_sem.at[1],
            device_id=partners["core"][0],
            device_id_type=MESH,
        )

        def q_first(c):
            q_copy(0, c).wait_recv()
            q_add(c, q_y)

            @pl.when(near == 1)
            def _():
                q_copy(1, c).start()

        def q_second(c):
            @pl.when(near == 0)
            def _():
                q_copy(1, c).wait_recv()
                q_add(c, q_near)

                @pl.when(far == 1)
                def _():
                    q_copy(2, c).start()

        def q_third(c):
            @pl.when((near == 0) & (far == 0))
            def _():
                q_copy(2, c).wait_recv()
                q_add(c, q_far)
                q_deliver(c, "start")

        q_first(0)
        dx_pass(seqs - 1, per_seq - 1)
        q_first(1)
        q_second(0)
        q_first(2)
        q_second(1)
        for f in range(3):
            flow_add(f, 3)
        to_sibling.start()
        q_third(0)
        q_second(2)
        q_third(1)
        dx_end(0)
        q_third(2)
        to_sibling.wait_recv()
        kept = pl.ds(pl.multiple_of(core * HALF, HALF), HALF)
        given = pl.ds(pl.multiple_of((1 - core) * HALF, HALF), HALF)
        raw_ref[:, kept, :] = final[pl.ds(core * owned, owned)]
        raw_ref[:, given, :] = final_other[...]
        for m in range(1, seqs):
            dx_end(m)

        @pl.when(first_tile + owned <= N_QKV)
        def _():
            pltpu.make_async_copy(q_own, q_own, q_in).wait()
            raw_ref[...] = q_own[...].astype(f32)

        part = N_QKV % owned
        if part:

            @pl.when((first_tile < N_QKV) & (first_tile + owned > N_QKV))
            def _():
                at = pl.ds(0, part)
                pltpu.make_async_copy(q_own.at[at], q_own.at[at], q_in).wait()
                raw_ref[0:part] = q_own[0:part].astype(f32)

        in_copy(seqs - 1).wait()
        to_sibling.wait_send()
        for m in range(seqs):
            for pair in range(2):
                dx_core_copy(m, 2 * pair + 1 - core).wait_send()
            dx_across_copy(m).wait_send()
        for f in range(3):
            for k in range(4):
                flow_send_copy(f, k).wait_send()
        for c in range(3):
            q_copy(0, c).wait_send()

            @pl.when(near == 1)
            def _():
                q_copy(1, c).wait_send()

            @pl.when((near == 0) & (far == 1))
            def _():
                q_copy(2, c).wait_send()

            @pl.when((near == 0) & (far == 0))
            def _():
                q_deliver(c, "wait")


def attend_back_sum(lengths, fresh, q, k, v, o, g, lse, x, w, half):
    blocks, seqs, span, _ = x.shape
    width = q.shape[1]
    heads = width // HD
    count = blocks * span
    owned = half.shape[0] // 32
    per_seq = count // BACK_KEY_BLOCK
    pair = 2 * owned
    edges = [pair * p // 3 for p in range(4)]
    flows = [
        (low, high - low, flow_stages(order))
        for low, high, order in zip(edges, edges[1:], FLOW_ORDERS)
    ]
    one = lambda shape: pl.BlockSpec((1,) + shape, lambda i, *_: (i // per_seq,) + (0,) * len(shape))
    mid = lambda shape: pl.BlockSpec((blocks, 1) + shape, lambda i, *_: (0, i // per_seq, 0, 0))
    single = lambda shape: pl.BlockSpec(
        (1,) + shape, lambda i, *_: (i // per_seq, 0, 0), pipeline_mode=pl.Buffered(1)
    )
    dma = pltpu.SemaphoreType.DMA
    return pl.pallas_call(
        functools.partial(attend_back_sum_kernel, heads, flows),
        grid_spec=pltpu.PrefetchScalarGridSpec(
            num_scalar_prefetch=2,
            grid=(seqs * per_seq,),
            in_specs=[
                one((width, count)),
                single((width, count)),
                single((width, count)),
                pl.BlockSpec(
                    (blocks, 1, width, span),
                    lambda i, *_: (0, i // per_seq, 0, 0),
                    pipeline_mode=pl.Buffered(1),
                ),
                mid((width, span)),
                one((8, count)),
                pl.BlockSpec(
                    (blocks, 1, span, D),
                    lambda i, *_: (0, i // per_seq, 0, 0),
                    pipeline_mode=pl.Buffered(1),
                ),
                pl.BlockSpec(
                    (3 * width, D), lambda i, *_: (0, 0), pipeline_mode=pl.Buffered(1)
                ),
                pl.BlockSpec(memory_space=pl.ANY),
            ],
            out_specs=[
                pl.BlockSpec(memory_space=pl.ANY),
                mid((width, span)),
                whole((owned, TILE, TILE)),
                whole((1, 3 * width)),
            ],
            scratch_shapes=[
                pltpu.VMEM((3 * width, D), f32),
                pltpu.VMEM((heads, count, HD + 16), bf16),
                pltpu.VMEM((heads, HD + 16, count), bf16),
                pltpu.VMEM((heads, count, HD + 16), bf16),
                pltpu.VMEM((heads, HD + 16, count), bf16),
                pltpu.VMEM((width, count), bf16),
                pltpu.VMEM((width, count), f32),
                pltpu.VMEM((8, count), f32),
                pltpu.VMEM((3 * width, BACK_KEY_BLOCK), bf16),
                pltpu.VMEM((width, BACK_KEY_BLOCK), f32),
                pltpu.VMEM((width, BACK_KEY_BLOCK), f32),
                pltpu.VMEM((heads, BACK_QUERY_BLOCK, BACK_KEY_BLOCK), bf16),
                pltpu.VMEM((heads, BACK_QUERY_BLOCK, BACK_KEY_BLOCK), bf16),
                pltpu.VMEM((seqs, blocks, span, D), bf16),
                pltpu.VMEM((seqs, 2, span, D), bf16),
                pltpu.VMEM((seqs, span, D), bf16),
                pltpu.VMEM((span, D), f32),
                pltpu.VMEM((8, -(-pair // 3), HALF, TILE), bf16),
                pltpu.VMEM((pair, HALF, TILE), f32),
                pltpu.VMEM((owned, HALF, TILE), f32),
                pltpu.VMEM((2, Q_UNITS, HALF, TILE), bf16),
                pltpu.VMEM((Q_UNITS, HALF, TILE), bf16),
                pltpu.VMEM((Q_UNITS, HALF, TILE), bf16),
                pltpu.VMEM((Q_UNITS, HALF, TILE), bf16),
                pltpu.VMEM((owned, TILE, TILE), bf16),
                dma((seqs, 2, 2)),
                dma((seqs, 2)),
                dma((seqs,)),
                dma((3,)),
                dma((3, 4)),
                dma((3, 4)),
                dma((2,)),
                dma((3, 3)),
                dma((3, 3)),
                dma((Q_UNITS,)),
                dma(()),
            ]
            + [
                pltpu.VMEM((8 >> k, size, HALF, TILE), bf16)
                for _, size, _ in flows
                for k in range(4)
            ],
        ),
        out_shape=[
            jax.ShapeDtypeStruct((seqs, span, D), f32),
            jax.ShapeDtypeStruct((blocks, seqs, width, span), bf16),
            jax.ShapeDtypeStruct((owned, TILE, TILE), f32),
            jax.ShapeDtypeStruct((1, 3 * width), f32),
        ],
        compiler_params=pltpu.CompilerParams(
            dimension_semantics=("arbitrary",),
            collective_id=5,
            has_side_effects=True,
            vmem_limit_bytes=VMEM_LIMIT,
        ),
        cost_estimate=pl.CostEstimate(
            flops=70_000_000_000, bytes_accessed=25_000_000, transcendentals=0
        ),
        name="attend_back_sum",
    )(lengths, fresh, q, k, v, o, g, lse, x, w, half.reshape(16, pair, HALF, TILE))


VEC_ROWS = 72


def finish_kernel(
    stages,
    raw_ref,
    gain_ref,
    rows_ref,
    hsum_ref,
    db_ref,
    master_ref,
    left_ref,
    right_ref,
    left_root_ref,
    right_root_ref,
    par_ref,
    stat_ref,
    clip_out,
    left_out,
    right_out,
    tiles_out,
    vec_out,
    stat_out,
    par_out,
    norm_out,
    total,
    landing,
    send_sem,
    recv_sem,
):
    owned = raw_ref.shape[0]
    used = par_ref.shape[0]
    partners = [partner_of(axis, bit)[0] for axis, bit in stages]
    greet(partners)
    squares = jnp.zeros((TILE, TILE), f32)
    for t in range(owned):
        squares = squares + raw_ref[t] * raw_ref[t]
    per = D // TILE
    width = db_ref.shape[1] // 3
    group = lax.axis_index("seq")
    total[...] = jnp.zeros_like(total)
    for piece, (ref, row) in enumerate(
        ((gain_ref, 0), (gain_ref, 1), (rows_ref, 0), (rows_ref, 1), (None, 0), (rows_ref, 2), (rows_ref, 3))
    ):
        if ref is not None:
            for c in range(per):
                total[piece * per + c : piece * per + c + 1, :] = ref[
                    row : row + 1, c * TILE : (c + 1) * TILE
                ]
    for part, start in ((0, 4 * per), (2, 7 * per)):
        for unit in range(width // HALF):
            value = db_ref[:, part * width + unit * HALF : part * width + (unit + 1) * HALF]
            both = jnp.concatenate([value, value], axis=1)
            lane = lax.broadcasted_iota(jnp.int32, (1, TILE), 1) // HALF
            place = group * (width // HALF) + unit
            room = (D if part == 0 else VW) // HALF
            row = start + jnp.minimum(place, room - 1) // 2
            keep = (lane == place % 2) & (place < room)
            total[pl.ds(row, 1), :] = total[pl.ds(row, 1), :] + jnp.where(keep, both, 0.0)
    for c in range(FF // TILE):
        at = 7 * per + VW // TILE + c
        total[at : at + 1, :] = hsum_ref[:, c * TILE : (c + 1) * TILE]
    total[used : used + 1, :] = jnp.sum(squares, axis=0, keepdims=True)
    for i, device in enumerate(partners):
        landing[i, 0] = total[...]
        copy = pltpu.make_async_remote_copy(
            src_ref=landing.at[i, 0],
            dst_ref=landing.at[i, 1],
            send_sem=send_sem.at[i],
            recv_sem=recv_sem.at[i],
            device_id=device,
            device_id_type=MESH,
        )
        copy.start()
        copy.wait()
        total[...] = total[...] + landing[i, 1]
    vector = total[0:used, :]
    square_sum = jnp.sum(total[used : used + 1, :], axis=1, keepdims=True) + jnp.sum(
        jnp.sum(vector * vector, axis=0, keepdims=True), axis=1, keepdims=True
    )
    grad_norm = jnp.sqrt(square_sum)
    factor = jnp.minimum(1.0, CLIP / (grad_norm + clip_eps))
    norm_out[...] = jnp.broadcast_to(grad_norm, norm_out.shape)
    grads = vector * factor
    vec_out[...] = grads
    stat = decay_rate * stat_ref[...] + (1.0 - decay_rate) * grads * grads
    stat_out[...] = stat
    par_out[...] = par_ref[...] - vector_rate * grads / (jnp.sqrt(stat) + moment_eps)
    first = (lax.axis_index("dp") * lax.axis_size("seq") + lax.axis_index("seq")) * owned

    def exact(a, b, dims):
        return lax.dot_general(a, b, dims, precision=highest, preferred_element_type=f32)

    for t in range(owned):
        index = first + t
        turned = (index < N_QKV) | (index >= FIRST_PROJ)
        raw = raw_ref[t]
        tile = jnp.where(turned, raw.T, raw) * factor
        clip_out[t] = tile
        left_out[t] = decay_rate * left_ref[t] + (1.0 - decay_rate) * exact(tile, tile, NT)
        flipped = tile.T
        right_out[t] = decay_rate * right_ref[t] + (1.0 - decay_rate) * exact(flipped, flipped, NT)
        inner = exact(tile, right_root_ref[t], NN)
        tiles_out[t] = master_ref[t] - matrix_rate * exact(left_root_ref[t], inner, NN)


def finish(raw, vectors, master, left, right, left_root, right_root, par, stat, dp, seq):
    stages = exchange_bits(dp, seq)
    tiles = jax.ShapeDtypeStruct(raw.shape, f32)
    vector = jax.ShapeDtypeStruct(par.shape, f32)
    vm = pl.BlockSpec(memory_space=pltpu.VMEM)
    return pl.pallas_call(
        functools.partial(finish_kernel, stages),
        in_specs=[vm] * 12,
        out_specs=[vm] * 8,
        out_shape=[tiles] * 4 + [vector] * 3 + [jax.ShapeDtypeStruct((8, TILE), f32)],
        scratch_shapes=[
            pltpu.VMEM((VEC_ROWS, TILE), f32),
            pltpu.VMEM((len(stages), 2, VEC_ROWS, TILE), f32),
            pltpu.SemaphoreType.DMA((len(stages),)),
            pltpu.SemaphoreType.DMA((len(stages),)),
        ],
        compiler_params=pltpu.CompilerParams(
            collective_id=2, has_side_effects=True, vmem_limit_bytes=VMEM_LIMIT
        ),
        name="finish",
    )(raw, *vectors, master, left, right, left_root, right_root, par, stat)


def per_device(
    tokens,
    first_values,
    cotangent,
    lengths,
    master_tiles,
    left_stat,
    right_stat,
    left_root,
    right_root,
    vector_params,
    vector_stat,
):
    seqs, span, _ = tokens.shape
    owned_count = master_tiles.shape[0]
    groups = lax.axis_size("seq")
    me_seq = lax.axis_index("seq")
    width = D // groups
    fresh_groups = VW // width
    total_tiles = owned_count * groups * lax.axis_size("dp")

    (
        gain_one,
        shift_one,
        gain_two,
        shift_two,
        query_bias,
        out_bias,
        proj_bias,
        value_bias,
        hidden_bias,
    ) = split_vector(vector_params)

    fits = front_fits(lax.axis_size("dp"), groups, owned_count)
    flat_tokens = tokens.reshape(-1, D).astype(f32)
    normed_one, unit_one, inv_one = norm_forward(flat_tokens, gain_one, shift_one)
    first_turned = first_values.transpose(2, 0, 1).reshape(groups - fresh_groups, width, seqs, span)
    first_turned = first_turned.transpose(0, 2, 1, 3)
    if fits:
        norm_rows = jnp.concatenate(
            [jnp.stack([gain_one, shift_one]), jnp.zeros((6, D), f32)]
        )
        x_all, w_mine, first_mine, g_one, g_two = front(
            tokens, norm_rows, master_tiles, first_turned
        )

        def swap(value, bit):
            pairs = [(d, d ^ bit) for d in range(32)]
            return lax.ppermute(value, ("dp", "seq"), pairs)

        g_one_y, g_two_x = swap(g_one, 4), swap(g_two, 2)
        g_one_core, g_two_core = swap(g_one, 1), swap(g_two, 1)
    else:
        normed_one = normed_one.astype(bf16).reshape(seqs, span, D)
        x_all = lax.all_gather(normed_one, "seq", axis=0, tiled=False)
        gathered = lax.all_gather(
            master_tiles.astype(bf16), ("dp", "seq"), axis=0, tiled=True
        )
        sources = (gathered,)
        first_send = jnp.concatenate(
            [jnp.zeros((fresh_groups,) + first_turned.shape[1:], bf16), first_turned], axis=0
        )
        first_mine = lax.all_to_all(first_send, "seq", 0, 0, tiled=True)
    is_fresh = (me_seq < fresh_groups).astype(jnp.int32).reshape(1)
    fresh_seq = jnp.minimum(me_seq, fresh_groups - 1)

    def turned(start, cols):
        amount = D // TILE * (cols // TILE)
        tiles = gathered[start : start + amount].reshape(D // TILE, cols // TILE, TILE, TILE)
        return tiles.transpose(1, 3, 0, 2).reshape(cols, D)

    if not fits:
        wq = lax.dynamic_slice_in_dim(turned(0, D), me_seq * width, width, 0)
        wk = lax.dynamic_slice_in_dim(turned(N_OUT, D), me_seq * width, width, 0)
        wv = lax.dynamic_slice_in_dim(turned(2 * N_OUT, VW), fresh_seq * width, width, 0)
        w_mine = jnp.concatenate([wq, wk, wv], axis=0)
    qb = lax.dynamic_slice_in_dim(query_bias, me_seq * width, width, 0).reshape(width, 1)
    vb = lax.dynamic_slice_in_dim(value_bias, fresh_seq * width, width, 0).reshape(width, 1)

    o_heads, q, k, v, lse = attend_forward(
        lengths, is_fresh, x_all, w_mine, qb, vb, first_mine
    )
    if fits:
        g_one_y, g_two_x, o_heads = lax.optimization_barrier((g_one_y, g_two_x, o_heads))
        sources = (g_one, g_one_y, g_two, g_two_x)
        sources += (g_one_core, swap(g_one_y, 1), g_two_core, swap(g_two_x, 1))
    att = lax.all_to_all(o_heads, "seq", 0, 0, tiled=True)
    rows = jnp.concatenate(
        [jnp.stack([gain_two, shift_two, out_bias, proj_bias]), jnp.zeros((4, D), f32)]
    )
    position = (me_seq * span).astype(jnp.int32).reshape(1)
    (
        block_output,
        residual_grad,
        att_grad,
        act,
        hidden_grad,
        normed_two,
        branch_grad,
        out_grad,
        row_sums,
        hidden_bias_grad,
    ) = feed_forward(
        lengths,
        position,
        att,
        tokens,
        cotangent,
        sources,
        total_tiles,
        rows,
        hidden_bias.reshape(1, FF),
    )
    g_heads = lax.all_to_all(att_grad, "seq", 0, 0, tiled=True)
    grad_args = (att, branch_grad, out_grad, normed_two, act, hidden_grad)
    back_args = (q, k, v, o_heads, g_heads, lse, x_all, w_mine)
    if fits:
        half_tiles = paired_grads(total_tiles, *grad_args)
        norm_one_in, dv, owned, db = attend_back_sum(lengths, is_fresh, *back_args, half_tiles)
        norm_one_in = norm_one_in.reshape(-1, D)
    else:
        all_tiles = weight_grads(total_tiles, *grad_args)
        group = me_seq.astype(jnp.int32).reshape(1)
        dx, dv, all_tiles, db = attend_backward(lengths, is_fresh, group, *back_args, all_tiles)
        norm_one_in = (
            lax.psum_scatter(dx, "seq", scatter_dimension=0, tiled=True)
            .reshape(-1, D)
            .astype(f32)
        )
        owned = tile_sum(all_tiles, lax.axis_size("dp"), groups)
    dv_back = lax.all_to_all(dv, "seq", 0, 0, tiled=True)
    first_grad = (
        dv_back[fresh_groups:]
        .transpose(1, 3, 0, 2)
        .reshape(first_values.shape)
        .astype(f32)
    )
    token_part = norm_backward(norm_one_in, unit_one, inv_one, gain_one)
    tokens_grad = residual_grad + token_part.reshape(tokens.shape)
    gain_one_grad = jnp.sum(norm_one_in * unit_one, axis=0)
    shift_one_grad = jnp.sum(norm_one_in, axis=0)

    used = vector_params.shape[0] // TILE
    gain_sums = jnp.stack([gain_one_grad, shift_one_grad])
    clipped, left_new, right_new, tiles_new, vector_grads, vector_stat_new, vector_new, norm = (
        finish(
            owned,
            (gain_sums, row_sums, hidden_bias_grad, db),
            master_tiles,
            left_stat,
            right_stat,
            left_root,
            right_root,
            vector_params.reshape(used, TILE),
            vector_stat.reshape(used, TILE),
            lax.axis_size("dp"),
            groups,
        )
    )
    return (
        block_output,
        tokens_grad,
        first_grad,
        clipped,
        left_new,
        right_new,
        tiles_new,
        vector_grads.reshape(-1),
        vector_stat_new.reshape(-1),
        vector_new.reshape(-1),
        norm[0, 0],
    )


def solution(mesh):
    tiles = P(("dp", "seq"), None, None)
    seqs = P("dp", "seq", None)
    in_specs = (seqs, seqs, seqs, P("dp"), tiles, tiles, tiles, tiles, tiles, P(), P())
    out_specs = (seqs, seqs, seqs, tiles, tiles, tiles, tiles, P(), P(), P(), P())
    return jax.shard_map(
        per_device, mesh=mesh, in_specs=in_specs, out_specs=out_specs, check_vma=False
    )
```

```python
import functools

import jax
import jax.numpy as jnp
from jax import lax
from jax.experimental import pallas as pl
from jax.experimental.pallas import tpu as pltpu
from jax.sharding import PartitionSpec as P

D = 768
HD = 64
FF = 3072
VW = 384
TILE = 128
CLIP = 256
LOG2E = 1.4426950408889634
SCALE = HD**-0.5
QUERY_BLOCK = 512
KEY_BLOCK = 512
BACK_QUERY_BLOCK = 512
BACK_KEY_BLOCK = 512
HALF_BLOCK = 256
STRIPE = 256
SUB_ROWS = 256
SUB_COLS = 256
N_QKV = 90
N_OUT = 36
N_HID = 144
N_PROJ = 144
N_REST = N_OUT + N_HID + N_PROJ
FIRST_PROJ = N_QKV + N_OUT + N_HID

highest = lax.Precision.HIGHEST
norm_eps = 1e-05
clip_eps = 1e-06
decay_rate = 0.5
matrix_rate = 0.3
vector_rate = 0.1
moment_eps = 1e-08
masked_score = -1e30

f32 = jnp.float32
bf16 = jnp.bfloat16
NN = (((1,), (0,)), ((), ()))
NT = (((1,), (1,)), ((), ()))
TN = (((0,), (0,)), ((), ()))
VMEM_LIMIT = 60 << 20
MESH = pl.DeviceIdType.MESH


def dot(left_in, right_in, dims=NN):
    return lax.dot_general(left_in, right_in, dims, preferred_element_type=f32)


def split_vector(vector):
    pieces = []
    offset = 0
    for length in (D, D, D, D, D, D, D, VW, FF):
        pieces.append(vector[offset : offset + length])
        offset = offset + length
    return pieces


def norm_forward(values, gain_row, shift_row):
    centered = values - jnp.mean(values, axis=-1, keepdims=True)
    variance = jnp.mean(centered * centered, axis=-1, keepdims=True)
    inv_std = lax.rsqrt(variance + norm_eps)
    unit_rows = centered * inv_std
    return (unit_rows * gain_row + shift_row, unit_rows, inv_std)


def norm_backward(grad_in, unit_rows, inv_std, gain_row):
    scaled = grad_in * gain_row
    term = (
        scaled
        - jnp.mean(scaled, axis=-1, keepdims=True)
        - unit_rows * jnp.mean(scaled * unit_rows, axis=-1, keepdims=True)
    )
    return term * inv_std


def whole(shape):
    return pl.BlockSpec(shape, lambda i, *_: (0,) * len(shape))


def params():
    return pltpu.CompilerParams(dimension_semantics=("arbitrary",), vmem_limit_bytes=VMEM_LIMIT)


W_SLOTS = 56
W_SHARE = W_SLOTS // 4
W_CHUNKS = ((0, 4), (4, 4), (8, 4), (12, 2))
X_CHUNKS = 4


def front_fits(dp, seq, owned):
    return dp == 8 and seq == 4 and 8 * owned >= N_QKV


def front_kernel(
    tok_ref,
    rows_ref,
    master_ref,
    fv_ref,
    x_ref,
    w_ref,
    fv_all,
    g_one,
    g_two,
    normed,
    plain,
    staged,
    slots,
    x_send,
    x_recv,
    own_sem,
    first_send,
    first_recv,
    w_send,
    w_recv,
    g_own,
    g_send,
    g_recv,
    z_send,
    z_recv,
    fv_send,
    fv_recv,
):
    dp, s = lax.axis_index("dp"), lax.axis_index("seq")
    depth = lax.axis_size("dp") // 2
    z, y, x, core = dp // 2, dp % 2, s // 2, s % 2
    owned = master_ref.shape[0]
    first = (dp * 4 + s) * owned
    seqs, span, _ = tok_ref.shape
    other_y, other_x, sibling = dp + 1 - 2 * y, s + 2 - 4 * x, s + 1 - 2 * core

    barrier = pltpu.get_barrier_semaphore()
    for dy in range(2):
        for ds in range(4):
            if dy or ds:
                mate = (2 * z + (y + dy) % 2, (s + ds) % 4)
                pl.semaphore_signal(barrier, inc=1, device_id=mate, device_id_type=MESH)

    @pl.when(z > 0)
    def _():
        pl.semaphore_signal(barrier, inc=1, device_id=(dp - 2, s), device_id_type=MESH)

    @pl.when(z < depth - 1)
    def _():
        pl.semaphore_signal(barrier, inc=1, device_id=(dp + 2, s), device_id_type=MESH)

    at_end = (z == 0) | (z == depth - 1)

    @pl.when(at_end)
    def _():
        pl.semaphore_wait(barrier, 8)

    @pl.when(jnp.logical_not(at_end))
    def _():
        pl.semaphore_wait(barrier, 9)

    def tile_sends(t, act):
        index = first + t
        is_value = index >= 2 * N_OUT
        within = index % N_OUT
        col = within % (D // TILE)
        slot = jnp.where(
            is_value,
            index,
            (index // N_OUT) * 18 + (within // (D // TILE)) * 3 + col % 3,
        )
        slot = jnp.where(is_value, index - N_OUT, slot)
        share = slot // W_SHARE
        chunk = (slot % W_SHARE) // 4
        for copy_index in range(2):
            to_x = jnp.where(is_value, copy_index, col // 3)
            target = (share // 2, to_x * 2 + share % 2)
            needed = (index < N_QKV) & (is_value | (copy_index == 0))
            here = (target[0] == dp) & (target[1] == s)

            @pl.when(needed & here)
            def _():
                if act == "start":
                    pltpu.make_async_copy(
                        staged.at[t], slots.at[slot], first_recv.at[chunk]
                    ).start()

            @pl.when(needed & jnp.logical_not(here))
            def _():
                copy = pltpu.make_async_remote_copy(
                    src_ref=staged.at[t],
                    dst_ref=slots.at[slot],
                    send_sem=first_send.at[t, copy_index],
                    recv_sem=first_recv.at[chunk],
                    device_id=target,
                    device_id_type=MESH,
                )
                if act == "start":
                    copy.start()
                else:
                    copy.wait_send()

    one = g_one.shape[2]
    parts = (
        (plain.at[pl.ds(0, one)], g_one.at[z, x], (dp, other_x)),
        (plain.at[pl.ds(one, owned - one)], g_two.at[dp], (other_y, s)),
    )

    def g_local(f):
        source, target, _ = parts[f]
        return pltpu.make_async_copy(source, target, g_own.at[f])

    def g_first(f):
        source, target, device = parts[f]
        return pltpu.make_async_remote_copy(
            src_ref=source,
            dst_ref=target,
            send_sem=g_send.at[f],
            recv_sem=g_recv.at[f],
            device_id=device,
            device_id_type=MESH,
        )

    def z_copy(up, h, f):
        plane = z - h if up else z + h
        block = g_one.at[plane] if f == 0 else g_two.at[pl.ds(2 * plane, 2)]
        return pltpu.make_async_remote_copy(
            src_ref=block,
            dst_ref=block,
            send_sem=z_send.at[up, h, f],
            recv_sem=z_recv.at[up, h, f],
            device_id=(dp + 2, s) if up else (dp - 2, s),
            device_id_type=MESH,
        )

    def z_landed(up, h, f):
        plane = z - 1 - h if up else z + 1 + h
        block = g_one.at[plane] if f == 0 else g_two.at[pl.ds(2 * plane, 2)]
        return pltpu.make_async_copy(block, block, z_recv.at[up, h, f])

    def z_hop(h):
        for up in (1, 0):
            if h:
                came = (z - h >= 0) if up else (z + h <= depth - 1)

                @pl.when(came)
                def _():
                    for f in range(2):
                        z_landed(up, h - 1, f).wait()

            if h < z_send.shape[1]:
                goes = ((z < depth - 1) & (z - h >= 0)) if up else ((z > 0) & (z + h <= depth - 1))

                @pl.when(goes)
                def _():
                    for f in range(2):
                        z_copy(up, h, f).start()

    for t in range(owned):
        plain[t] = master_ref[t].astype(bf16)
    for f in range(2):
        g_first(f).start()
        g_local(f).start()

    @pl.when(first < N_QKV)
    def _():
        for t in range(owned):
            staged[t] = plain[t].T
        for t in range(owned):
            tile_sends(t, "start")

    rows_each = seqs * span // X_CHUNKS
    per_seq = span // rows_each

    def x_copy(kind, j):
        n, part = j // per_seq, j % per_seq
        at = pl.ds(part * rows_each, rows_each)
        block = other_x if kind == 2 else s
        return pltpu.make_async_remote_copy(
            src_ref=x_ref.at[block, n, at] if kind == 2 else normed.at[n, at],
            dst_ref=x_ref.at[block, n, at],
            send_sem=x_send.at[kind, j],
            recv_sem=x_recv.at[kind, j],
            device_id=(dp, other_x) if kind == 0 else (dp, sibling),
            device_id_type=MESH,
        )

    def own_copy(j):
        n, part = j // per_seq, j % per_seq
        at = pl.ds(part * rows_each, rows_each)
        return pltpu.make_async_copy(normed.at[n, at], x_ref.at[s, n, at], own_sem.at[j])

    for j in range(X_CHUNKS):
        n, part = j // per_seq, j % per_seq
        at = pl.ds(part * rows_each, rows_each)
        value = tok_ref[n, at, :].astype(f32)
        normed[n, at, :] = norm_forward(value, rows_ref[0:1, :], rows_ref[1:2, :])[0].astype(bf16)
        x_copy(0, j).start()
        x_copy(1, j).start()
        own_copy(j).start()

    def fv_copies(act):
        for c in range(2):
            to = 2 + c

            @pl.when(s == to)
            def _():
                copy = pltpu.make_async_copy(fv_ref.at[c], fv_all.at[s], fv_recv.at[to])
                if act == "start":
                    copy.start()

            @pl.when(s != to)
            def _():
                copy = pltpu.make_async_remote_copy(
                    src_ref=fv_ref.at[c],
                    dst_ref=fv_all.at[s],
                    send_sem=fv_send.at[c],
                    recv_sem=fv_recv.at[s],
                    device_id=(dp, to),
                    device_id_type=MESH,
                )
                copy.start() if act == "start" else copy.wait_send()

    fv_copies("start")

    share = y * 2 + core

    def w_copy(kind, j):
        low, size = W_CHUNKS[j]
        base = ((1 - y) * 2 + core) * W_SHARE if kind == 3 else share * W_SHARE
        at = pl.ds(base + low, size)
        device = ((dp + 2, s), (other_y, s), (dp, sibling), (dp, sibling))[kind]
        return pltpu.make_async_remote_copy(
            src_ref=slots.at[at],
            dst_ref=slots.at[at],
            send_sem=w_send.at[kind, j],
            recv_sem=w_recv.at[kind, j],
            device_id=device,
            device_id_type=MESH,
        )

    def landed(j, size):
        low, _ = W_CHUNKS[j]
        at = pl.ds(share * W_SHARE + low, size)
        pltpu.make_async_copy(slots.at[at], slots.at[at], first_recv.at[j]).wait()

    used = 3 * 18 - 3 * W_SHARE
    @pl.when((z == 0) & (share == 3))
    def _():
        slots[3 * W_SHARE + used : W_SLOTS] = jnp.zeros(
            (W_SHARE - used,) + slots.shape[1:], bf16
        )

    for f in range(2):
        g_first(f).wait_recv()
        g_local(f).wait()
    z_hop(0)
    for j in range(len(W_CHUNKS)):
        if j < len(W_CHUNKS):
            low, size = W_CHUNKS[j]
            short = min(size, used - low)

            @pl.when((z == 0) & (share < 3))
            def _():
                landed(j, size)

            if short > 0:

                @pl.when((z == 0) & (share == 3))
                def _():
                    landed(j, short)

            @pl.when(z > 0)
            def _():
                w_copy(0, j).wait_recv()

            @pl.when(z < depth - 1)
            def _():
                w_copy(0, j).start()

            w_copy(1, j).start()
            w_copy(2, j).start()
        if j < len(W_CHUNKS):
            w_copy(1, j).wait_recv()
            w_copy(3, j).start()
    z_hop(1)
    for j in range(X_CHUNKS):
        if j == X_CHUNKS - 1:
            z_hop(2)
        x_copy(0, j).wait_recv()
        x_copy(2, j).start()
    for j in range(len(W_CHUNKS)):
        w_copy(2, j).wait_recv()
        w_copy(3, j).wait_recv()
    width = HD * 3
    for which in range(3):
        for piece in range(3):
            unit = core * 3 + piece
            rows = pl.ds(pl.multiple_of((unit % 2) * HD, HD), HD)
            at = which * width + piece * HD
            for r in range(D // TILE):
                w_ref[at : at + HD, r * TILE : (r + 1) * TILE] = slots[
                    which * 18 + r * 3 + unit // 2, rows, :
                ]
    for j in range(X_CHUNKS):
        x_copy(1, j).wait_recv()
        x_copy(2, j).wait_recv()
        own_copy(j).wait()
        for kind in range(3):
            x_copy(kind, j).wait_send()
    @pl.when(x == 1)
    def _():
        for block in range(4):
            pltpu.make_async_copy(fv_all.at[block], fv_all.at[block], fv_recv.at[block]).wait()

    fv_copies("wait")
    z_hop(3)
    for f in range(2):
        g_first(f).wait_send()
        for h in range(z_send.shape[1]):

            @pl.when((z < depth - 1) & (z - h >= 0))
            def _():
                z_copy(1, h, f).wait_send()

            @pl.when((z > 0) & (z + h <= depth - 1))
            def _():
                z_copy(0, h, f).wait_send()

    for j in range(len(W_CHUNKS)):

        @pl.when(z < depth - 1)
        def _():
            w_copy(0, j).wait_send()

        for kind in range(1, 4):
            w_copy(kind, j).wait_send()

    @pl.when(first < N_QKV)
    def _():
        for t in range(owned):
            tile_sends(t, "wait")


def front(tokens, rows, master, first_turned):
    seqs, span, _ = tokens.shape
    owned = master.shape[0]
    one = (owned + 1) // 2
    vm, hbm = pl.BlockSpec(memory_space=pltpu.VMEM), pl.BlockSpec(memory_space=pl.ANY)
    dma = pltpu.SemaphoreType.DMA
    chunks = len(W_CHUNKS)
    return pl.pallas_call(
        front_kernel,
        in_specs=[vm] * 3 + [hbm],
        out_specs=[hbm, vm, hbm, hbm, hbm],
        out_shape=[
            jax.ShapeDtypeStruct((4, seqs, span, D), bf16),
            jax.ShapeDtypeStruct((9 * HD, D), bf16),
            jax.ShapeDtypeStruct((4,) + first_turned.shape[1:], bf16),
            jax.ShapeDtypeStruct((4, 2, one, TILE, TILE), bf16),
            jax.ShapeDtypeStruct((8, owned - one, TILE, TILE), bf16),
        ],
        scratch_shapes=[
            pltpu.VMEM((seqs, span, D), bf16),
            pltpu.VMEM((owned, TILE, TILE), bf16),
            pltpu.VMEM((owned, TILE, TILE), bf16),
            pltpu.VMEM((W_SLOTS, TILE, TILE), bf16),
            dma((3, X_CHUNKS)),
            dma((3, X_CHUNKS)),
            dma((X_CHUNKS,)),
            dma((owned, 2)),
            dma((chunks,)),
            dma((4, chunks)),
            dma((4, chunks)),
            dma((2,)),
            dma((2,)),
            dma((2,)),
            dma((2, 3, 2)),
            dma((2, 3, 2)),
            dma((2,)),
            dma((4,)),
        ],
        compiler_params=pltpu.CompilerParams(
            collective_id=3, has_side_effects=True, vmem_limit_bytes=VMEM_LIMIT
        ),
        cost_estimate=pl.CostEstimate(
            flops=40_000_000_000, bytes_accessed=20_000_000, transcendentals=0
        ),
        name="front",
    )(tokens, rows, master, first_turned)


def attend_forward_kernel(
    heads,
    len_ref,
    fresh_ref,
    x_ref,
    w_ref,
    qb_ref,
    vb_ref,
    fv_ref,
    o_ref,
    q_ref,
    k_ref,
    v_ref,
    lse_ref,
    k_heads,
    q_wide,
    values,
    acc,
    top,
    fades,
    probs,
):
    blocks, _, span, width_in = x_ref.shape
    count = blocks * span
    length = len_ref[pl.program_id(0)]
    x = x_ref[...].reshape(count, width_in)
    width = heads * HD
    q_ref[0] = (dot(w_ref[0:width, :], x, NT) + qb_ref[...]).astype(bf16)
    keys = dot(x, w_ref[width : 2 * width, :], NT).astype(bf16)
    k_ref[0] = keys.T
    dead = lax.broadcasted_iota(jnp.int32, (count, 1), 0) >= length
    bias = jnp.broadcast_to(jnp.where(dead, masked_score, 0.0).astype(bf16), (count, 16))
    ones = (lax.broadcasted_iota(jnp.int32, (16, count), 0) == 0).astype(f32).astype(bf16)
    for h in range(heads):
        k_heads[h, :, 0:HD] = keys[:, h * HD : (h + 1) * HD]
        k_heads[h, :, HD : HD + 16] = bias
        q_wide[h, 0:HD] = q_ref[0, h * HD : (h + 1) * HD, :]
        q_wide[h, HD : HD + 16] = ones

    @pl.when(fresh_ref[0] == 1)
    def _():
        v_ref[0] = (dot(w_ref[2 * width :, :], x, NT) + vb_ref[...]).astype(bf16)

    @pl.when(fresh_ref[0] == 0)
    def _():
        for b in range(blocks):
            v_ref[0, :, b * span : (b + 1) * span] = fv_ref[b, 0]

    for h in range(heads):
        values[h, 0:HD] = v_ref[0, h * HD : (h + 1) * HD, :]
        values[h, HD : HD + 16] = ones
    bq, bk = QUERY_BLOCK, KEY_BLOCK

    def one_query_block(qi, carry):
        q0 = pl.multiple_of(qi * bq, bq)
        top[...] = jnp.full_like(top, masked_score)
        acc[...] = jnp.zeros_like(acc)

        def step(ki, masked, low=0, rows_here=bk):
            k0 = pl.multiple_of(ki * bk + low, HALF_BLOCK)
            skip = low if masked else 0
            for h in range(heads):
                for c0 in range(skip, bq, STRIPE):
                    cols = slice(c0, c0 + STRIPE)
                    at = pl.ds(pl.multiple_of(q0 + c0, TILE), STRIPE)
                    parts = []
                    for r0 in range(0, rows_here, HALF_BLOCK):
                        keys = pl.ds(pl.multiple_of(k0 + r0, HALF_BLOCK), HALF_BLOCK)
                        s = dot(k_heads[h, keys, :], q_wide[h, :, at])
                        if masked and c0 - low - r0 < HALF_BLOCK:
                            shape = (HALF_BLOCK, STRIPE)
                            allowed = low + r0 + lax.broadcasted_iota(
                                jnp.int32, shape, 0
                            ) <= c0 + lax.broadcasted_iota(jnp.int32, shape, 1)
                            s = jnp.where(allowed, s, masked_score)
                        parts.append(s)
                    top_old = top[h : h + 1, cols]
                    top_new = top_old
                    for s in parts:
                        top_new = jnp.maximum(top_new, jnp.max(s, axis=0, keepdims=True))
                    top[h : h + 1, cols] = top_new
                    fades[h : h + 1, cols] = jnp.exp2((top_old - top_new) * (SCALE * LOG2E))
                    for part, s in enumerate(parts):
                        probs[h, part * HALF_BLOCK : (part + 1) * HALF_BLOCK, cols] = jnp.exp2(
                            (s - top_new) * (SCALE * LOG2E)
                        ).astype(bf16)
            wide = slice(skip, bq)
            for h in range(heads):
                acc[h, :, wide] = acc[h, :, wide] * fades[h : h + 1, wide] + dot(
                    values[h, :, pl.ds(k0, rows_here)], probs[h, 0:rows_here, wide]
                )

        lax.fori_loop(
            0, jnp.minimum(qi, (length + bk - 1) // bk), lambda i, c: (step(i, False), c)[1], 0
        )

        @pl.when(q0 < length)
        def _():
            step(qi, True, 0, HALF_BLOCK)
            step(qi, True, HALF_BLOCK, HALF_BLOCK)

        for h in range(heads):
            rows = slice(h * HD, (h + 1) * HD)
            sums = acc[h, HD : HD + 1, :]
            o_ref[qi, 0, rows, :] = (acc[h, 0:HD, :] / sums).astype(bf16)
            lse_ref[0, h : h + 1, pl.ds(q0, bq)] = (
                top[h : h + 1, :] * (SCALE * LOG2E) + jnp.log2(sums)
            )
        return carry

    lax.fori_loop(0, count // bq, one_query_block, 0)


def attend_forward(lengths, fresh, x, w, qb, vb, fv):
    blocks, seqs, span, _ = x.shape
    width = w.shape[0] // 3
    heads = width // HD
    count = blocks * span
    one = lambda shape: pl.BlockSpec((1,) + shape, lambda i, *_: (i,) + (0,) * len(shape))
    mid = lambda shape: pl.BlockSpec((blocks, 1) + shape, lambda i, *_: (0, i, 0, 0))
    return pl.pallas_call(
        functools.partial(attend_forward_kernel, heads),
        grid_spec=pltpu.PrefetchScalarGridSpec(
            num_scalar_prefetch=2,
            grid=(seqs,),
            in_specs=[mid((span, D))]
            + [whole((3 * width, D))]
            + [whole((width, 1))] * 2
            + [mid((width, span))],
            out_specs=[
                mid((width, span)),
                one((width, count)),
                one((width, count)),
                one((width, count)),
                one((8, count)),
            ],
            scratch_shapes=[
                pltpu.VMEM((heads, count, HD + 16), bf16),
                pltpu.VMEM((heads, HD + 16, count), bf16),
                pltpu.VMEM((heads, HD + 16, count), bf16),
                pltpu.VMEM((heads, HD + 16, QUERY_BLOCK), f32),
                pltpu.VMEM((8, QUERY_BLOCK), f32),
                pltpu.VMEM((8, QUERY_BLOCK), f32),
                pltpu.VMEM((heads, KEY_BLOCK, QUERY_BLOCK), bf16),
            ],
        ),
        out_shape=[
            jax.ShapeDtypeStruct((blocks, seqs, width, span), bf16),
            jax.ShapeDtypeStruct((seqs, width, count), bf16),
            jax.ShapeDtypeStruct((seqs, width, count), bf16),
            jax.ShapeDtypeStruct((seqs, width, count), bf16),
            jax.ShapeDtypeStruct((seqs, 8, count), f32),
        ],
        compiler_params=params(),
        cost_estimate=pl.CostEstimate(
            flops=40_000_000_000, bytes_accessed=20_000_000, transcendentals=0
        ),
        name="attend_forward",
    )(lengths, fresh, x, w, qb, vb, fv)


def attend_backward_kernel(
    heads,
    len_ref,
    fresh_ref,
    group_ref,
    q_ref,
    k_ref,
    v_ref,
    o_ref,
    g_ref,
    lse_ref,
    x_ref,
    w_ref,
    all_in_ref,
    dx_ref,
    dv_ref,
    all_ref,
    db_ref,
    dw_ref,
    tiles,
    sem,
    k_heads,
    v_heads,
    q_heads,
    g_heads,
    k_turned,
    g_turned,
    dq_acc,
    delta,
    grads,
    dk_acc,
    dv_acc,
):
    n = pl.program_id(0)
    blocks, _, span, width_in = x_ref.shape
    count = blocks * span
    width = heads * HD
    length = len_ref[n]
    bq, bk = BACK_QUERY_BLOCK, BACK_KEY_BLOCK
    delta[...] = jnp.zeros_like(delta)
    for h in range(heads):
        rows = slice(h * HD, (h + 1) * HD)
        k_heads[h] = k_ref[0, rows, :].T
        v_heads[h] = v_ref[0, rows, :].T
        q_heads[h] = q_ref[0, rows, :].T
    for b in range(blocks):
        at = slice(b * span, (b + 1) * span)
        g_block = g_ref[b, 0]
        g_turned[:, at] = g_block
        product = o_ref[b, 0].astype(f32) * g_block.astype(f32)
        for h in range(heads):
            rows = slice(h * HD, (h + 1) * HD)
            g_heads[h, at, :] = g_block[rows, :].T
            delta[h : h + 1, at] = jnp.sum(product[rows, :], axis=0, keepdims=True)
    k_turned[...] = k_ref[0]
    dq_acc[...] = jnp.zeros_like(dq_acc)
    grads[...] = jnp.zeros_like(grads)
    key_blocks = (length + bk - 1) // bk
    query_blocks = (length + bq - 1) // bq

    def one_key_block(ki, carry):
        k0 = pl.multiple_of(ki * bk, bk)
        dk_acc[...] = jnp.zeros_like(dk_acc)
        dv_acc[...] = jnp.zeros_like(dv_acc)

        def step(qi, masked):
            q0 = pl.multiple_of(qi * bq, bq)
            at = pl.ds(q0, bq)
            if masked:
                key_pos = k0 + lax.broadcasted_iota(jnp.int32, (bk, bq), 0)
                query_pos = q0 + lax.broadcasted_iota(jnp.int32, (bk, bq), 1)
                allowed = (key_pos <= query_pos) & (key_pos < length)
            for h in range(heads):
                rows = slice(h * HD, (h + 1) * HD)
                s = dot(k_heads[h, pl.ds(k0, bk), :], q_ref[0, rows, at])
                dp = dot(v_heads[h, pl.ds(k0, bk), :], g_turned[rows, at])
                p = jnp.exp2(s * (SCALE * LOG2E) - lse_ref[0, h : h + 1, at])
                if masked:
                    p = jnp.where(allowed, p, 0.0)
                ds = (p * (dp - delta[h : h + 1, at])).astype(bf16)
                dv_acc[h] = dv_acc[h] + dot(p.astype(bf16), g_heads[h, at, :])
                dk_acc[h] = dk_acc[h] + dot(ds, q_heads[h, at, :])
                dq_acc[rows, at] = dq_acc[rows, at] + dot(k_turned[rows, pl.ds(k0, bk)], ds)

        first = k0 // bq
        plain = jnp.where(k0 + bk <= length, (k0 + bk + bq - 1) // bq, query_blocks)
        plain = jnp.minimum(plain, query_blocks)
        lax.fori_loop(first, plain, lambda i, c: (step(i, True), c)[1], 0)
        lax.fori_loop(plain, query_blocks, lambda i, c: (step(i, False), c)[1], 0)
        for h in range(heads):
            grads[pl.ds(k0, bk), width + h * HD : width + (h + 1) * HD] = (
                dk_acc[h] * SCALE
            ).astype(bf16)
            grads[pl.ds(k0, bk), 2 * width + h * HD : 2 * width + (h + 1) * HD] = dv_acc[h].astype(
                bf16
            )
        return carry

    lax.fori_loop(0, key_blocks, one_key_block, 0)
    grads[:, 0:width] = (dq_acc[...] * SCALE).astype(bf16).T
    for b in range(blocks):
        dv_ref[b, 0] = grads[b * span : (b + 1) * span, 2 * width : 3 * width].T

    @pl.when(fresh_ref[0] == 0)
    def _():
        grads[:, 2 * width : 3 * width] = jnp.zeros((count, width), bf16)

    dx_ref[...] = dot(grads[...], w_ref[...]).astype(bf16).reshape(dx_ref.shape)
    dw = dot(grads[...], x_ref[...].reshape(count, width_in), TN)
    db = jnp.sum(grads[...].astype(f32), axis=0, keepdims=True)

    @pl.when(n == 0)
    def _():
        dw_ref[...] = dw
        db_ref[...] = db

    @pl.when(n > 0)
    def _():
        dw_ref[...] += dw
        db_ref[...] += db

    @pl.when(n == pl.num_programs(0) - 1)
    def _():
        tiles[...] = jnp.zeros_like(tiles)
        for which, (start, per_row) in enumerate(
            ((0, D // TILE), (N_OUT, D // TILE), (2 * N_OUT, VW // TILE))
        ):

            def put(group):
                for piece in range(heads):
                    unit = group * heads + piece
                    rows = pl.ds(pl.multiple_of((unit % 2) * HD, HD), HD)
                    at = which * width + piece * HD
                    for r in range(D // TILE):
                        tiles[start + r * per_row + unit // 2, rows, :] = dw_ref[
                            at : at + HD, r * TILE : (r + 1) * TILE
                        ].astype(bf16)

            if which < 2:
                put(group_ref[0])
            else:
                pl.when(fresh_ref[0] == 1)(lambda: put(group_ref[0]))
        copy = pltpu.make_async_copy(tiles, all_ref.at[pl.ds(0, N_QKV)], sem.at[0])
        copy.start()
        copy.wait()


def attend_backward(lengths, fresh, group, q, k, v, o, g, lse, x, w, all_tiles):
    blocks, seqs, span, _ = x.shape
    width = q.shape[1]
    heads = width // HD
    count = blocks * span
    one = lambda shape: pl.BlockSpec((1,) + shape, lambda i, *_: (i,) + (0,) * len(shape))
    mid = lambda shape: pl.BlockSpec((blocks, 1) + shape, lambda i, *_: (0, i, 0, 0))
    return pl.pallas_call(
        functools.partial(attend_backward_kernel, heads),
        grid_spec=pltpu.PrefetchScalarGridSpec(
            num_scalar_prefetch=3,
            grid=(seqs,),
            in_specs=[
                one((width, count)),
                one((width, count)),
                one((width, count)),
                mid((width, span)),
                mid((width, span)),
                one((8, count)),
                mid((span, D)),
                whole((3 * width, D)),
                pl.BlockSpec(memory_space=pl.ANY),
            ],
            out_specs=[
                mid((span, D)),
                mid((width, span)),
                pl.BlockSpec(memory_space=pl.ANY),
                whole((1, 3 * width)),
            ],
            scratch_shapes=[
                pltpu.VMEM((3 * width, D), f32),
                pltpu.VMEM((N_QKV, TILE, TILE), bf16),
                pltpu.SemaphoreType.DMA((1,)),
            ]
            + [pltpu.VMEM((heads, count, HD), bf16)] * 4
            + [
                pltpu.VMEM((width, count), bf16),
                pltpu.VMEM((width, count), bf16),
                pltpu.VMEM((width, count), f32),
                pltpu.VMEM((8, count), f32),
                pltpu.VMEM((count, 3 * width), bf16),
                pltpu.VMEM((heads, BACK_KEY_BLOCK, HD), f32),
                pltpu.VMEM((heads, BACK_KEY_BLOCK, HD), f32),
            ],
        ),
        out_shape=[
            jax.ShapeDtypeStruct((blocks, seqs, span, D), bf16),
            jax.ShapeDtypeStruct((blocks, seqs, width, span), bf16),
            jax.ShapeDtypeStruct(all_tiles.shape, bf16),
            jax.ShapeDtypeStruct((1, 3 * width), f32),
        ],
        input_output_aliases={11: 2},
        compiler_params=params(),
        cost_estimate=pl.CostEstimate(
            flops=70_000_000_000, bytes_accessed=25_000_000, transcendentals=0
        ),
        name="attend_backward",
    )(lengths, fresh, group, q, k, v, o, g, lse, x, w, all_tiles)


HIDDEN_CHUNK = 1024
GELU_A = 0.7978845608028654
GELU_B = 0.044715


def feed_forward_kernel(
    part_count,
    len_ref,
    pos_ref,
    att_ref,
    tok_ref,
    cot_ref,
    rows_ref,
    hb_ref,
    *rest,
):
    sources, rest = rest[:part_count], rest[part_count:]
    feed_forward_body(
        len_ref, pos_ref, att_ref, tok_ref, cot_ref, rows_ref, hb_ref, sources, *rest
    )


def feed_forward_body(
    len_ref,
    pos_ref,
    att_ref,
    tok_ref,
    cot_ref,
    rows_ref,
    hb_ref,
    sources,
    out_ref,
    rg_ref,
    ag_ref,
    act_ref,
    hg_ref,
    nt_ref,
    bg_ref,
    og_ref,
    sums_ref,
    hsum_ref,
    tiles,
    w_out,
    w_hidden,
    w_proj,
    output_acc,
    sem,
):
    n = pl.program_id(0)
    span = tok_ref.shape[1]

    @pl.when(n == 0)
    def _():
        if len(sources) == 1:
            skipped = N_QKV
            copies = [
                pltpu.make_async_copy(
                    sources[0].at[pl.ds(N_QKV, N_REST)], tiles, sem.at[0]
                )
            ]
        else:
            skipped = 0
            dp, s = lax.axis_index("dp"), lax.axis_index("seq")
            y, x, core = dp % 2, s // 2, s % 2
            one = sources[0].shape[2]
            owned = tiles.shape[0] // 32
            spread = tiles.reshape(4, 2, 2, 2, owned, TILE, TILE)
            copies = []
            for c in range(2):
                at_core = core if c == 0 else 1 - core
                for other in range(2):
                    at_y = y if other == 0 else 1 - y
                    at_x = x if other == 0 else 1 - x
                    copies.append(
                        pltpu.make_async_copy(
                            sources[c * 4 + other],
                            spread.at[:, at_y, :, at_core, pl.ds(0, one)],
                            sem.at[c * 4 + other],
                        )
                    )
                    source = sources[c * 4 + 2 + other]
                    copies.append(
                        pltpu.make_async_copy(
                            source.reshape(4, 2, owned - one, TILE, TILE),
                            spread.at[:, :, at_x, at_core, pl.ds(one, owned - one)],
                            sem.at[c * 4 + 2 + other],
                        )
                    )
        for copy in copies:
            copy.start()
        for copy in copies:
            copy.wait()
        for start, matrix in zip((0, N_OUT, N_OUT + N_HID), (w_out, w_hidden, w_proj)):
            start = start + N_QKV - skipped
            row_tiles, col_tiles = matrix.shape[0] // TILE, matrix.shape[1] // TILE

            def place(r, carry):
                at = pl.ds(pl.multiple_of(r * TILE, TILE), TILE)
                for c in range(col_tiles):
                    matrix[at, c * TILE : (c + 1) * TILE] = tiles[start + r * col_tiles + c]
                return carry

            lax.fori_loop(0, row_tiles, place, 0)
        sums_ref[...] = jnp.zeros_like(sums_ref)
        hsum_ref[...] = jnp.zeros_like(hsum_ref)

    gain_two, shift_two = rows_ref[0:1, :], rows_ref[1:2, :]
    out_bias, proj_bias = rows_ref[2:3, :], rows_ref[3:4, :]
    attended = att_ref[...].reshape(D, span)
    residual = tok_ref[0].astype(f32) + dot(attended, w_out[...], TN) + out_bias
    normed, unit, inv = norm_forward(residual, gain_two, shift_two)
    normed = normed.astype(bf16)
    nt_ref[...] = normed
    live = pos_ref[0] + lax.broadcasted_iota(jnp.int32, (span, 1), 0) < len_ref[n]
    out_grad = jnp.where(live, cot_ref[0].astype(f32), 0.0)
    out_grad_low = out_grad.astype(bf16)
    og_ref[...] = out_grad_low
    output_acc[...] = residual + proj_bias
    rg_ref[0] = jnp.zeros((span, D), f32)

    def chunk(c, carry):
        cols = pl.ds(pl.multiple_of(c * HIDDEN_CHUNK, HIDDEN_CHUNK), HIDDEN_CHUNK)
        hidden = dot(nt_ref[...], w_hidden[:, cols]) + hb_ref[:, cols]
        square = hidden * hidden
        bend = jnp.tanh(GELU_A * (hidden + GELU_B * (hidden * square)))
        active = (0.5 * hidden * (1.0 + bend)).astype(bf16)
        slope = 0.5 * (1.0 + bend) + 0.5 * hidden * (1.0 - bend * bend) * (
            GELU_A * (1.0 + (3.0 * GELU_B) * square)
        )
        act_ref[:, cols] = active
        hidden_grad = (dot(og_ref[...], w_proj[cols, :], NT) * slope).astype(bf16)
        hg_ref[:, cols] = hidden_grad
        hsum_ref[:, cols] += jnp.sum(hidden_grad.astype(f32), axis=0, keepdims=True)
        output_acc[...] += dot(active, w_proj[cols, :])
        rg_ref[0] += dot(hidden_grad, w_hidden[:, cols], NT)
        return carry

    lax.fori_loop(0, FF // HIDDEN_CHUNK, chunk, 0)
    out_ref[0] = output_acc[...].astype(bf16)
    norm_in = rg_ref[0]
    residual_grad = out_grad + norm_backward(norm_in, unit, inv, gain_two)
    rg_ref[0] = residual_grad
    branch = residual_grad.astype(bf16)
    bg_ref[...] = branch
    ag_ref[...] = dot(w_out[...], branch, NT).astype(bf16).reshape(ag_ref.shape)
    sums_ref[0:1, :] += jnp.sum(norm_in * unit, axis=0, keepdims=True)
    sums_ref[1:2, :] += jnp.sum(norm_in, axis=0, keepdims=True)
    sums_ref[2:3, :] += jnp.sum(branch.astype(f32), axis=0, keepdims=True)
    sums_ref[3:4, :] += jnp.sum(out_grad, axis=0, keepdims=True)


def feed_forward(lengths, position, att, tokens, cotangent, sources, total_tiles, rows, hidden_bias):
    groups, seqs, width, span = att.shape
    one = lambda shape: pl.BlockSpec((1,) + shape, lambda i, *_: (i,) + (0,) * len(shape))
    mid = lambda shape: pl.BlockSpec((groups, 1) + shape, lambda i, *_: (0, i, 0, 0))
    row = lambda cols: pl.BlockSpec((span, cols), lambda i, *_: (i, 0))
    single = pl.BlockSpec(
        (1, span, D), lambda i, *_: (i, 0, 0), pipeline_mode=pl.Buffered(1)
    )
    total = seqs * span
    return pl.pallas_call(
        functools.partial(feed_forward_kernel, len(sources)),
        grid_spec=pltpu.PrefetchScalarGridSpec(
            num_scalar_prefetch=2,
            grid=(seqs,),
            in_specs=[
                pl.BlockSpec(
                    (groups, 1, width, span),
                    lambda i, *_: (0, i, 0, 0),
                    pipeline_mode=pl.Buffered(1),
                ),
                single,
                single,
                whole((8, D)),
                whole((1, FF)),
            ]
            + [pl.BlockSpec(memory_space=pl.ANY)] * len(sources),
            out_specs=[
                one((span, D)),
                one((span, D)),
                mid((width, span)),
                row(FF),
                row(FF),
                row(D),
                row(D),
                row(D),
                whole((8, D)),
                whole((1, FF)),
            ],
            scratch_shapes=[
                pltpu.VMEM((N_REST if len(sources) == 1 else total_tiles, TILE, TILE), bf16),
                pltpu.VMEM((D, D), bf16),
                pltpu.VMEM((D, FF), bf16),
                pltpu.VMEM((FF, D), bf16),
                pltpu.VMEM((span, D), f32),
                pltpu.SemaphoreType.DMA((8,)),
            ],
        ),
        out_shape=[
            jax.ShapeDtypeStruct((seqs, span, D), bf16),
            jax.ShapeDtypeStruct((seqs, span, D), f32),
            jax.ShapeDtypeStruct((groups, seqs, width, span), bf16),
            jax.ShapeDtypeStruct((total, FF), bf16),
            jax.ShapeDtypeStruct((total, FF), bf16),
            jax.ShapeDtypeStruct((total, D), bf16),
            jax.ShapeDtypeStruct((total, D), bf16),
            jax.ShapeDtypeStruct((total, D), bf16),
            jax.ShapeDtypeStruct((8, D), f32),
            jax.ShapeDtypeStruct((1, FF), f32),
        ],
        compiler_params=params(),
        cost_estimate=pl.CostEstimate(
            flops=24_000_000_000, bytes_accessed=40_000_000, transcendentals=0
        ),
        name="feed_forward",
    )(lengths, position, att, tokens, cotangent, rows, hidden_bias, *sources)


GRAD_CHUNK = 256


def weight_grad_kernel(
    att_ref,
    bg_ref,
    og_ref,
    nt_ref,
    act_ref,
    hg_ref,
    all_ref,
    out_tiles,
    hid_tiles,
    proj_tiles,
    og_turned,
    nt_turned,
    sem,
    out_sem,
):
    i = pl.program_id(0)
    last = pl.num_programs(0) - 1
    groups, seqs, width, span = att_ref.shape
    d_tiles, f_tiles, per = D // TILE, FF // TILE, GRAD_CHUNK // TILE
    spare = all_ref.shape[0] - N_QKV - N_REST
    slot = lax.rem(i, 2)

    def first_copies():
        copies = [
            pltpu.make_async_copy(
                out_tiles.at[pl.ds(0, N_OUT)], all_ref.at[pl.ds(N_QKV, N_OUT)], out_sem.at[0]
            )
        ]
        if spare:
            copies.append(
                pltpu.make_async_copy(
                    out_tiles.at[pl.ds(N_OUT, spare)],
                    all_ref.at[pl.ds(N_QKV + N_REST, spare)],
                    out_sem.at[1],
                )
            )
        return copies

    def copies_of(step, slot):
        made = [
            pltpu.make_async_copy(
                hid_tiles.at[slot, r],
                all_ref.at[pl.ds(N_QKV + N_OUT + r * f_tiles + step * per, per)],
                sem.at[slot, r],
            )
            for r in range(d_tiles)
        ]
        made.append(
            pltpu.make_async_copy(
                proj_tiles.at[slot],
                all_ref.at[pl.ds(FIRST_PROJ + step * per * d_tiles, per * d_tiles)],
                sem.at[slot, d_tiles],
            )
        )
        return made

    @pl.when(i == 0)
    def _():
        og_turned[...] = og_ref[...].T
        nt_turned[...] = nt_ref[...].T
        total = jnp.zeros((D, D), f32)
        for s in range(seqs):
            total = total + dot(
                att_ref[:, s].reshape(groups * width, span), bg_ref[s * span : (s + 1) * span, :]
            )
        total = total.astype(bf16)
        for r in range(d_tiles):
            for c in range(d_tiles):
                out_tiles[r * d_tiles + c] = total[
                    r * TILE : (r + 1) * TILE, c * TILE : (c + 1) * TILE
                ]
        if spare:
            out_tiles[N_OUT : N_OUT + spare] = jnp.zeros((spare, TILE, TILE), bf16)
        for copy in first_copies():
            copy.start()

    proj = dot(og_turned[...], act_ref[...]).astype(bf16)
    hid = dot(nt_turned[...], hg_ref[...]).astype(bf16)

    @pl.when(i >= 2)
    def _():
        for copy in copies_of(i - 2, slot):
            copy.wait()

    for c in range(per):
        for r in range(d_tiles):
            rows, cols = slice(r * TILE, (r + 1) * TILE), slice(c * TILE, (c + 1) * TILE)
            proj_tiles[slot, c * d_tiles + r] = proj[rows, cols]
            hid_tiles[slot, r, c] = hid[rows, cols]
    for copy in copies_of(i, slot):
        copy.start()

    @pl.when(i == last)
    def _():
        for copy in copies_of(i - 1, 1 - slot):
            copy.wait()
        for copy in copies_of(i, slot):
            copy.wait()
        for copy in first_copies():
            copy.wait()


def weight_grads(total_tiles, att, bg, og, nt, act, hg):
    total = bg.shape[0]
    chunks = FF // GRAD_CHUNK
    per = GRAD_CHUNK // TILE
    spare = total_tiles - N_QKV - N_REST
    return pl.pallas_call(
        weight_grad_kernel,
        grid=(chunks,),
        in_specs=[
            whole(att.shape),
            whole(bg.shape),
            whole(og.shape),
            whole(nt.shape),
            pl.BlockSpec((total, GRAD_CHUNK), lambda i: (0, i)),
            pl.BlockSpec((total, GRAD_CHUNK), lambda i: (0, i)),
        ],
        out_specs=pl.BlockSpec(memory_space=pl.ANY),
        out_shape=jax.ShapeDtypeStruct((total_tiles, TILE, TILE), bf16),
        scratch_shapes=[
            pltpu.VMEM((N_OUT + spare, TILE, TILE), bf16),
            pltpu.VMEM((2, D // TILE, per, TILE, TILE), bf16),
            pltpu.VMEM((2, per * (D // TILE), TILE, TILE), bf16),
            pltpu.VMEM((D, total), bf16),
            pltpu.VMEM((D, total), bf16),
            pltpu.SemaphoreType.DMA((2, D // TILE + 1)),
            pltpu.SemaphoreType.DMA((2,)),
        ],
        compiler_params=params(),
        cost_estimate=pl.CostEstimate(
            flops=12_000_000_000, bytes_accessed=40_000_000, transcendentals=0
        ),
        name="weight_grads",
    )(att, bg, og, nt, act, hg)


def bits_of(size):
    return size.bit_length() - 1


def exchange_bits(dp, seq):
    return (
        [("seq", 0)]
        + [("dp", b) for b in range(bits_of(dp))]
        + [("seq", b) for b in range(1, bits_of(seq))]
    )


def partner_of(axis, bit):
    here = {"dp": lax.axis_index("dp"), "seq": lax.axis_index("seq")}
    side = (here[axis] // (1 << bit)) % 2
    here[axis] = here[axis] + (1 << bit) * (1 - 2 * side)
    return (here["dp"], here["seq"]), side


def greet(partners):
    barrier = pltpu.get_barrier_semaphore()
    for device in partners:
        pl.semaphore_signal(barrier, inc=1, device_id=device, device_id_type=MESH)
    pl.semaphore_wait(barrier, len(partners))


def tile_sum_kernel(stages, chunks, g_ref, out_ref, mine, *rest):
    count = len(stages)
    received = rest[:count]
    send_sem, recv_sem, copy_sem = rest[count:]
    partners = [partner_of(axis, bit) for axis, bit, _, _ in stages]
    greet([device for device, _ in partners])

    def view(ref, above, below):
        return ref.reshape(above, 2, below, *ref.shape[-3:])

    def send(stage, k):
        _, _, above, below = stages[stage]
        device, side = partners[stage]
        source = g_ref if stage == 0 else received[stage - 1]
        at = pl.ds(*chunks[k])
        return pltpu.make_async_remote_copy(
            src_ref=view(source, above, below).at[:, 1 - side, :, at],
            dst_ref=received[stage].reshape(above, below, *received[stage].shape[-3:]).at[:, :, at],
            send_sem=send_sem.at[stage, k],
            recv_sem=recv_sem.at[stage, k],
            device_id=device,
            device_id_type=MESH,
        )

    def own(k):
        _, _, above, below = stages[0]
        at = pl.ds(*chunks[k])
        return pltpu.make_async_copy(
            view(g_ref, above, below).at[:, partners[0][1], :, at],
            mine.reshape(above, below, *mine.shape[-3:]).at[:, :, at],
            copy_sem.at[k],
        )

    for k in range(len(chunks)):
        send(0, k).start()
        own(k).start()
    for step in range(1, len(chunks) + count):
        for k in range(len(chunks)):
            stage = step - k
            if not 1 <= stage <= count:
                continue
            send(stage - 1, k).wait_recv()
            _, _, above, below = stages[stage - 1]
            side = partners[stage - 1][1]
            at = pl.ds(*chunks[k])
            if stage == 1:
                own(k).wait()

            def add(i, carry):
                if stage == 1:
                    kept = mine[i, at]
                else:
                    up, low = i // below, i % below
                    kept = received[stage - 2][(up * 2 + side) * below + low, at]
                total = kept.astype(f32) + received[stage - 1][i, at].astype(f32)
                if stage == count:
                    out_ref[at] = total
                else:
                    received[stage - 1][i, at] = total.astype(bf16)
                return carry

            lax.fori_loop(0, above * below, add, 0)
            if stage < count:
                send(stage, k).start()
    for stage in range(count):
        for k in range(len(chunks)):
            send(stage, k).wait_send()


def tile_sum(g, dp, seq):
    devices = dp * seq
    owned = g.shape[0] // devices
    tail = (owned, TILE, TILE)
    left = [("dp", b) for b in reversed(range(bits_of(dp)))] + [
        ("seq", b) for b in reversed(range(bits_of(seq)))
    ]
    stages = []
    for axis, bit in exchange_bits(dp, seq):
        place = left.index((axis, bit))
        stages.append((axis, bit, 1 << place, 1 << (len(left) - 1 - place)))
        left.pop(place)
    pieces = min(4, owned)
    edges = [owned * p // pieces for p in range(pieces + 1)]
    chunks = [(low, high - low) for low, high in zip(edges, edges[1:])]
    buffers = [
        pltpu.VMEM((devices >> (i + 1),) + tail, bf16) for i in range(len(stages))
    ]
    return pl.pallas_call(
        functools.partial(tile_sum_kernel, stages, chunks),
        in_specs=[pl.BlockSpec(memory_space=pl.ANY)],
        out_specs=pl.BlockSpec(memory_space=pltpu.VMEM),
        out_shape=jax.ShapeDtypeStruct(tail, f32),
        scratch_shapes=[pltpu.VMEM((devices // 2,) + tail, bf16)]
        + buffers
        + [
            pltpu.SemaphoreType.DMA((len(stages), len(chunks))),
            pltpu.SemaphoreType.DMA((len(stages), len(chunks))),
            pltpu.SemaphoreType.DMA((len(chunks),)),
        ],
        compiler_params=pltpu.CompilerParams(
            collective_id=1, has_side_effects=True, vmem_limit_bytes=VMEM_LIMIT
        ),
        cost_estimate=pl.CostEstimate(
            flops=60_000_000_000, bytes_accessed=40_000_000, transcendentals=0
        ),
        name="tile_sum",
    )(g.reshape((devices,) + tail))


AXIS_BITS = {
    "far": ("dp", 2),
    "near": ("dp", 1),
    "y": ("dp", 0),
    "x": ("seq", 1),
    "core": ("seq", 0),
}
ADDRESS = ("far", "near", "y", "x")
FLOW_ORDERS = (("y", "near", "far", "x"), ("near", "x", "y", "far"), ("x", "y", "near", "far"))
HALF = TILE // 2


def flow_stages(order):
    left = list(ADDRESS)
    stages = []
    for name in order:
        place = left.index(name)
        stages.append((name, 1 << place, 1 << (len(left) - 1 - place)))
        left.pop(place)
    return stages


def paired_grad_kernel(
    att_ref,
    bg_ref,
    og_ref,
    nt_ref,
    act_ref,
    hg_ref,
    half_ref,
    made,
    landed,
    done,
    out_made,
    out_landed,
    out_done,
    zeros,
    og_turned,
    nt_turned,
    send_sem,
    recv_sem,
    done_sem,
    out_sem,
    zero_sem,
):
    i = pl.program_id(0)
    last = pl.num_programs(0) - 1
    groups, seqs, width, span = att_ref.shape
    d_tiles, f_tiles, per = D // TILE, FF // TILE, GRAD_CHUNK // TILE
    count = per * d_tiles
    spare = half_ref.shape[0] - N_QKV - N_REST
    sibling, core = partner_of("seq", 0)
    kept = pl.ds(pl.multiple_of(core * HALF, HALF), HALF)
    given = pl.ds(pl.multiple_of((1 - core) * HALF, HALF), HALF)
    slot = lax.rem(i, 2)

    def to_sibling(step, slot):
        return pltpu.make_async_remote_copy(
            src_ref=made.at[slot, :, given],
            dst_ref=landed.at[step],
            send_sem=send_sem.at[slot],
            recv_sem=recv_sem.at[step],
            device_id=sibling,
            device_id_type=MESH,
        )

    def out_to_sibling():
        return pltpu.make_async_remote_copy(
            src_ref=out_made.at[:, given],
            dst_ref=out_landed,
            send_sem=out_sem.at[0],
            recv_sem=out_sem.at[1],
            device_id=sibling,
            device_id_type=MESH,
        )

    def out_copy():
        return pltpu.make_async_copy(out_done, half_ref.at[pl.ds(N_QKV, N_OUT)], out_sem.at[2])

    def zero_copies():
        spots = [(N_QKV // 3 * j, N_QKV // 3) for j in range(3)]
        if spare:
            spots.append((N_QKV + N_REST, spare))
        return [
            pltpu.make_async_copy(
                zeros.at[pl.ds(0, size)], half_ref.at[pl.ds(low, size)], zero_sem.at[j]
            )
            for j, (low, size) in enumerate(spots)
        ]

    def done_copies(step, slot):
        copies = [
            pltpu.make_async_copy(
                done.at[slot, pl.ds(r * per, per)],
                half_ref.at[pl.ds(N_QKV + N_OUT + r * f_tiles + step * per, per)],
                done_sem.at[slot, r],
            )
            for r in range(d_tiles)
        ]
        copies.append(
            pltpu.make_async_copy(
                done.at[slot, pl.ds(count, count)],
                half_ref.at[pl.ds(FIRST_PROJ + step * count, count)],
                done_sem.at[slot, d_tiles],
            )
        )
        return copies

    @pl.when(i == 0)
    def _():
        greet([sibling])
        zeros[...] = jnp.zeros_like(zeros)
        for copy in zero_copies():
            copy.start()
        total = jnp.zeros((D, D), f32)
        for s in range(seqs):
            total = total + dot(
                att_ref[:, s].reshape(groups * width, span), bg_ref[s * span : (s + 1) * span, :]
            )
        total = total.astype(bf16)
        for r in range(d_tiles):
            for c in range(d_tiles):
                out_made[r * d_tiles + c] = total[
                    r * TILE : (r + 1) * TILE, c * TILE : (c + 1) * TILE
                ]
        out_to_sibling().start()
        og_turned[...] = og_ref[...].T
        nt_turned[...] = nt_ref[...].T

    @pl.when(i < last)
    def _():
        @pl.when(i >= 2)
        def _():
            to_sibling(i - 2, slot).wait_send()

        proj = dot(og_turned[...], act_ref[...]).astype(bf16)
        hid = dot(nt_turned[...], hg_ref[...]).astype(bf16)
        for c in range(per):
            for r in range(d_tiles):
                rows, cols = slice(r * TILE, (r + 1) * TILE), slice(c * TILE, (c + 1) * TILE)
                made[slot, count + c * d_tiles + r] = proj[rows, cols]
                made[slot, r * per + c] = hid[rows, cols]
        to_sibling(i, slot).start()

    @pl.when(i >= 1)
    def _():
        before = 1 - slot

        @pl.when(i >= 3)
        def _():
            for copy in done_copies(i - 3, before):
                copy.wait()

        to_sibling(i - 1, before).wait_recv()
        done[before] = (
            made[before, :, kept].astype(f32) + landed[i - 1].astype(f32)
        ).astype(bf16)
        for copy in done_copies(i - 1, before):
            copy.start()

    @pl.when(i == 1)
    def _():
        out_to_sibling().wait_recv()
        out_done[...] = (out_made[:, kept].astype(f32) + out_landed[...].astype(f32)).astype(bf16)
        out_copy().start()

    @pl.when(i == last)
    def _():
        to_sibling(i - 2, slot).wait_send()
        to_sibling(i - 1, 1 - slot).wait_send()
        out_to_sibling().wait_send()
        out_copy().wait()
        for copy in zero_copies():
            copy.wait()
        for copy in done_copies(i - 2, slot):
            copy.wait()
        for copy in done_copies(i - 1, 1 - slot):
            copy.wait()


def paired_grads(total_tiles, att, bg, og, nt, act, hg):
    total = bg.shape[0]
    chunks = FF // GRAD_CHUNK
    per = GRAD_CHUNK // TILE
    count = per * (D // TILE)
    dma = pltpu.SemaphoreType.DMA
    column = pl.BlockSpec((total, GRAD_CHUNK), lambda i: (0, jnp.minimum(i, chunks - 1)))
    return pl.pallas_call(
        paired_grad_kernel,
        grid=(chunks + 1,),
        in_specs=[whole(a.shape) for a in (att, bg, og, nt)] + [column, column],
        out_specs=pl.BlockSpec(memory_space=pl.ANY),
        out_shape=jax.ShapeDtypeStruct((total_tiles, HALF, TILE), bf16),
        scratch_shapes=[
            pltpu.VMEM((2, 2 * count, TILE, TILE), bf16),
            pltpu.VMEM((chunks, 2 * count, HALF, TILE), bf16),
            pltpu.VMEM((2, 2 * count, HALF, TILE), bf16),
            pltpu.VMEM((N_OUT, TILE, TILE), bf16),
            pltpu.VMEM((N_OUT, HALF, TILE), bf16),
            pltpu.VMEM((N_OUT, HALF, TILE), bf16),
            pltpu.VMEM((N_QKV // 3, HALF, TILE), bf16),
            pltpu.VMEM((D, total), bf16),
            pltpu.VMEM((D, total), bf16),
            dma((2,)),
            dma((chunks,)),
            dma((2, D // TILE + 1)),
            dma((3,)),
            dma((4,)),
        ],
        compiler_params=pltpu.CompilerParams(
            dimension_semantics=("arbitrary",),
            collective_id=4,
            has_side_effects=True,
            vmem_limit_bytes=VMEM_LIMIT,
        ),
        cost_estimate=pl.CostEstimate(
            flops=12_000_000_000, bytes_accessed=40_000_000, transcendentals=0
        ),
        name="paired_grads",
    )(att, bg, og, nt, act, hg)


Q_UNITS = 27


def attend_back_sum_kernel(
    heads,
    flows,
    len_ref,
    fresh_ref,
    q_ref,
    k_ref,
    v_ref,
    o_ref,
    g_ref,
    lse_ref,
    x_ref,
    w_ref,
    half_ref,
    in_ref,
    dv_ref,
    raw_ref,
    db_ref,
    dw,
    q_wide,
    k_wide,
    g_wide,
    v_wide,
    g_turned,
    dq_acc,
    delta,
    grads,
    dk_acc,
    dv_acc,
    probs,
    score_grads,
    dxs,
    dx_core,
    dx_across,
    in_made,
    mine,
    final,
    final_other,
    q_parts,
    q_y,
    q_near,
    q_far,
    q_own,
    core_sem,
    across_sem,
    in_sem,
    own_sem,
    flow_send,
    flow_recv,
    final_sem,
    q_send,
    q_recv,
    q_out,
    q_in,
    *lands,
):
    i = pl.program_id(0)
    blocks, _, span, width_in = x_ref.shape
    count = blocks * span
    width = heads * HD
    bq, bk = BACK_QUERY_BLOCK, BACK_KEY_BLOCK
    per_seq = count // bk
    seqs = dxs.shape[0]
    n, ki = i // per_seq, i % per_seq
    length = len_ref[n]
    dp, s = lax.axis_index("dp"), lax.axis_index("seq")
    y, x, core = dp % 2, s // 2, s % 2
    near, far = (dp // 2) % 2, dp // 4
    owned = raw_ref.shape[0]
    first_tile = (dp * 4 + s) * owned
    partners = {name: partner_of(axis, bit) for name, (axis, bit) in AXIS_BITS.items()}

    def view(ref, above, below):
        return ref.reshape(above, 2, below, *ref.shape[-3:])

    def flow_send_copy(f, k):
        low, size, stages = flows[f]
        name, above, below = stages[k]
        device, side = partners[name]
        land = lands[f * 4 + k]
        if k == 0:
            source = view(half_ref, above, below).at[:, 1 - side, :, pl.ds(low, size)]
        else:
            source = view(lands[f * 4 + k - 1], above, below).at[:, 1 - side]
        return pltpu.make_async_remote_copy(
            src_ref=source,
            dst_ref=land.reshape(above, below, *land.shape[-3:]),
            send_sem=flow_send.at[f, k],
            recv_sem=flow_recv.at[f, k],
            device_id=device,
            device_id_type=MESH,
        )

    def own_copy(f):
        low, size, stages = flows[f]
        name, above, below = stages[0]
        return pltpu.make_async_copy(
            view(half_ref, above, below).at[:, partners[name][1], :, pl.ds(low, size)],
            mine.reshape(above, below, *mine.shape[-3:]).at[:, :, pl.ds(0, size)],
            own_sem.at[f],
        )

    def flow_add(f, k):
        low, size, stages = flows[f]
        name, above, below = stages[k]
        side = partners[name][1]
        land = lands[f * 4 + k]
        flow_send_copy(f, k).wait_recv()
        if k == 0:
            own_copy(f).wait()

        def add(e, carry):
            if k == 0:
                kept = mine[e, 0:size]
            else:
                kept = lands[f * 4 + k - 1][((e // below) * 2 + side) * below + e % below]
            total = kept.astype(f32) + land[e].astype(f32)
            if k == 3:
                final[low : low + size] = total
            else:
                land[e] = total.astype(bf16)
            return carry

        lax.fori_loop(0, above * below, add, 0)

    def dx_core_copy(m, block):
        return pltpu.make_async_remote_copy(
            src_ref=dxs.at[m, block],
            dst_ref=dx_core.at[m, block // 2],
            send_sem=core_sem.at[m, block // 2, 0],
            recv_sem=core_sem.at[m, block // 2, 1],
            device_id=partners["core"][0],
            device_id_type=MESH,
        )

    def dx_across_copy(m):
        return pltpu.make_async_remote_copy(
            src_ref=dx_core.at[m, 1 - x],
            dst_ref=dx_across.at[m],
            send_sem=across_sem.at[m, 0],
            recv_sem=across_sem.at[m, 1],
            device_id=partners["x"][0],
            device_id_type=MESH,
        )

    def dx_pass(m, block):
        @pl.when(block % 2 == core)
        def _():
            dx_core_copy(m, block).wait_recv()

            @pl.when(block // 2 != x)
            def _():
                dx_core[m, 1 - x] = (
                    dxs[m, block].astype(f32) + dx_core[m, 1 - x].astype(f32)
                ).astype(bf16)
                dx_across_copy(m).start()

    def dx_end(m):
        dx_across_copy(m).wait_recv()
        if m:
            in_copy(m - 1).wait()
        in_made[...] = (
            dxs[m, s].astype(f32) + dx_core[m, x].astype(f32) + dx_across[m].astype(f32)
        )
        in_copy(m).start()

    def in_copy(m):
        return pltpu.make_async_copy(in_made, in_ref.at[m], in_sem.at[m])

    @pl.when(i == 0)
    def _():
        mates = [
            (dp - y + (y + dy) % 2, (s + ds) % 4) for dy in range(2) for ds in range(4) if dy or ds
        ]
        greet(mates + [partners["near"][0], partners["far"][0]])
        for f in range(3):
            flow_send_copy(f, 0).start()
        own_copy(0).start()
        delta[...] = jnp.zeros_like(delta)
        dw[...] = jnp.zeros_like(dw)
        db_ref[...] = jnp.zeros_like(db_ref)

    @pl.when(i == per_seq - 1)
    def _():
        for f in range(3):
            flow_add(f, 0)
            if f < 2:
                own_copy(f + 1).start()
            flow_send_copy(f, 1).start()

    @pl.when(i > 0)
    def _():
        dx_pass((i - 1) // per_seq, (i - 1) % per_seq)

    @pl.when(i == per_seq + 1)
    def _():
        for f in range(3):
            flow_add(f, 1)
            flow_send_copy(f, 2).start()

    @pl.when(i == per_seq + 2)
    def _():
        for f in range(1, 3):
            flow_add(f, 2)
            flow_send_copy(f, 3).start()

    @pl.when(i == per_seq + 3)
    def _():
        flow_add(0, 2)
        flow_send_copy(0, 3).start()

    @pl.when(ki == 0)
    def _():
        row = lax.broadcasted_iota(jnp.int32, (16, count), 0)
        dead = lax.broadcasted_iota(jnp.int32, (16, count), 1) >= length
        ones = jnp.where(row < 3, 1.0, 0.0)
        key_side = jnp.where((row == 3) & dead, masked_score, ones).astype(bf16)
        ones = ones.astype(bf16)

        def in_parts(line, last):
            high = line.astype(bf16).astype(f32)
            rest = line - high
            middle = rest.astype(bf16).astype(f32)
            low = rest - middle
            parts = jnp.where(row == 0, high, jnp.where(row == 1, middle, low))
            return jnp.where(row < 3, parts, jnp.where(row == 3, last, 0.0)).astype(bf16)

        for b in range(blocks):
            at = slice(b * span, (b + 1) * span)
            g_block = g_ref[b, 0]
            g_turned[:, at] = g_block
            product = o_ref[b, 0].astype(f32) * g_block.astype(f32)
            for h in range(heads):
                rows = slice(h * HD, (h + 1) * HD)
                delta[h : h + 1, at] = jnp.sum(product[rows, :], axis=0, keepdims=True)
        for h in range(heads):
            rows = slice(h * HD, (h + 1) * HD)
            lse_part = in_parts(lse_ref[0, h : h + 1, :] * (-1.0 / (SCALE * LOG2E)), 1.0)
            delta_part = in_parts(-delta[h : h + 1, :], 0.0)
            q_wide[h] = jnp.concatenate([q_ref[0, rows, :], lse_part], axis=0).T
            g_wide[h] = jnp.concatenate([g_turned[rows, :], delta_part], axis=0).T
            k_wide[h, 0:HD] = k_ref[0, rows, :]
            k_wide[h, HD : HD + 16] = key_side
            v_wide[h, 0:HD] = v_ref[0, rows, :]
            v_wide[h, HD : HD + 16] = ones
        dq_acc[...] = jnp.zeros_like(dq_acc)

    k0 = pl.multiple_of(ki * bk, bk)
    dk_acc[...] = jnp.zeros_like(dk_acc)
    dv_acc[...] = jnp.zeros_like(dv_acc)

    def step(qi, masked, low=0, cols_here=bk):
        skip = low if masked else 0
        here = slice(low, low + cols_here)
        keys = pl.ds(pl.multiple_of(k0 + low, HALF_BLOCK), cols_here)
        at = pl.ds(pl.multiple_of(qi * bq + skip, HALF_BLOCK), bq - skip)
        tall = bq - skip
        for h in range(heads):
            rows = slice(h * HD, (h + 1) * HD)
            for c0 in range(0, cols_here, SUB_COLS):
                some = pl.ds(pl.multiple_of(k0 + low + c0, TILE), SUB_COLS)
                cols = slice(c0, c0 + SUB_COLS)
                for r0 in range(0, tall, SUB_ROWS):
                    part = pl.ds(pl.multiple_of(qi * bq + skip + r0, TILE), SUB_ROWS)
                    p = jnp.exp2(dot(q_wide[h, part, :], k_wide[h, :, some]) * (SCALE * LOG2E))
                    if masked and r0 < c0 + SUB_COLS - 1:
                        shape = (SUB_ROWS, SUB_COLS)
                        allowed = c0 + lax.broadcasted_iota(
                            jnp.int32, shape, 1
                        ) <= r0 + lax.broadcasted_iota(jnp.int32, shape, 0)
                        p = jnp.where(allowed, p, 0.0)
                    probs[h, r0 : r0 + SUB_ROWS, cols] = p.astype(bf16)
                    score_grads[h, r0 : r0 + SUB_ROWS, cols] = (
                        p * dot(g_wide[h, part, :], v_wide[h, :, some])
                    ).astype(bf16)
        for h in range(heads):
            rows = slice(h * HD, (h + 1) * HD)
            p = probs[h, 0:tall, 0:cols_here]
            ds = score_grads[h, 0:tall, 0:cols_here]
            dv_acc[rows, here] = dv_acc[rows, here] + dot(g_turned[rows, at], p)
            dk_acc[rows, here] = dk_acc[rows, here] + dot(q_ref[0, rows, at], ds)
            dq_acc[rows, at] = dq_acc[rows, at] + dot(k_ref[0, rows, keys], ds, NT)

    step(ki, True, 0, HALF_BLOCK)
    step(ki, True, HALF_BLOCK, HALF_BLOCK)
    lax.fori_loop(ki + 1, count // bq, lambda j, c: (step(j, False), c)[1], 0)
    grads[0:width, :] = (dq_acc[:, pl.ds(k0, bk)] * SCALE).astype(bf16)
    grads[width : 2 * width, :] = (dk_acc[...] * SCALE).astype(bf16)
    grads[2 * width :, :] = dv_acc[...].astype(bf16)
    dv_ref[ki, 0] = grads[2 * width :, :]

    @pl.when(x == 1)
    def _():
        grads[2 * width :, :] = jnp.zeros((width, bk), bf16)

    dw[...] += dot(grads[...], x_ref[ki, 0])
    db_ref[...] += dot(jnp.ones((8, bk), bf16), grads[...], NT)[0:1]

    def q_copy(kind, c):
        at = pl.ds(c * 9, 9)
        if kind == 0:
            source, target, name = q_parts.at[1 - y, at], q_y.at[at], "y"
        elif kind == 1:
            source, target, name = q_y.at[at], q_near.at[at], "near"
        else:
            source, target, name = q_y.at[at], q_far.at[at], "far"
        return pltpu.make_async_remote_copy(
            src_ref=source,
            dst_ref=target,
            send_sem=q_send.at[kind, c],
            recv_sem=q_recv.at[kind, c],
            device_id=partners[name][0],
            device_id_type=MESH,
        )

    def q_deliver(c, act):
        for e in range(c * 9, c * 9 + 9):
            r = 3 * y + (e // 3) % 3
            unit = core * 3 + e % 3
            if c < 2:
                index = c * N_OUT + r * (D // TILE) + 3 * x + unit // 2
            else:
                index = 2 * N_OUT + r * (VW // TILE) + unit // 2
            owner = index // owned
            target = (owner // 4, owner % 4)
            rows = pl.ds(pl.multiple_of((unit % 2) * HALF, HALF), HALF)
            here = (target[0] == dp) & (target[1] == s)
            real = (x == 0) if c == 2 else (x >= 0)
            spot = q_own.at[index % owned, rows]

            @pl.when(real & here)
            def _():
                if act == "start":
                    pltpu.make_async_copy(q_y.at[e], spot, q_in).start()

            @pl.when(real & jnp.logical_not(here))
            def _():
                copy = pltpu.make_async_remote_copy(
                    src_ref=q_y.at[e],
                    dst_ref=spot,
                    send_sem=q_out.at[e],
                    recv_sem=q_in,
                    device_id=target,
                    device_id_type=MESH,
                )
                if act == "start":
                    copy.start()
                else:
                    copy.wait_send()

    def q_add(c, extra):
        at = slice(c * 9, c * 9 + 9)
        kept = q_parts[y, at] if extra is q_y else q_y[at]
        q_y[at] = (kept.astype(f32) + extra[at].astype(f32)).astype(bf16)

    @pl.when(i == seqs * per_seq - 1)
    def _():
        for e in range(Q_UNITS):
            which, rr, piece = e // 9, (e // 3) % 3, e % 3
            at = which * width + piece * HALF
            for yy in range(2):
                r = 3 * yy + rr
                q_parts[yy, e] = dw[at : at + HALF, r * TILE : (r + 1) * TILE].astype(bf16)
        for c in range(3):
            q_copy(0, c).start()

    dxs[n, ki] = dot(grads[...], w_ref[...], TN).astype(bf16)

    @pl.when(ki % 2 != core)
    def _():
        dx_core_copy(n, ki).start()

    @pl.when(i == seqs * per_seq - 1)
    def _():
        to_sibling = pltpu.make_async_remote_copy(
            src_ref=final.at[pl.ds((1 - core) * owned, owned)],
            dst_ref=final_other,
            send_sem=final_sem.at[0],
            recv_sem=final_sem.at[1],
            device_id=partners["core"][0],
            device_id_type=MESH,
        )

        def q_first(c):
            q_copy(0, c).wait_recv()
            q_add(c, q_y)

            @pl.when(near == 1)
            def _():
                q_copy(1, c).start()

        def q_second(c):
            @pl.when(near == 0)
            def _():
                q_copy(1, c).wait_recv()
                q_add(c, q_near)

                @pl.when(far == 1)
                def _():
                    q_copy(2, c).start()

        def q_third(c):
            @pl.when((near == 0) & (far == 0))
            def _():
                q_copy(2, c).wait_recv()
                q_add(c, q_far)
                q_deliver(c, "start")

        q_first(0)
        dx_pass(seqs - 1, per_seq - 1)
        q_first(1)
        q_second(0)
        q_first(2)
        q_second(1)
        for f in range(3):
            flow_add(f, 3)
        to_sibling.start()
        q_third(0)
        q_second(2)
        q_third(1)
        dx_end(0)
        q_third(2)
        to_sibling.wait_recv()
        kept = pl.ds(pl.multiple_of(core * HALF, HALF), HALF)
        given = pl.ds(pl.multiple_of((1 - core) * HALF, HALF), HALF)
        raw_ref[:, kept, :] = final[pl.ds(core * owned, owned)]
        raw_ref[:, given, :] = final_other[...]
        for m in range(1, seqs):
            dx_end(m)

        @pl.when(first_tile + owned <= N_QKV)
        def _():
            pltpu.make_async_copy(q_own, q_own, q_in).wait()
            raw_ref[...] = q_own[...].astype(f32)

        part = N_QKV % owned
        if part:

            @pl.when((first_tile < N_QKV) & (first_tile + owned > N_QKV))
            def _():
                at = pl.ds(0, part)
                pltpu.make_async_copy(q_own.at[at], q_own.at[at], q_in).wait()
                raw_ref[0:part] = q_own[0:part].astype(f32)

        in_copy(seqs - 1).wait()
        to_sibling.wait_send()
        for m in range(seqs):
            for pair in range(2):
                dx_core_copy(m, 2 * pair + 1 - core).wait_send()
            dx_across_copy(m).wait_send()
        for f in range(3):
            for k in range(4):
                flow_send_copy(f, k).wait_send()
        for c in range(3):
            q_copy(0, c).wait_send()

            @pl.when(near == 1)
            def _():
                q_copy(1, c).wait_send()

            @pl.when((near == 0) & (far == 1))
            def _():
                q_copy(2, c).wait_send()

            @pl.when((near == 0) & (far == 0))
            def _():
                q_deliver(c, "wait")


def attend_back_sum(lengths, fresh, q, k, v, o, g, lse, x, w, half):
    blocks, seqs, span, _ = x.shape
    width = q.shape[1]
    heads = width // HD
    count = blocks * span
    owned = half.shape[0] // 32
    per_seq = count // BACK_KEY_BLOCK
    pair = 2 * owned
    edges = [pair * p // 3 for p in range(4)]
    flows = [
        (low, high - low, flow_stages(order))
        for low, high, order in zip(edges, edges[1:], FLOW_ORDERS)
    ]
    one = lambda shape: pl.BlockSpec((1,) + shape, lambda i, *_: (i // per_seq,) + (0,) * len(shape))
    mid = lambda shape: pl.BlockSpec((blocks, 1) + shape, lambda i, *_: (0, i // per_seq, 0, 0))
    single = lambda shape: pl.BlockSpec(
        (1,) + shape, lambda i, *_: (i // per_seq, 0, 0), pipeline_mode=pl.Buffered(1)
    )
    dma = pltpu.SemaphoreType.DMA
    return pl.pallas_call(
        functools.partial(attend_back_sum_kernel, heads, flows),
        grid_spec=pltpu.PrefetchScalarGridSpec(
            num_scalar_prefetch=2,
            grid=(seqs * per_seq,),
            in_specs=[
                one((width, count)),
                single((width, count)),
                single((width, count)),
                pl.BlockSpec(
                    (blocks, 1, width, span),
                    lambda i, *_: (0, i // per_seq, 0, 0),
                    pipeline_mode=pl.Buffered(1),
                ),
                mid((width, span)),
                one((8, count)),
                pl.BlockSpec(
                    (blocks, 1, span, D),
                    lambda i, *_: (0, i // per_seq, 0, 0),
                    pipeline_mode=pl.Buffered(1),
                ),
                pl.BlockSpec(
                    (3 * width, D), lambda i, *_: (0, 0), pipeline_mode=pl.Buffered(1)
                ),
                pl.BlockSpec(memory_space=pl.ANY),
            ],
            out_specs=[
                pl.BlockSpec(memory_space=pl.ANY),
                mid((width, span)),
                whole((owned, TILE, TILE)),
                whole((1, 3 * width)),
            ],
            scratch_shapes=[
                pltpu.VMEM((3 * width, D), f32),
                pltpu.VMEM((heads, count, HD + 16), bf16),
                pltpu.VMEM((heads, HD + 16, count), bf16),
                pltpu.VMEM((heads, count, HD + 16), bf16),
                pltpu.VMEM((heads, HD + 16, count), bf16),
                pltpu.VMEM((width, count), bf16),
                pltpu.VMEM((width, count), f32),
                pltpu.VMEM((8, count), f32),
                pltpu.VMEM((3 * width, BACK_KEY_BLOCK), bf16),
                pltpu.VMEM((width, BACK_KEY_BLOCK), f32),
                pltpu.VMEM((width, BACK_KEY_BLOCK), f32),
                pltpu.VMEM((heads, BACK_QUERY_BLOCK, BACK_KEY_BLOCK), bf16),
                pltpu.VMEM((heads, BACK_QUERY_BLOCK, BACK_KEY_BLOCK), bf16),
                pltpu.VMEM((seqs, blocks, span, D), bf16),
                pltpu.VMEM((seqs, 2, span, D), bf16),
                pltpu.VMEM((seqs, span, D), bf16),
                pltpu.VMEM((span, D), f32),
                pltpu.VMEM((8, -(-pair // 3), HALF, TILE), bf16),
                pltpu.VMEM((pair, HALF, TILE), f32),
                pltpu.VMEM((owned, HALF, TILE), f32),
                pltpu.VMEM((2, Q_UNITS, HALF, TILE), bf16),
                pltpu.VMEM((Q_UNITS, HALF, TILE), bf16),
                pltpu.VMEM((Q_UNITS, HALF, TILE), bf16),
                pltpu.VMEM((Q_UNITS, HALF, TILE), bf16),
                pltpu.VMEM((owned, TILE, TILE), bf16),
                dma((seqs, 2, 2)),
                dma((seqs, 2)),
                dma((seqs,)),
                dma((3,)),
                dma((3, 4)),
                dma((3, 4)),
                dma((2,)),
                dma((3, 3)),
                dma((3, 3)),
                dma((Q_UNITS,)),
                dma(()),
            ]
            + [
                pltpu.VMEM((8 >> k, size, HALF, TILE), bf16)
                for _, size, _ in flows
                for k in range(4)
            ],
        ),
        out_shape=[
            jax.ShapeDtypeStruct((seqs, span, D), f32),
            jax.ShapeDtypeStruct((blocks, seqs, width, span), bf16),
            jax.ShapeDtypeStruct((owned, TILE, TILE), f32),
            jax.ShapeDtypeStruct((1, 3 * width), f32),
        ],
        compiler_params=pltpu.CompilerParams(
            dimension_semantics=("arbitrary",),
            collective_id=5,
            has_side_effects=True,
            vmem_limit_bytes=VMEM_LIMIT,
        ),
        cost_estimate=pl.CostEstimate(
            flops=70_000_000_000, bytes_accessed=25_000_000, transcendentals=0
        ),
        name="attend_back_sum",
    )(lengths, fresh, q, k, v, o, g, lse, x, w, half.reshape(16, pair, HALF, TILE))


VEC_ROWS = 72


def finish_kernel(
    stages,
    raw_ref,
    gain_ref,
    rows_ref,
    hsum_ref,
    db_ref,
    master_ref,
    left_ref,
    right_ref,
    left_root_ref,
    right_root_ref,
    par_ref,
    stat_ref,
    clip_out,
    left_out,
    right_out,
    tiles_out,
    vec_out,
    stat_out,
    par_out,
    norm_out,
    total,
    landing,
    send_sem,
    recv_sem,
):
    owned = raw_ref.shape[0]
    used = par_ref.shape[0]
    partners = [partner_of(axis, bit)[0] for axis, bit in stages]
    greet(partners)
    squares = jnp.zeros((TILE, TILE), f32)
    for t in range(owned):
        squares = squares + raw_ref[t] * raw_ref[t]
    per = D // TILE
    width = db_ref.shape[1] // 3
    group = lax.axis_index("seq")
    total[...] = jnp.zeros_like(total)
    for piece, (ref, row) in enumerate(
        ((gain_ref, 0), (gain_ref, 1), (rows_ref, 0), (rows_ref, 1), (None, 0), (rows_ref, 2), (rows_ref, 3))
    ):
        if ref is not None:
            for c in range(per):
                total[piece * per + c : piece * per + c + 1, :] = ref[
                    row : row + 1, c * TILE : (c + 1) * TILE
                ]
    for part, start in ((0, 4 * per), (2, 7 * per)):
        for unit in range(width // HALF):
            value = db_ref[:, part * width + unit * HALF : part * width + (unit + 1) * HALF]
            both = jnp.concatenate([value, value], axis=1)
            lane = lax.broadcasted_iota(jnp.int32, (1, TILE), 1) // HALF
            place = group * (width // HALF) + unit
            room = (D if part == 0 else VW) // HALF
            row = start + jnp.minimum(place, room - 1) // 2
            keep = (lane == place % 2) & (place < room)
            total[pl.ds(row, 1), :] = total[pl.ds(row, 1), :] + jnp.where(keep, both, 0.0)
    for c in range(FF // TILE):
        at = 7 * per + VW // TILE + c
        total[at : at + 1, :] = hsum_ref[:, c * TILE : (c + 1) * TILE]
    total[used : used + 1, :] = jnp.sum(squares, axis=0, keepdims=True)
    for i, device in enumerate(partners):
        landing[i, 0] = total[...]
        copy = pltpu.make_async_remote_copy(
            src_ref=landing.at[i, 0],
            dst_ref=landing.at[i, 1],
            send_sem=send_sem.at[i],
            recv_sem=recv_sem.at[i],
            device_id=device,
            device_id_type=MESH,
        )
        copy.start()
        copy.wait()
        total[...] = total[...] + landing[i, 1]
    vector = total[0:used, :]
    square_sum = jnp.sum(total[used : used + 1, :], axis=1, keepdims=True) + jnp.sum(
        jnp.sum(vector * vector, axis=0, keepdims=True), axis=1, keepdims=True
    )
    grad_norm = jnp.sqrt(square_sum)
    factor = jnp.minimum(1.0, CLIP / (grad_norm + clip_eps))
    norm_out[...] = jnp.broadcast_to(grad_norm, norm_out.shape)
    grads = vector * factor
    vec_out[...] = grads
    stat = decay_rate * stat_ref[...] + (1.0 - decay_rate) * grads * grads
    stat_out[...] = stat
    par_out[...] = par_ref[...] - vector_rate * grads / (jnp.sqrt(stat) + moment_eps)
    first = (lax.axis_index("dp") * lax.axis_size("seq") + lax.axis_index("seq")) * owned

    def exact(a, b, dims):
        return lax.dot_general(a, b, dims, precision=highest, preferred_element_type=f32)

    for t in range(owned):
        index = first + t
        turned = (index < N_QKV) | (index >= FIRST_PROJ)
        raw = raw_ref[t]
        tile = jnp.where(turned, raw.T, raw) * factor
        clip_out[t] = tile
        left_out[t] = decay_rate * left_ref[t] + (1.0 - decay_rate) * exact(tile, tile, NT)
        flipped = tile.T
        right_out[t] = decay_rate * right_ref[t] + (1.0 - decay_rate) * exact(flipped, flipped, NT)
        inner = exact(tile, right_root_ref[t], NN)
        tiles_out[t] = master_ref[t] - matrix_rate * exact(left_root_ref[t], inner, NN)


def finish(raw, vectors, master, left, right, left_root, right_root, par, stat, dp, seq):
    stages = exchange_bits(dp, seq)
    tiles = jax.ShapeDtypeStruct(raw.shape, f32)
    vector = jax.ShapeDtypeStruct(par.shape, f32)
    vm = pl.BlockSpec(memory_space=pltpu.VMEM)
    return pl.pallas_call(
        functools.partial(finish_kernel, stages),
        in_specs=[vm] * 12,
        out_specs=[vm] * 8,
        out_shape=[tiles] * 4 + [vector] * 3 + [jax.ShapeDtypeStruct((8, TILE), f32)],
        scratch_shapes=[
            pltpu.VMEM((VEC_ROWS, TILE), f32),
            pltpu.VMEM((len(stages), 2, VEC_ROWS, TILE), f32),
            pltpu.SemaphoreType.DMA((len(stages),)),
            pltpu.SemaphoreType.DMA((len(stages),)),
        ],
        compiler_params=pltpu.CompilerParams(
            collective_id=2, has_side_effects=True, vmem_limit_bytes=VMEM_LIMIT
        ),
        name="finish",
    )(raw, *vectors, master, left, right, left_root, right_root, par, stat)


def per_device(
    tokens,
    first_values,
    cotangent,
    lengths,
    master_tiles,
    left_stat,
    right_stat,
    left_root,
    right_root,
    vector_params,
    vector_stat,
):
    seqs, span, _ = tokens.shape
    owned_count = master_tiles.shape[0]
    groups = lax.axis_size("seq")
    me_seq = lax.axis_index("seq")
    width = D // groups
    fresh_groups = VW // width
    total_tiles = owned_count * groups * lax.axis_size("dp")

    (
        gain_one,
        shift_one,
        gain_two,
        shift_two,
        query_bias,
        out_bias,
        proj_bias,
        value_bias,
        hidden_bias,
    ) = split_vector(vector_params)

    fits = front_fits(lax.axis_size("dp"), groups, owned_count)
    flat_tokens = tokens.reshape(-1, D).astype(f32)
    normed_one, unit_one, inv_one = norm_forward(flat_tokens, gain_one, shift_one)
    first_turned = first_values.transpose(2, 0, 1).reshape(groups - fresh_groups, width, seqs, span)
    first_turned = first_turned.transpose(0, 2, 1, 3)
    if fits:
        norm_rows = jnp.concatenate(
            [jnp.stack([gain_one, shift_one]), jnp.zeros((6, D), f32)]
        )
        x_all, w_mine, first_mine, g_one, g_two = front(
            tokens, norm_rows, master_tiles, first_turned
        )

        def swap(value, bit):
            pairs = [(d, d ^ bit) for d in range(32)]
            return lax.ppermute(value, ("dp", "seq"), pairs)

        g_one_y, g_two_x = swap(g_one, 4), swap(g_two, 2)
        g_one_core, g_two_core = swap(g_one, 1), swap(g_two, 1)
    else:
        normed_one = normed_one.astype(bf16).reshape(seqs, span, D)
        x_all = lax.all_gather(normed_one, "seq", axis=0, tiled=False)
        gathered = lax.all_gather(
            master_tiles.astype(bf16), ("dp", "seq"), axis=0, tiled=True
        )
        sources = (gathered,)
        first_send = jnp.concatenate(
            [jnp.zeros((fresh_groups,) + first_turned.shape[1:], bf16), first_turned], axis=0
        )
        first_mine = lax.all_to_all(first_send, "seq", 0, 0, tiled=True)
    is_fresh = (me_seq < fresh_groups).astype(jnp.int32).reshape(1)
    fresh_seq = jnp.minimum(me_seq, fresh_groups - 1)

    def turned(start, cols):
        amount = D // TILE * (cols // TILE)
        tiles = gathered[start : start + amount].reshape(D // TILE, cols // TILE, TILE, TILE)
        return tiles.transpose(1, 3, 0, 2).reshape(cols, D)

    if not fits:
        wq = lax.dynamic_slice_in_dim(turned(0, D), me_seq * width, width, 0)
        wk = lax.dynamic_slice_in_dim(turned(N_OUT, D), me_seq * width, width, 0)
        wv = lax.dynamic_slice_in_dim(turned(2 * N_OUT, VW), fresh_seq * width, width, 0)
        w_mine = jnp.concatenate([wq, wk, wv], axis=0)
    qb = lax.dynamic_slice_in_dim(query_bias, me_seq * width, width, 0).reshape(width, 1)
    vb = lax.dynamic_slice_in_dim(value_bias, fresh_seq * width, width, 0).reshape(width, 1)

    o_heads, q, k, v, lse = attend_forward(
        lengths, is_fresh, x_all, w_mine, qb, vb, first_mine
    )
    if fits:
        g_one_y, g_two_x, o_heads = lax.optimization_barrier((g_one_y, g_two_x, o_heads))
        sources = (g_one, g_one_y, g_two, g_two_x)
        sources += (g_one_core, swap(g_one_y, 1), g_two_core, swap(g_two_x, 1))
    att = lax.all_to_all(o_heads, "seq", 0, 0, tiled=True)
    rows = jnp.concatenate(
        [jnp.stack([gain_two, shift_two, out_bias, proj_bias]), jnp.zeros((4, D), f32)]
    )
    position = (me_seq * span).astype(jnp.int32).reshape(1)
    (
        block_output,
        residual_grad,
        att_grad,
        act,
        hidden_grad,
        normed_two,
        branch_grad,
        out_grad,
        row_sums,
        hidden_bias_grad,
    ) = feed_forward(
        lengths,
        position,
        att,
        tokens,
        cotangent,
        sources,
        total_tiles,
        rows,
        hidden_bias.reshape(1, FF),
    )
    g_heads = lax.all_to_all(att_grad, "seq", 0, 0, tiled=True)
    grad_args = (att, branch_grad, out_grad, normed_two, act, hidden_grad)
    back_args = (q, k, v, o_heads, g_heads, lse, x_all, w_mine)
    if fits:
        half_tiles = paired_grads(total_tiles, *grad_args)
        norm_one_in, dv, owned, db = attend_back_sum(lengths, is_fresh, *back_args, half_tiles)
        norm_one_in = norm_one_in.reshape(-1, D)
    else:
        all_tiles = weight_grads(total_tiles, *grad_args)
        group = me_seq.astype(jnp.int32).reshape(1)
        dx, dv, all_tiles, db = attend_backward(lengths, is_fresh, group, *back_args, all_tiles)
        norm_one_in = (
            lax.psum_scatter(dx, "seq", scatter_dimension=0, tiled=True)
            .reshape(-1, D)
            .astype(f32)
        )
        owned = tile_sum(all_tiles, lax.axis_size("dp"), groups)
    dv_back = lax.all_to_all(dv, "seq", 0, 0, tiled=True)
    first_grad = (
        dv_back[fresh_groups:]
        .transpose(1, 3, 0, 2)
        .reshape(first_values.shape)
        .astype(f32)
    )
    token_part = norm_backward(norm_one_in, unit_one, inv_one, gain_one)
    tokens_grad = residual_grad + token_part.reshape(tokens.shape)
    gain_one_grad = jnp.sum(norm_one_in * unit_one, axis=0)
    shift_one_grad = jnp.sum(norm_one_in, axis=0)

    used = vector_params.shape[0] // TILE
    gain_sums = jnp.stack([gain_one_grad, shift_one_grad])
    clipped, left_new, right_new, tiles_new, vector_grads, vector_stat_new, vector_new, norm = (
        finish(
            owned,
            (gain_sums, row_sums, hidden_bias_grad, db),
            master_tiles,
            left_stat,
            right_stat,
            left_root,
            right_root,
            vector_params.reshape(used, TILE),
            vector_stat.reshape(used, TILE),
            lax.axis_size("dp"),
            groups,
        )
    )
    return (
        block_output,
        tokens_grad,
        first_grad,
        clipped,
        left_new,
        right_new,
        tiles_new,
        vector_grads.reshape(-1),
        vector_stat_new.reshape(-1),
        vector_new.reshape(-1),
        norm[0, 0],
    )


def solution(mesh):
    tiles = P(("dp", "seq"), None, None)
    seqs = P("dp", "seq", None)
    in_specs = (seqs, seqs, seqs, P("dp"), tiles, tiles, tiles, tiles, tiles, P(), P())
    out_specs = (seqs, seqs, seqs, tiles, tiles, tiles, tiles, P(), P(), P(), P())
    return jax.shard_map(
        per_device, mesh=mesh, in_specs=in_specs, out_specs=out_specs, check_vma=False
    )
```
